128 devices in a mesh: mx: 16 (over y, x), my: 8 (over z, core).
Axes of the slice: x: 4, y: 4, z: 4, core: 2. Of those that a mesh axis runs over, the one named last changes fastest.
Arguments:
- density: float32 [256, 128, 128], P('mx', 'my'), may hold values from 0.5 to 2
- momentum: float32 [3, 256, 128, 128], P(None, 'mx', 'my'), may hold values from -1.8 to 1.8
- energy: float32 [256, 128, 128], P('mx', 'my'), may hold values from -6 to 6
- entropy: float32 [256, 128, 128], P('mx', 'my'), may hold values from 0.5 to 16, as said below
- tracers: float32 [9, 256, 128, 128], P(None, 'mx', 'my'), may hold values from -6 to 6
- leaf_flags: int32 [32, 16, 16], P('mx', 'my'), may hold values 0 or 1
Outputs:
- section: float32 [15, 256, 128, 128], P(None, 'mx', 'my')
- gravity_accel: float32 [3, 256, 128, 128], P(None, 'mx', 'my')
The draws below stay inside these ranges and needn't reach their ends.
Inputs may be any that keep to these rules, and one draw needn't show every extreme that they name: `entropy`: positive.
All inputs are finite; a program needn't handle non-finite values. No bound on the sum of `leaf_flags` on one device may be relied on, other than what follows from the above.
Results may differ from the reference program's by a relative error of at most 0.0003.
Values sent between devices are 32-bit elements; how exact they have to be, the bound alone decides.
No kernel may reach another device: no remote copies, remote signals or barrier semaphores. Data moves between devices by JAX's collectives and lax.ppermute only.
A program may use at most 128 MiB of HBM per device.

```python
import math
import jax
import jax.numpy as jnp
import numpy as np
from jax import lax

SUB = 8
NF = 15
LEVELS = 3
GZ = 16
SX = 32
SY = 16
NX = 256
NY = 128
NZ = 128


def draw_entropy(key, part):
    base_value = jnp.exp(jax.random.uniform(key, (NX, NY, NZ), jnp.float32, math.log(0.5), math.log(2.0)))
    across_x = jnp.arange(NX, dtype=jnp.float32)[:, None, None] / NX
    across_y = jnp.arange(NY, dtype=jnp.float32)[None, :, None] / NY
    return base_value * jnp.exp2(2.0 * across_x + across_y)


def set_ends(drawn, key, low, top_value):
    index_at = [jax.random.randint(jax.random.fold_in(key, axis), (), 0, length) for axis, length in enumerate(drawn.shape)]
    widest = drawn.shape.index(max(drawn.shape))
    next_to = index_at[:widest] + [(index_at[widest] + 1) % drawn.shape[widest]] + index_at[widest + 1:]
    return drawn.at[tuple(index_at)].set(low).at[tuple(next_to)].set(top_value)


def block_scale(rng, dims, cuts, least, top_value):
    def one(position, shards_of):
        steps = jax.random.uniform(jax.random.fold_in(jax.random.fold_in(rng, 6), position), (shards_of,), jnp.float32, least / len(cuts), top_value / len(cuts))
        return jnp.repeat(jnp.exp(steps), dims[position] // shards_of).reshape((-1,) + (1,) * (len(dims) - position - 1))

    factor_of = one(*cuts[0])
    for cut in cuts[1:]:
        factor_of = factor_of * one(*cut)
    return factor_of


def bell_draw(key, shape, deviation, limit, pieces=(), kind=jnp.bfloat16):
    array = jax.random.normal(key, shape, jnp.float32) * deviation
    if len(pieces) > 0:
        array = block_scale(key, shape, pieces, -0.22, 0.18) * array
    return jnp.clip(array, min=-limit, max=limit).astype(kind)


def setup_inputs(seed: int = 0) -> dict:
    keys = jax.random.split(jax.random.key(seed), 7)
    density = jnp.clip(jnp.exp(math.log(2.0) - 1.3862944 * jax.random.uniform(keys[0], (NX, NY, NZ), jnp.float32) ** block_scale(keys[0], (NX, NY, NZ), ((0, 16), (1, 8)), -0.2, 0.2)), 0.5, 2.0)
    momentum = bell_draw(keys[1], (3, NX, NY, NZ), 0.3, 1.8, ((1, 16), (2, 8)), jnp.float32)
    energy = bell_draw(keys[2], (NX, NY, NZ), 1.0, 6.0, ((0, 16), (1, 8)), jnp.float32)
    entropy = draw_entropy(jax.random.fold_in(keys[6], 71), 0)
    tracers = bell_draw(keys[4], (NF - 6, NX, NY, NZ), 1.0, 6.0, ((1, 16), (2, 8)), jnp.float32)
    leaf_flags = set_ends((jax.random.randint(keys[5], (SX, SY, GZ), 0, 4) < 3).astype(jnp.int32), jax.random.fold_in(keys[5], 1), 0, 1)
    return dict(density=density, momentum=momentum, energy=energy, entropy=entropy, tracers=tracers, leaf_flags=leaf_flags)


gamma_gas = 5.0 / 3.0
courant = 0.3
gravity = 0.02
highest = lax.Precision.HIGHEST
multi_index = [(power_x, power_y, degree_sum - power_x - power_y) for degree_sum in range(4) for power_x in range(degree_sum, -1, -1) for power_y in range(degree_sum - power_x, -1, -1)]

def factorial_of(exponent):
    return math.factorial(exponent[0]) * math.factorial(exponent[1]) * math.factorial(exponent[2])

def inverse_derivative(exponent, vectors):
    axes_list = [0] * exponent[0] + [1] * exponent[1] + [2] * exponent[2]
    radius = np.sqrt(np.sum(vectors * vectors, axis=1))
    radius_safe = np.where(radius > 0.0, radius, 1.0)
    degree = len(axes_list)
    if degree == 0:
        result = 1.0 / radius_safe
    elif degree == 1:
        result = -vectors[:, axes_list[0]] / radius_safe ** 3
    elif degree == 2:
        index_one, index_two = axes_list
        result = 3.0 * vectors[:, index_one] * vectors[:, index_two] / radius_safe ** 5 - float(index_one == index_two) / radius_safe ** 3
    else:
        index_one, index_two, index_three = axes_list
        crossed = float(index_one == index_two) * vectors[:, index_three] + float(index_one == index_three) * vectors[:, index_two] + float(index_two == index_three) * vectors[:, index_one]
        result = -15.0 * vectors[:, index_one] * vectors[:, index_two] * vectors[:, index_three] / radius_safe ** 7 + 3.0 * crossed / radius_safe ** 5
    return np.where(radius > 0.0, result, 0.0)

def offset_grid(reach_x, reach_y, reach_z):
    return [(shift_x, shift_y, shift_z) for shift_x in range(-reach_x, reach_x + 1) for shift_y in range(-reach_y, reach_y + 1) for shift_z in range(-reach_z, reach_z + 1)]

def translation_kernel(spacing, offsets):
    vectors = np.asarray(offsets) * (-1.0 * spacing)
    entries = np.zeros((len(offsets), len(multi_index), len(multi_index)))
    for row_index, target_power in enumerate(multi_index):
        for column_index, source_power in enumerate(multi_index):
            if sum(target_power) + sum(source_power) <= 3:
                joined = (target_power[0] + source_power[0], target_power[1] + source_power[1], target_power[2] + source_power[2])
                entries[:, row_index, column_index] = -gravity * (-1.0) ** sum(source_power) / factorial_of(source_power) * inverse_derivative(joined, vectors)
    return jnp.asarray(entries, dtype=jnp.float32)

def upward_matrices(spacing):
    entries = np.zeros((2, 2, 2, len(multi_index), len(multi_index)))
    for octant in range(8):
        octant_bits = (octant >> 2 & 1, octant >> 1 & 1, octant & 1)
        displacement = [(octant_bits[dimension] - 0.5) * spacing for dimension in range(3)]
        for row_index, target_power in enumerate(multi_index):
            for column_index, source_power in enumerate(multi_index):
                if all((source_power[dimension] <= target_power[dimension] for dimension in range(3))):
                    entry_value = 1.0
                    for dimension in range(3):
                        entry_value *= math.comb(target_power[dimension], source_power[dimension]) * displacement[dimension] ** (target_power[dimension] - source_power[dimension])
                    entries[octant_bits[0], octant_bits[1], octant_bits[2], row_index, column_index] = entry_value
    return jnp.asarray(entries, dtype=jnp.float32)

def downward_matrices(spacing):
    entries = np.zeros((2, 2, 2, len(multi_index), len(multi_index)))
    for octant in range(8):
        octant_bits = (octant >> 2 & 1, octant >> 1 & 1, octant & 1)
        displacement = [(octant_bits[dimension] - 0.5) * spacing for dimension in range(3)]
        for row_index, target_power in enumerate(multi_index):
            for column_index, source_power in enumerate(multi_index):
                if all((source_power[dimension] >= target_power[dimension] for dimension in range(3))):
                    entry_value = 1.0
                    for dimension in range(3):
                        lifted = source_power[dimension] - target_power[dimension]
                        entry_value *= displacement[dimension] ** lifted / math.factorial(lifted)
                    entries[octant_bits[0], octant_bits[1], octant_bits[2], row_index, column_index] = entry_value
    return jnp.asarray(entries, dtype=jnp.float32)

def moment_table(cells_edge):
    centres = (np.arange(cells_edge) + 0.5) / cells_edge - 0.5
    volume = 1.0 / cells_edge ** 3
    entries = np.zeros((cells_edge, cells_edge, cells_edge, len(multi_index)))
    for column_index, exponent in enumerate(multi_index):
        entries[:, :, :, column_index] = volume * centres[:, None, None] ** exponent[0] * centres[None, :, None] ** exponent[1] * centres[None, None, :] ** exponent[2]
    return jnp.asarray(entries, dtype=jnp.float32)

def field_table(cells_edge):
    centres = (np.arange(cells_edge) + 0.5) / cells_edge - 0.5
    entries = np.zeros((cells_edge, cells_edge, cells_edge, 3, len(multi_index)))
    for column_index, exponent in enumerate(multi_index):
        for dimension in range(3):
            if exponent[dimension] > 0:
                lowered = list(exponent)
                lowered[dimension] -= 1
                entries[:, :, :, dimension, column_index] = -exponent[dimension] / factorial_of(exponent) * centres[:, None, None] ** lowered[0] * centres[None, :, None] ** lowered[1] * centres[None, None, :] ** lowered[2]
    return jnp.asarray(entries, dtype=jnp.float32)

def allowed(coords, offset, rule_name):
    touching = (jnp.abs(offset[0]) <= 1) & (jnp.abs(offset[1]) <= 1) & (jnp.abs(offset[2]) <= 1)
    accepted = (coords[0] >= 0) & (coords[1] >= 0) & (coords[2] >= 0)
    if rule_name == 'coarsest':
        return accepted & jnp.logical_not(touching)
    for dimension in range(3):
        parent_step = jnp.floor_divide(coords[dimension] + offset[dimension], 2) - jnp.floor_divide(coords[dimension], 2)
        accepted = accepted & (jnp.abs(parent_step) <= 1)
    if rule_name == 'finest':
        nonzero = (offset[0] != 0) | (offset[1] != 0) | (offset[2] != 0)
        return accepted & nonzero
    return accepted & jnp.logical_not(touching)

def coordinates(start_x, start_y, start_z, block_shape):
    along_x = start_x + jnp.arange(block_shape[0], dtype=jnp.int32)[:, None, None]
    along_y = start_y + jnp.arange(block_shape[1], dtype=jnp.int32)[None, :, None]
    along_z = start_z + jnp.arange(block_shape[2], dtype=jnp.int32)[None, None, :]
    return (along_x, along_y, along_z)

def local_from_far(extended, margins, kernels, offsets, coords, block_shape, rule_name):
    offset_table = jnp.asarray(offsets, dtype=jnp.int32)
    moments_count = extended.shape[0]
    zero_index = jnp.zeros((), jnp.int32)

    def visit(running, item):
        kernel_matrix, offset = item
        starts = (zero_index, margins[0] + offset[0], margins[1] + offset[1], margins[2] + offset[2])
        source = lax.dynamic_slice(extended, starts, (moments_count,) + tuple(block_shape))
        weight = allowed(coords, offset, rule_name).astype(jnp.float32)
        term = jnp.einsum('ga,axyz->gxyz', kernel_matrix, source, precision=highest)
        return (running + term * weight, None)
    initial = jnp.zeros((moments_count,) + tuple(block_shape), jnp.float32)
    running, _ = lax.scan(visit, initial, (kernels, offset_table))
    return running

def upward(child, matrices):
    moments_count, size_x, size_y, size_z = child.shape
    grouped = child.reshape(moments_count, size_x // 2, 2, size_y // 2, 2, size_z // 2, 2)
    return jnp.einsum('uvwga,axuyvzw->gxyz', matrices, grouped, precision=highest)

def downward(parent, matrices):
    moments_count, size_x, size_y, size_z = parent.shape
    spread = jnp.einsum('uvwgb,bxyz->gxuyvzw', matrices, parent, precision=highest)
    return spread.reshape(moments_count, 2 * size_x, 2 * size_y, 2 * size_z)

def gravity_field(density, leaf_flags):
    size_x, size_y, size_z = leaf_flags.shape
    cells_edge = density.shape[0] // size_x
    grouped = density.reshape(size_x, cells_edge, size_y, cells_edge, size_z, cells_edge)
    moments = jnp.einsum('xaybzc,abcg->gxyz', grouped, moment_table(cells_edge), precision=highest)
    moments = moments * leaf_flags.astype(jnp.float32)[None]
    levels_list = [moments]
    for level_index in range(1, LEVELS + 1):
        levels_list.append(upward(levels_list[-1], upward_matrices(2.0 ** (level_index - 1))))
    coarsest = levels_list[LEVELS]
    coarse_shape = coarsest.shape[1:]
    reach_top = (coarse_shape[0] - 1, coarse_shape[1] - 1, coarse_shape[2] - 1)
    top_offsets = offset_grid(reach_top[0], reach_top[1], reach_top[2])
    padded = jnp.pad(coarsest, ((0, 0), (reach_top[0], reach_top[0]), (reach_top[1], reach_top[1]), (reach_top[2], reach_top[2])))
    expansion = local_from_far(padded, reach_top, translation_kernel(2.0 ** LEVELS, top_offsets), top_offsets, coordinates(0, 0, 0, coarse_shape), coarse_shape, 'coarsest')
    near_offsets = offset_grid(3, 3, 3)
    for level_index in range(LEVELS - 1, -1, -1):
        current = levels_list[level_index]
        block_shape = current.shape[1:]
        padded = jnp.pad(current, ((0, 0), (3, 3), (3, 3), (3, 3)))
        rule_name = 'finest' if level_index == 0 else 'middle'
        carried = downward(expansion, downward_matrices(2.0 ** level_index))
        expansion = carried + local_from_far(padded, (3, 3, 3), translation_kernel(2.0 ** level_index, near_offsets), near_offsets, coordinates(0, 0, 0, block_shape), block_shape, rule_name)
    accel_cells = jnp.einsum('abcig,gxyz->ixaybzc', field_table(cells_edge), expansion, precision=highest)
    return accel_cells.reshape(3, density.shape[0], density.shape[1], density.shape[2])

def flux_of(states, direction):
    mass_density = states[0]
    velocity = states[1 + direction] / mass_density
    pressure = (gamma_gas - 1.0) * states[5] ** gamma_gas
    sound_speed = jnp.sqrt(gamma_gas * pressure / mass_density)
    flux_vector = states * velocity[None]
    flux_vector = flux_vector.at[1 + direction].add(pressure)
    flux_vector = flux_vector.at[4].add(pressure * velocity)
    return (flux_vector, jnp.abs(velocity) + sound_speed)

def face_flux(extended, direction):
    axis_dim = direction + 1
    faces = extended.shape[axis_dim] - 5
    outer_left, inner_left, left_cell, right_cell, inner_right, outer_right = [lax.slice_in_dim(extended, begin_index, begin_index + faces, axis=axis_dim) for begin_index in range(6)]
    interface = (37.0 * (left_cell + right_cell) - 8.0 * (inner_left + inner_right) + (outer_left + outer_right)) / 60.0
    left_state = jnp.clip(interface, jnp.minimum(jnp.minimum(inner_left, left_cell), right_cell), jnp.maximum(jnp.maximum(inner_left, left_cell), right_cell))
    right_state = jnp.clip(interface, jnp.minimum(jnp.minimum(left_cell, right_cell), inner_right), jnp.maximum(jnp.maximum(left_cell, right_cell), inner_right))
    flux_left, speed_left = flux_of(left_state, direction)
    flux_right, speed_right = flux_of(right_state, direction)
    speed_face = jnp.maximum(speed_left, speed_right)
    return 0.5 * (flux_left + flux_right) - 0.5 * speed_face[None] * (right_state - left_state)

def cell_speed(conserved):
    velocity = conserved[1:4] / conserved[0][None]
    pressure = (gamma_gas - 1.0) * conserved[5] ** gamma_gas
    sound_speed = jnp.sqrt(gamma_gas * pressure / conserved[0])
    return lax.optimization_barrier(jnp.max(jnp.abs(velocity), axis=0)) + sound_speed

def reference(density, momentum, energy, entropy, tracers, leaf_flags):
    conserved = jnp.concatenate([density[None], momentum, energy[None], entropy[None], tracers], axis=0)
    gravity_accel = gravity_field(density, leaf_flags)
    fastest = jnp.max(cell_speed(conserved))
    step_size = courant / (SUB * fastest)
    tendency = jnp.zeros_like(conserved)
    for direction in range(3):
        widths = [(0, 0), (0, 0), (0, 0), (0, 0)]
        widths[direction + 1] = (3, 3)
        extended = jnp.pad(conserved, widths, mode='edge')
        tendency = tendency - jnp.diff(face_flux(extended, direction), axis=direction + 1) * SUB
    tendency = tendency.at[1:4].add(density[None] * gravity_accel)
    tendency = tendency.at[4].add(lax.optimization_barrier(jnp.sum(momentum * gravity_accel, axis=0)))
    return (conserved + step_size * tendency, gravity_accel)
```

```python
import functools
import math

import jax
import jax.numpy as jnp
import ml_dtypes
import numpy as np
from jax import lax
from jax.experimental import pallas as pl
from jax.experimental.pallas import tpu as pltpu
from jax.sharding import PartitionSpec as P

F32 = jnp.float32
BF16 = jnp.bfloat16
HIGHEST = lax.Precision.HIGHEST
GRAVITY = 0.02
GAMMA = 5.0 / 3.0
COURANT = 0.3
SUB = 8
NF = 15
GX, GY = 16, 8
ROWS = 256

ALPHA = [
    (px, py, d - px - py)
    for d in range(4)
    for px in range(d, -1, -1)
    for py in range(d - px, -1, -1)
]
NA = len(ALPHA)
NG = 24
WIN = 40
PAIRS = [(px, py) for px in range(4) for py in range(4 - px)]


def factorial_of(e):
    return math.factorial(e[0]) * math.factorial(e[1]) * math.factorial(e[2])


def inverse_derivative(exponent, r):
    axes = [0] * exponent[0] + [1] * exponent[1] + [2] * exponent[2]
    norm = math.sqrt(r[0] ** 2 + r[1] ** 2 + r[2] ** 2)
    if norm == 0.0:
        return 0.0
    if not axes:
        return 1.0 / norm
    if len(axes) == 1:
        return -r[axes[0]] / norm**3
    if len(axes) == 2:
        a, b = axes
        return 3.0 * r[a] * r[b] / norm**5 - float(a == b) / norm**3
    a, b, c = axes
    crossed = float(a == b) * r[c] + float(a == c) * r[b] + float(b == c) * r[a]
    return -15.0 * r[a] * r[b] * r[c] / norm**7 + 3.0 * crossed / norm**5


def split_np(x):
    high = x.astype(np.float32).astype(ml_dtypes.bfloat16)
    low = (x - high.astype(np.float64)).astype(ml_dtypes.bfloat16)
    return high, low


@functools.cache
def constants():
    out = {}
    w = np.zeros((7, NG, NA, WIN))
    for z in range(7):
        for i in range(6):
            for j in range(6):
                r = (-(i - 2.0), -(j - 2.0), -(z - 3.0))
                for g, eg in enumerate(ALPHA):
                    for a, ea in enumerate(ALPHA):
                        if sum(eg) + sum(ea) <= 3:
                            e = tuple(eg[k] + ea[k] for k in range(3))
                            w[z, g, a, i * 6 + j] = (
                                -GRAVITY * (-1.0) ** sum(ea) / factorial_of(ea) * inverse_derivative(e, r)
                            )
    out["w_high"], out["w_low"] = split_np(w.reshape(7 * NG, NA * WIN))
    sel = np.zeros((4, WIN, 72))
    sign = np.zeros((4, 384))
    for c in range(4):
        cx, cy = c >> 1, c & 1
        for i in range(6):
            for j in range(6):
                si, sj = (5 - i if cx else i), (5 - j if cy else j)
                sel[c, i * 6 + j, ((si // 2) * 3 + sj // 2) * 8 + (si % 2) * 2 + sj % 2] = 1.0
        for a, e in enumerate(ALPHA):
            sign[c, a * 16 : a * 16 + 16] = (-1.0) ** (cx * e[0] + cy * e[1])
    out["sel_zero"] = sel.reshape(4 * WIN, 72).astype(ml_dtypes.bfloat16)
    lanes = np.zeros((16, 384), np.float32)
    lanes[0:4] = sign
    for a, e in enumerate(ALPHA):
        for r in range(16):
            lane = a * 16 + r
            level = 1 if r < 8 else 2 if r < 12 else 3
            lanes[4 + level, lane] = e[0] % 2
            lanes[8 + level, lane] = e[1] % 2
    out["lane_odd"] = lanes
    up = np.zeros((384, 384))
    for t, et in enumerate(ALPHA):
        for s, es in enumerate(ALPHA):
            if all(es[k] <= et[k] for k in range(3)):
                for base, to, count in ((0, 8, 8), (8, 12, 4)):
                    for z in range(count):
                        v = 2.0 ** -sum(et)
                        for k in range(3):
                            d = -0.5 if k < 2 or z % 2 == 0 else 0.5
                            v *= math.comb(et[k], es[k]) * d ** (et[k] - es[k])
                        up[s * 16 + base + z, t * 16 + to + z // 2] = v
    assert np.array_equal(up, up.astype(ml_dtypes.bfloat16).astype(np.float64))
    out["up"] = up.astype(ml_dtypes.bfloat16)
    odd = np.zeros((16, 384), np.float32)
    for a, e in enumerate(ALPHA):
        odd[0, a * 16 : a * 16 + 16] = e[0] % 2
        odd[1, a * 16 : a * 16 + 16] = e[1] % 2
    out["alpha_odd"] = odd
    agg = np.zeros((32, 128))
    for x in range(GX):
        for y in range(GY):
            agg[(x // 2) * 4 + y // 2, x * 8 + y] = 1.0
    out["agg"] = agg.astype(ml_dtypes.bfloat16)
    mask = np.zeros((8, 128), np.float32)
    info = np.zeros((16, 128), np.float32)
    expand = np.zeros((128, 128), np.float32)
    for lane in range(96):
        g, r = lane // 16, lane % 16
        if g < 4:
            n, z, level = 16, r, 0
        elif r < 8:
            n, z, level = 8, r, 1
        elif r < 12:
            n, z, level = 4, r - 8, 2
        elif r < 14:
            n, z, level = 2, r - 12, 3
        else:
            continue
        for k in range(7):
            o = k - 3
            ok = 0 <= z + o < n and abs((z + o) // 2 - z // 2) <= 1
            if g == 4:
                ok = ok and abs(o) > 1
            if g == 5:
                ok = ok and abs(o) <= 1
            mask[k, lane] = float(ok)
        if g < 5:
            info[0, lane] = 2.0**-level
            info[1, lane] = float(g >> 1) if level == 0 else 0.0
            info[2, lane] = float(g & 1) if level == 0 else 0.0
            info[2 + 2 * level, lane] = 1.0 if level else info[2, lane]
            info[9, lane] = float(z % 2)
            if level == 0:
                expand[64 + z // 2, lane] = 1.0
            elif level == 1:
                expand[64 + 8 + z // 2, lane] = 1.0
            elif level == 2:
                expand[64 + 12 + z // 2, lane] = 1.0
    out["mask"] = mask
    out["info"] = info
    out["expand"] = expand
    gamma_odd = np.zeros((3 * NG, 128), np.float32)
    down = np.zeros((NG, NG), np.float32)
    for g, eg in enumerate(ALPHA):
        for k in range(3):
            gamma_odd[k * NG + g] = eg[k] % 2
        for b, eb in enumerate(ALPHA):
            if all(eb[k] >= eg[k] for k in range(3)):
                v = 2.0 ** -sum(eg)
                for k in range(3):
                    n = eb[k] - eg[k]
                    v *= (-0.25) ** n / math.factorial(n)
                down[g, b] = v
    out["gamma_odd"] = gamma_odd
    out["down"] = down
    h = (np.arange(SUB) + 0.5) / SUB - 0.5
    spread = np.zeros((16, 384))
    for k in range(3):
        for z in range(128):
            spread[z // 8, k * 128 + z] = h[z % 8] ** k
    out["spread"] = spread.astype(np.float32)
    poly = np.zeros((3, 8, 8, 3, NG))
    for i in range(3):
        for g, e in enumerate(ALPHA):
            if e[i] > 0:
                low = list(e)
                low[i] -= 1
                poly[i, :, :, low[2], g] = (
                    -e[i] / factorial_of(e) * h[:, None] ** low[0] * h[None, :] ** low[1]
                )
    out["poly"] = poly.reshape(192, 72).astype(np.float32)
    cells = np.arange(16)
    near = h[cells % 8]
    far = ((cells + 0.5) / 8 - 1.0) / 2
    left = np.zeros((2, len(PAIRS), 8, 16, 16))
    for q, (px, py) in enumerate(PAIRS):
        for c in range(4):
            block = ((cells // 8 == c >> 1)[:, None] & (cells // 8 == (c & 1))[None, :]).astype(float)
            left[0, q, c] = block * near[:, None] ** px * near[None, :] ** py
            left[1, q, c] = block * far[:, None] ** px * far[None, :] ** py
    out["left"] = left.reshape(160, 256).astype(np.float32)
    right = np.zeros((128, 128))
    flag = np.zeros((128, 128))
    for z in range(128):
        s = z // 8
        f = ((z % 16 + 0.5) / 8 - 1.0) / 2
        for pz in range(4):
            right[z, pz * 16 + s] = h[z % 8] ** pz / SUB**3
            right[z, 64 + (s % 2) * 32 + pz * 8 + s // 2] = f**pz / SUB**3
    for s in range(16):
        for pz in range(4):
            flag[s, pz * 16 + s] = 1.0
            flag[s, 64 + (s % 2) * 32 + pz * 8 + s // 2] = 1.0
    out["right"] = right.astype(np.float32)
    out["flag"] = flag.astype(ml_dtypes.bfloat16)
    return out


def split(x):
    high = x.astype(BF16)
    return high, (x - high.astype(F32)).astype(BF16)


def mxu(a, b):
    return jnp.dot(a, b, preferred_element_type=F32)


def exact(a, b):
    return jnp.dot(a, b, precision=HIGHEST, preferred_element_type=F32)


def lane_ids(shape):
    return lax.broadcasted_iota(jnp.int32, shape, len(shape) - 1)


def row_ids(shape):
    return lax.broadcasted_iota(jnp.int32, shape, len(shape) - 2)


def power(s):
    return jnp.exp(GAMMA * jnp.log(s))


def field_ref(refs, f):
    den, mom, ene, ent, tra = refs
    if f == 0:
        return den, 0
    if f < 4:
        return mom, (f - 1) * ROWS
    if f == 4:
        return ene, 0
    if f == 5:
        return ent, 0
    return tra, (f - 6) * ROWS


def prepare_kernel(den, mom, ene, ent, tra, flags, left, right, flag, pay, xlo, xhi, ylo, yhi, fl):
    refs = (den, mom, ene, ent, tra)
    for f in range(NF):
        ref, base = field_ref(refs, f)
        for k in range(3):
            xlo[f * 3 + k] = ref[base + k * 16 : base + k * 16 + 16]
            xhi[f * 3 + k] = ref[base + (13 + k) * 16 : base + (13 + k) * 16 + 16]
            for s in range(2):
                ylo[f * 3 + k, s * 8 : s * 8 + 8] = ref[pl.ds(base + s * 128 + k, 8, stride=16)]
                yhi[f * 3 + k, s * 8 : s * 8 + 8] = ref[pl.ds(base + s * 128 + 13 + k, 8, stride=16)]
    rho = den[...]
    inverse = 1.0 / rho
    fast = jnp.maximum(jnp.maximum(jnp.abs(mom[0:ROWS]), jnp.abs(mom[ROWS : 2 * ROWS])), jnp.abs(mom[2 * ROWS :]))
    sound = jnp.sqrt(GAMMA * (GAMMA - 1.0) * power(ent[...]) * inverse)
    fastest = jnp.max(fast * inverse + sound)
    fl[...] = jnp.zeros((8, 128), F32)
    fl[0:2, 0:16] = flags[0].astype(F32)
    fl[2:4, 0:16] = flags[1].astype(F32)
    tile = mxu(fl[...].astype(BF16), flag[...])
    sums = exact(left[...], exact(rho, right[...]))
    lane = lane_ids((8, 128))
    row = row_ids((8, 128))
    tiles = [jnp.zeros((8, 128), F32) for _ in range(3)]
    zero, one = {}, {}
    for q, pair in enumerate(PAIRS):
        zero[pair] = sums[q * 8 : q * 8 + 8] * tile
        v = jnp.sum(sums[80 + q * 8 : 88 + q * 8] * tile, axis=0, keepdims=True)
        v = jnp.broadcast_to(v, (8, 128))
        one[pair] = v + pltpu.roll(v, 96, 1)
    for a, e in enumerate(ALPHA):
        c, to = a // 8, (a % 8) * 16
        low = pltpu.roll(zero[e[0], e[1]], (to - e[2] * 16) % 128, 1)
        top = pltpu.roll(one[e[0], e[1]], (to - 64 - e[2] * 8) % 128, 1)
        here = (lane >= to) & (lane < to + 16)
        tiles[c] = jnp.where(here & (row < 4), low, tiles[c])
        tiles[c] = jnp.where(here & (row == 4) & (lane < to + 8), top, tiles[c])
    tiles[2] = jnp.where((row == 4) & (lane >= 64), fastest, tiles[2])
    for c in range(3):
        pay[c * 8 : c * 8 + 8] = tiles[c]


def states(ol, il, l, r, ir, orr):
    face = (37.0 / 60.0) * (l + r) - (8.0 / 60.0) * (il + ir) + (1.0 / 60.0) * (ol + orr)
    low, high = jnp.minimum(l, r), jnp.maximum(l, r)
    left = jnp.minimum(jnp.maximum(face, jnp.minimum(il, low)), jnp.maximum(il, high))
    right = jnp.minimum(jnp.maximum(face, jnp.minimum(low, ir)), jnp.maximum(high, ir))
    return left, right


def fluxes(load, d):
    rl, rr = load(0)
    ml, mr = load(1 + d)
    sl, sr = load(5)
    il, ir = 1.0 / rl, 1.0 / rr
    vl, vr = ml * il, mr * ir
    pl_, pr = (GAMMA - 1.0) * power(sl), (GAMMA - 1.0) * power(sr)
    cl, cr = jnp.sqrt(GAMMA * pl_ * il), jnp.sqrt(GAMMA * pr * ir)
    a = 4.0 * jnp.maximum(jnp.abs(vl) + cl, jnp.abs(vr) + cr)
    wl, wr = 4.0 * vl, 4.0 * vr
    kl, kr = wl + a, wr - a
    got = {0: (rl, rr), 1 + d: (ml, mr), 5: (sl, sr)}
    out = []
    for f in range(NF):
        left, right = got[f] if f in got else load(f)
        flux = left * kl + right * kr
        if f == 1 + d:
            flux = flux + 4.0 * (pl_ + pr)
        if f == 4:
            flux = flux + (pl_ * wl + pr * wr)
        out.append(flux)
    return out


def flux_kernel(pos, den, mom, ene, ent, tra, xl, xr, yl, yr, out, ux, uy, edge):
    refs = (den, mom, ene, ent, tra)
    first_x, last_x = pos[0] == 0, pos[0] == GX - 1
    first_y, last_y = pos[1] == 0, pos[1] == GY - 1
    for f in range(NF):
        ref, base = field_ref(refs, f)
        ux[f, 48 : 48 + ROWS] = ref[base : base + ROWS]
        for s in range(2):
            rows = slice(s * 8, s * 8 + 8)
            for y in range(16):
                uy[f, (3 + y) * 16 + s * 8 : (3 + y) * 16 + s * 8 + 8] = ref[pl.ds(base + s * 128 + y, 8, stride=16)]
            lo, hi = ref[base + s * 8 : base + s * 8 + 8], ref[base + 240 + s * 8 : base + 248 + s * 8]
            ylo, yhi = ref[pl.ds(base + s * 128, 8, stride=16)], ref[pl.ds(base + s * 128 + 15, 8, stride=16)]
            for k in range(3):
                ux[f, k * 16 + s * 8 : k * 16 + s * 8 + 8] = jnp.where(first_x, lo, xl[f * 3 + k, rows])
                ux[f, (19 + k) * 16 + s * 8 : (19 + k) * 16 + s * 8 + 8] = jnp.where(last_x, hi, xr[f * 3 + k, rows])
                uy[f, k * 16 + s * 8 : k * 16 + s * 8 + 8] = jnp.where(first_y, ylo, yl[f * 3 + k, rows])
                uy[f, (19 + k) * 16 + s * 8 : (19 + k) * 16 + s * 8 + 8] = jnp.where(last_y, yhi, yr[f * 3 + k, rows])

    def sweep(buf, d, s, emit):
        def faces(i):
            def load(f):
                cells = [buf[f, pl.ds(pl.multiple_of((i + k) * 16 + s * 8, 8), 8)] for k in range(6)]
                return states(*cells)

            return fluxes(load, d)

        def step(i, before):
            now = faces(i)
            for f in range(NF):
                emit(f, i - 1, before[f] - now[f])
            return tuple(now)

        lax.fori_loop(1, 17, step, tuple(faces(0)))

    for s in range(2):

        def emit_y(f, y, value, s=s):
            out[pl.ds(f * ROWS + s * 128 + y, 8, stride=16)] = value

        sweep(uy, 1, s, emit_y)
    for s in range(2):

        def emit_x(f, x, value, s=s):
            at = pl.ds(pl.multiple_of(f * ROWS + x * 16 + s * 8, 8), 8)
            out[at] = out[at] + value

        sweep(ux, 0, s, emit_x)

    lane = lane_ids((8, 128))
    group = lane // 8
    for s in range(2):

        def load_edge(f, s=s):
            packed = jnp.zeros((8, 128), F32)
            for x in range(16):
                u = ux[f, (3 + x) * 16 + s * 8 : (3 + x) * 16 + s * 8 + 8]
                packed = jnp.where(group == x, pltpu.roll(u, x * 8, 1), packed)
            one, two = pltpu.roll(packed, 127, 1), pltpu.roll(packed, 126, 1)
            return states(packed, packed, packed, packed, one, two)

        for f, value in enumerate(fluxes(load_edge, 2)):
            edge[f, s * 8 : s * 8 + 8] = value
    low_end, high_end = lane == 0, lane == 127

    def along_z(i, carry):
        x, s = i // 2, i % 2
        at = pl.multiple_of(i * 8, 8)

        def load(f):
            u = ux[f, pl.ds(48 + at, 8)]
            m1 = jnp.where(low_end, u, pltpu.roll(u, 1, 1))
            m2 = jnp.where(low_end, u, pltpu.roll(m1, 1, 1))
            p1 = jnp.where(high_end, u, pltpu.roll(u, 127, 1))
            p2 = jnp.where(high_end, u, pltpu.roll(p1, 127, 1))
            p3 = jnp.where(high_end, u, pltpu.roll(p2, 127, 1))
            return states(m2, m1, u, p1, p2, p3)

        for f, value in enumerate(fluxes(load, 2)):
            lower = pltpu.roll(edge[f, pl.ds(pl.multiple_of(s * 8, 8), 8)], lax.rem(128 - x * 8, 128), 1)
            below = jnp.where(low_end, lower, pltpu.roll(value, 1, 1))
            rows = pl.ds(pl.multiple_of(f * ROWS + i * 8, 8), 8)
            out[rows] = out[rows] + (below - value)
        return carry

    lax.fori_loop(0, 32, along_z, 0)


def tree_kernel(
    pos, far, mid, xl, xr, den, mom, ene, ent, tra, tend,
    w_high, w_low, sel_zero, lane_odd, up, alpha_odd, agg, mask, info, expand, gamma_odd, down, spread, poly,
    section, accel, rhs, field,
):
    px, py = pos[0], pos[1]
    around = jnp.concatenate(
        [
            jnp.concatenate([ref[(dy * 3 + c) * 8 : (dy * 3 + c) * 8 + 8] for ref in (xl, mid, xr) for dy in range(3)], 0)
            for c in range(3)
        ],
        1,
    )
    zero = mxu(sel_zero[...], jnp.concatenate(split(around), 1))
    zero = zero[:, :384] + zero[:, 384:]
    arrays = [zero[c * WIN : c * WIN + WIN] * lane_odd[c : c + 1] for c in range(4)]
    gathered = jnp.concatenate([far[:, c].reshape(128, 128) for c in range(3)], 1)
    speeds = far[:, 2].reshape(128, 128)
    fastest = jnp.max(jnp.where(lane_ids((128, 128)) >= 64, speeds, 0.0))

    def lifted(x, x_odd, y_odd):
        sign = (1.0 - 2.0 * x_odd * alpha_odd[0:1]) * (1.0 - 2.0 * y_odd * alpha_odd[1:2])
        n = x.shape[0]
        z = mxu(jnp.concatenate(split(x * sign), 0), up[...])
        return (z[:n] + z[n:]) * sign

    def picked(matrix, x):
        y = mxu(matrix, jnp.concatenate(split(x), 1))
        return y[:, :384] + y[:, 384:]

    dev = lax.broadcasted_iota(jnp.int32, (128, 1), 0)
    raised = lifted(gathered, ((dev // 8) % 2).astype(F32), (dev % 2).astype(F32))
    two = picked(agg[...], raised)
    cell = lax.broadcasted_iota(jnp.int32, (32, 1), 0)
    raised_two = lifted(two, ((cell // 4) % 2).astype(F32), (cell % 2).astype(F32))

    def window(level, columns, count_y, shift):
        tx, ty = px >> (level - 1), py >> (level - 1)
        row = lax.broadcasted_iota(jnp.int32, (WIN, columns), 0)
        col = lax.broadcasted_iota(jnp.int32, (WIN, columns), 1)
        i, j = row // 6, row % 6
        i = jnp.where((tx & 1) == 1, 5 - i, i) + 2 * ((tx >> 1) - 1)
        j = jnp.where((ty & 1) == 1, 5 - j, j) + 2 * ((ty >> 1) - 1)
        sx, sy = (col // count_y) >> shift, (col % count_y) >> shift
        return ((row < 36) & (sx == i) & (sy == j)).astype(F32).astype(BF16)

    levels = (
        picked(window(1, 128, 8, 0), gathered)
        + picked(window(2, 128, 8, 1), raised)
        + picked(window(3, 32, 4, 1), raised_two)
    )
    sign = jnp.ones((1, 384), F32)
    for level in (1, 2, 3):
        bx = ((px >> (level - 1)) & 1).astype(F32)
        by = ((py >> (level - 1)) & 1).astype(F32)
        sign = sign * (1.0 - 2.0 * bx * lane_odd[4 + level : 5 + level])
        sign = sign * (1.0 - 2.0 * by * lane_odd[8 + level : 9 + level])
    levels = levels * sign
    wrow = lax.broadcasted_iota(jnp.int32, (WIN, 384), 0)
    wi, wj = wrow // 6, wrow % 6
    touching = (wi >= 1) & (wi <= 3) & (wj >= 1) & (wj <= 3)
    arrays += [levels, jnp.where(touching, 0.0, levels)]
    lane = lane_ids((WIN, 128)) // 16
    for a in range(NA):
        c, off = a // 8, (a % 8) * 16
        block = jnp.zeros((WIN, 128), F32)
        for g, array in enumerate(arrays):
            block = jnp.where(lane == g, pltpu.roll(array[:, c * 128 : c * 128 + 128], (16 * g - off) % 128, 1), block)
        rhs[a * WIN : a * WIN + WIN] = block
    high, low = split(rhs[...])
    y = mxu(w_high[...], jnp.concatenate([high, low], 1))
    y = y[:, :128] + y[:, 128:] + mxu(w_low[...], high)
    base = jnp.zeros((NG, 128), F32)
    for k in range(7):
        base = base + mask[k : k + 1] * pltpu.roll(y[k * NG : k * NG + NG], (3 - k) % 128, 1)
    lanes = lane_ids((NG, 128)) // 16
    base = base + jnp.where(lanes == 4, pltpu.roll(base, 112, 1), 0.0)
    bx, by = info[1:2], info[2:3]
    for level in (1, 2, 3):
        bx = bx + info[2 + 2 * level : 3 + 2 * level] * ((px >> (level - 1)) & 1).astype(F32)
        by = by + info[2 + 2 * level : 3 + 2 * level] * ((py >> (level - 1)) & 1).astype(F32)
    flip = (1.0 - 2.0 * bx * gamma_odd[0:NG]) * (1.0 - 2.0 * by * gamma_odd[NG : 2 * NG])
    base = base * info[0:1] * flip
    flip = flip * (1.0 - 2.0 * info[9:10] * gamma_odd[2 * NG :])
    total = base
    for _ in range(3):
        total = base + flip * exact(down[...], flip * exact(total, expand[...]))
    rows = jnp.concatenate([pltpu.roll(total, (128 - 16 * c) % 128, 1) for c in range(4)], 0)[:, :16]
    spreads = exact(rows, spread[...])
    terms = jnp.concatenate(
        [
            jnp.concatenate([spreads[c * NG : c * NG + NG, k * 128 : k * 128 + 128] for k in range(3)], 0)
            for c in range(4)
        ],
        1,
    )
    field[...] = exact(poly[...], terms)
    step = jnp.full((8, 128), COURANT / SUB, F32) / fastest
    refs = (den, mom, ene, ent, tra)

    def finish(x, carry):
        for c in range(4):
            at = pl.multiple_of(((c >> 1) * 8 + x) * 16 + (c & 1) * 8, 8)
            acc = [field[pl.ds(pl.multiple_of(i * 64 + x * 8, 8), 8), c * 128 : c * 128 + 128] for i in range(3)]
            rho = den[pl.ds(at, 8)]
            moms = [mom[pl.ds(i * ROWS + at, 8)] for i in range(3)]
            for i in range(3):
                accel[pl.ds(i * ROWS + at, 8)] = acc[i]
            for f in range(NF):
                ref, start = field_ref(refs, f)
                change = tend[pl.ds(f * ROWS + at, 8)]
                if 1 <= f <= 3:
                    change = change + rho * acc[f - 1]
                if f == 4:
                    change = change + moms[0] * acc[0] + moms[1] * acc[1] + moms[2] * acc[2]
                section[pl.ds(f * ROWS + at, 8)] = ref[pl.ds(start + at, 8)] + step * change
        return carry

    lax.fori_loop(0, 8, finish, 0)


VMEM = pl.BlockSpec(memory_space=pltpu.VMEM)
SMEM = pl.BlockSpec(memory_space=pltpu.SMEM)


def call(kernel, ins, shapes, scratch, cost, name, smem=0):
    return pl.pallas_call(
        kernel,
        out_shape=[jax.ShapeDtypeStruct(s, F32) for s in shapes],
        in_specs=[SMEM] * smem + [VMEM] * (len(ins) - smem),
        out_specs=[VMEM] * len(shapes),
        scratch_shapes=scratch,
        cost_estimate=cost,
        name=name,
        compiler_params=pltpu.CompilerParams(vmem_limit_bytes=48 << 20),
    )(*ins)


def shards(density, momentum, energy, entropy, tracers, leaf_flags):
    con = {k: jnp.asarray(v) for k, v in constants().items()}
    fields = [
        density.reshape(ROWS, 128),
        momentum.reshape(3 * ROWS, 128),
        energy.reshape(ROWS, 128),
        entropy.reshape(ROWS, 128),
        tracers.reshape(9 * ROWS, 128),
    ]
    ix, iy = lax.axis_index("mx"), lax.axis_index("my")
    pos = jnp.stack([ix, iy]).astype(jnp.int32)
    pay, xlo, xhi, ylo, yhi = call(
        prepare_kernel,
        fields + [leaf_flags, con["left"], con["right"], con["flag"]],
        [(24, 128), (50, 16, 128), (50, 16, 128), (45, 16, 128), (45, 16, 128)],
        [pltpu.VMEM((8, 128), F32)],
        pl.CostEstimate(flops=10**7, bytes_accessed=3 * 10**6, transcendentals=10**5),
        "prepare",
    )
    up_x, down_x = [(i, i + 1) for i in range(GX - 1)], [(i + 1, i) for i in range(GX - 1)]
    up_y, down_y = [(i, i + 1) for i in range(GY - 1)], [(i + 1, i) for i in range(GY - 1)]
    yl = lax.ppermute(yhi, "my", up_y)
    yr = lax.ppermute(ylo, "my", down_y)
    column = lax.all_to_all(jnp.broadcast_to(pay[None], (GY, 24, 128)), "my", 0, 0)
    ones = jnp.transpose(column.reshape(GY, 3, 8, 128)[:, :, 4], (1, 0, 2))
    far = lax.all_to_all(jnp.broadcast_to(ones[None], (GX, 3, GY, 128)), "mx", 0, 0)
    padded = jnp.pad(column, ((1, 1), (0, 0), (0, 0)))
    mid = lax.dynamic_slice_in_dim(padded, iy, 3, 0).reshape(72, 128)
    extra = jnp.pad(mid, ((0, 8), (0, 0))).reshape(5, 16, 128)
    xl = lax.ppermute(lax.dynamic_update_slice_in_dim(xhi, extra, 45, 0), "mx", up_x)
    xr = lax.ppermute(lax.dynamic_update_slice_in_dim(xlo, extra, 45, 0), "mx", down_x)
    (tend,) = call(
        flux_kernel,
        [pos] + fields + [xl, xr, yl, yr],
        [(NF * ROWS, 128)],
        [pltpu.VMEM((NF, 22 * 16, 128), F32), pltpu.VMEM((NF, 22 * 16, 128), F32), pltpu.VMEM((NF, 16, 128), F32)],
        pl.CostEstimate(flops=5 * 10**7, bytes_accessed=6 * 10**6, transcendentals=10**6),
        "flux",
        smem=1,
    )
    names = (
        "w_high", "w_low", "sel_zero", "lane_odd", "up", "alpha_odd", "agg", "mask", "info", "expand", "gamma_odd",
        "down", "spread", "poly",
    )
    section, accel = call(
        tree_kernel,
        [pos, far, mid, xl[45:].reshape(80, 128), xr[45:].reshape(80, 128)] + fields + [tend] + [con[n] for n in names],
        [(NF * ROWS, 128), (3 * ROWS, 128)],
        [pltpu.VMEM((NA * WIN, 128), F32), pltpu.VMEM((192, 512), F32)],
        pl.CostEstimate(flops=10**8, bytes_accessed=8 * 10**6, transcendentals=0),
        "tree",
        smem=1,
    )
    return section.reshape(NF, 16, 16, 128), accel.reshape(3, 16, 16, 128)


def solution(mesh):
    placed = (
        P("mx", "my", None),
        P(None, "mx", "my", None),
        P("mx", "my", None),
        P("mx", "my", None),
        P(None, "mx", "my", None),
        P("mx", "my", None),
    )
    return jax.shard_map(
        shards,
        mesh=mesh,
        in_specs=placed,
        out_specs=(P(None, "mx", "my", None), P(None, "mx", "my", None)),
        check_vma=False,
    )
```

```python
import functools
import math

import jax
import jax.numpy as jnp
import ml_dtypes
import numpy as np
from jax import lax
from jax.experimental import pallas as pl
from jax.experimental.pallas import tpu as pltpu
from jax.sharding import PartitionSpec as P

F32 = jnp.float32
BF16 = jnp.bfloat16
HIGHEST = lax.Precision.HIGHEST
GRAVITY = 0.02
GAMMA = 5.0 / 3.0
COURANT = 0.3
SUB = 8
NF = 15
GX, GY = 16, 8
ROWS = 256

ALPHA = [
    (px, py, d - px - py)
    for d in range(4)
    for px in range(d, -1, -1)
    for py in range(d - px, -1, -1)
]
NA = len(ALPHA)
NG = 24
WIN = 40
PAIRS = [(px, py) for px in range(4) for py in range(4 - px)]


def factorial_of(e):
    return math.factorial(e[0]) * math.factorial(e[1]) * math.factorial(e[2])


def inverse_derivative(exponent, r):
    axes = [0] * exponent[0] + [1] * exponent[1] + [2] * exponent[2]
    norm = math.sqrt(r[0] ** 2 + r[1] ** 2 + r[2] ** 2)
    if norm == 0.0:
        return 0.0
    if not axes:
        return 1.0 / norm
    if len(axes) == 1:
        return -r[axes[0]] / norm**3
    if len(axes) == 2:
        a, b = axes
        return 3.0 * r[a] * r[b] / norm**5 - float(a == b) / norm**3
    a, b, c = axes
    crossed = float(a == b) * r[c] + float(a == c) * r[b] + float(b == c) * r[a]
    return -15.0 * r[a] * r[b] * r[c] / norm**7 + 3.0 * crossed / norm**5


def split_np(x):
    high = x.astype(np.float32).astype(ml_dtypes.bfloat16)
    low = (x - high.astype(np.float64)).astype(ml_dtypes.bfloat16)
    return high, low


@functools.cache
def constants():
    out = {}
    w = np.zeros((7, NG, NA, WIN))
    for z in range(7):
        for i in range(6):
            for j in range(6):
                r = (-(i - 2.0), -(j - 2.0), -(z - 3.0))
                for g, eg in enumerate(ALPHA):
                    for a, ea in enumerate(ALPHA):
                        if sum(eg) + sum(ea) <= 3:
                            e = tuple(eg[k] + ea[k] for k in range(3))
                            w[z, g, a, i * 6 + j] = (
                                -GRAVITY * (-1.0) ** sum(ea) / factorial_of(ea) * inverse_derivative(e, r)
                            )
    out["w_high"], out["w_low"] = split_np(w.reshape(7 * NG, NA * WIN))
    sel = np.zeros((4, WIN, 40))
    sign = np.zeros((4, 384))
    for c in range(4):
        cx, cy = c >> 1, c & 1
        for i in range(6):
            for j in range(6):
                si, sj = (5 - i if cx else i), (5 - j if cy else j)
                sel[c, i * 6 + j, ((si // 2) * 3 + sj // 2) * 4 + (si % 2) * 2 + sj % 2] = 1.0
        for a, e in enumerate(ALPHA):
            sign[c, a * 16 : a * 16 + 16] = (-1.0) ** (cx * e[0] + cy * e[1])
    out["sel_zero"] = sel.reshape(4 * WIN, 40).astype(ml_dtypes.bfloat16)
    lanes = np.zeros((16, 384), np.float32)
    lanes[0:4] = sign
    for a, e in enumerate(ALPHA):
        for r in range(16):
            lane = a * 16 + r
            level = 1 if r < 8 else 2 if r < 12 else 3
            lanes[4 + level, lane] = e[0] % 2
            lanes[8 + level, lane] = e[1] % 2
    out["lane_odd"] = lanes
    up = np.zeros((384, 384))
    for t, et in enumerate(ALPHA):
        for s, es in enumerate(ALPHA):
            if all(es[k] <= et[k] for k in range(3)):
                for base, to, count in ((0, 8, 8), (8, 12, 4)):
                    for z in range(count):
                        v = 2.0 ** -sum(et)
                        for k in range(3):
                            d = -0.5 if k < 2 or z % 2 == 0 else 0.5
                            v *= math.comb(et[k], es[k]) * d ** (et[k] - es[k])
                        up[s * 16 + base + z, t * 16 + to + z // 2] = v
    assert np.array_equal(up, up.astype(ml_dtypes.bfloat16).astype(np.float64))
    out["up"] = up.astype(ml_dtypes.bfloat16)
    odd = np.zeros((16, 384), np.float32)
    for a, e in enumerate(ALPHA):
        odd[0, a * 16 : a * 16 + 16] = e[0] % 2
        odd[1, a * 16 : a * 16 + 16] = e[1] % 2
    out["alpha_odd"] = odd
    agg = np.zeros((32, 128))
    for x in range(GX):
        for y in range(GY):
            agg[(x // 2) * 4 + y // 2, x * 8 + y] = 1.0
    out["agg"] = agg.astype(ml_dtypes.bfloat16)
    mask = np.zeros((8, 128), np.float32)
    info = np.zeros((16, 128), np.float32)
    expand = np.zeros((128, 128), np.float32)
    for lane in range(96):
        g, r = lane // 16, lane % 16
        if g < 4:
            n, z, level = 16, r, 0
        elif r < 8:
            n, z, level = 8, r, 1
        elif r < 12:
            n, z, level = 4, r - 8, 2
        elif r < 14:
            n, z, level = 2, r - 12, 3
        else:
            continue
        for k in range(7):
            o = k - 3
            ok = 0 <= z + o < n and abs((z + o) // 2 - z // 2) <= 1
            if g == 4:
                ok = ok and abs(o) > 1
            if g == 5:
                ok = ok and abs(o) <= 1
            mask[k, lane] = float(ok)
        if g < 5:
            info[0, lane] = 2.0**-level
            info[1, lane] = float(g >> 1) if level == 0 else 0.0
            info[2, lane] = float(g & 1) if level == 0 else 0.0
            info[2 + 2 * level, lane] = 1.0 if level else info[2, lane]
            info[9, lane] = float(z % 2)
            if level == 0:
                expand[64 + z // 2, lane] = 1.0
            elif level == 1:
                expand[64 + 8 + z // 2, lane] = 1.0
            elif level == 2:
                expand[64 + 12 + z // 2, lane] = 1.0
    out["mask"] = mask
    out["info"] = info
    out["expand"] = expand
    gamma_odd = np.zeros((3 * NG, 128), np.float32)
    down = np.zeros((NG, NG), np.float32)
    for g, eg in enumerate(ALPHA):
        for k in range(3):
            gamma_odd[k * NG + g] = eg[k] % 2
        for b, eb in enumerate(ALPHA):
            if all(eb[k] >= eg[k] for k in range(3)):
                v = 2.0 ** -sum(eg)
                for k in range(3):
                    n = eb[k] - eg[k]
                    v *= (-0.25) ** n / math.factorial(n)
                down[g, b] = v
    out["gamma_odd"] = gamma_odd
    out["down"] = down
    h = (np.arange(SUB) + 0.5) / SUB - 0.5
    spread = np.zeros((16, 384))
    for k in range(3):
        for z in range(128):
            spread[z // 8, k * 128 + z] = h[z % 8] ** k
    out["spread"] = spread.astype(np.float32)
    poly = np.zeros((3, 8, 8, 3, NG))
    for i in range(3):
        for g, e in enumerate(ALPHA):
            if e[i] > 0:
                low = list(e)
                low[i] -= 1
                poly[i, :, :, low[2], g] = (
                    -e[i] / factorial_of(e) * h[:, None] ** low[0] * h[None, :] ** low[1]
                )
    out["poly"] = poly.reshape(192, 72).astype(np.float32)
    cells = np.arange(16)
    near = h[cells % 8]
    far = ((cells + 0.5) / 8 - 1.0) / 2
    left = np.zeros((2, len(PAIRS), 8, 16, 16))
    for q, (px, py) in enumerate(PAIRS):
        for c in range(4):
            block = ((cells // 8 == c >> 1)[:, None] & (cells // 8 == (c & 1))[None, :]).astype(float)
            left[0, q, c] = block * near[:, None] ** px * near[None, :] ** py
            left[1, q, c] = block * far[:, None] ** px * far[None, :] ** py
    out["left"] = left.reshape(160, 256).astype(np.float32)
    right = np.zeros((128, 128))
    flag = np.zeros((128, 128))
    for z in range(128):
        s = z // 8
        f = ((z % 16 + 0.5) / 8 - 1.0) / 2
        for pz in range(4):
            right[z, pz * 16 + s] = h[z % 8] ** pz / SUB**3
            right[z, 64 + (s % 2) * 32 + pz * 8 + s // 2] = f**pz / SUB**3
    for s in range(16):
        for pz in range(4):
            flag[s, pz * 16 + s] = 1.0
            flag[s, 64 + (s % 2) * 32 + pz * 8 + s // 2] = 1.0
    out["right"] = right.astype(np.float32)
    out["flag"] = flag.astype(ml_dtypes.bfloat16)
    return out


def split(x):
    high = x.astype(BF16)
    return high, (x - high.astype(F32)).astype(BF16)


def mxu(a, b):
    return jnp.dot(a, b, preferred_element_type=F32)


def exact(a, b):
    return jnp.dot(a, b, precision=HIGHEST, preferred_element_type=F32)


def lane_ids(shape):
    return lax.broadcasted_iota(jnp.int32, shape, len(shape) - 1)


def row_ids(shape):
    return lax.broadcasted_iota(jnp.int32, shape, len(shape) - 2)


def power(s):
    return jnp.exp2(GAMMA * jnp.log2(s))


def root(x):
    return x * lax.rsqrt(x)


PLACES = ((0, 1), (1, 3), (4, 1), (5, 1), (6, 9))


def load_all(pairs, sems):
    copies = [pltpu.make_async_copy(source, target, sems.at[k]) for k, (source, target) in enumerate(pairs)]
    for copy in copies:
        copy.start()
    return copies


def fields_into(refs, target, source=slice(0, ROWS), rows=None):
    place = slice(0, source.stop - source.start) if rows is None else rows
    return [
        (ref.at[:, source], target.at[start : start + count, place]) for ref, (start, count) in zip(refs, PLACES)
    ]


def prepare_kernel(den, mom, ene, ent, tra, flags, left, right, flag, pay, xlo, xhi, ylo, yhi, u, fl, flv, leftv, rightv, flagv, sems):
    small = load_all(zip((flags, left, right, flag), (flv, leftv, rightv, flagv)), sems.at[7:11])
    loads = load_all(fields_into((den, mom, ene, ent, tra), u), sems.at[0:5])
    for copy in small:
        copy.wait()
    fl[...] = jnp.zeros((8, 128), F32)
    fl[0:2, 0:16] = flv[0].astype(F32)
    fl[2:4, 0:16] = flv[1].astype(F32)
    tile = mxu(fl[...].astype(BF16), flagv[...])
    for k in (0, 1, 3):
        loads[k].wait()
    rho = u[0]
    sums = exact(leftv[...], exact(rho, rightv[...]))
    inverse = 1.0 / rho
    fast = jnp.maximum(jnp.maximum(jnp.abs(u[1]), jnp.abs(u[2])), jnp.abs(u[3]))
    sound = root(GAMMA * (GAMMA - 1.0) * power(u[5]) * inverse)
    fastest = jnp.max(fast * inverse + sound)
    lane = lane_ids((8, 128))
    row = row_ids((8, 128))
    tiles = [jnp.zeros((8, 128), F32) for _ in range(3)]
    zero, one = {}, {}
    for q, pair in enumerate(PAIRS):
        zero[pair] = sums[q * 8 : q * 8 + 8] * tile
        v = jnp.sum(sums[80 + q * 8 : 88 + q * 8] * tile, axis=0, keepdims=True)
        v = jnp.broadcast_to(v, (8, 128))
        one[pair] = v + pltpu.roll(v, 96, 1)
    for a, e in enumerate(ALPHA):
        c, to = a // 8, (a % 8) * 16
        low = pltpu.roll(zero[e[0], e[1]], (to - e[2] * 16) % 128, 1)
        top = pltpu.roll(one[e[0], e[1]], (to - 64 - e[2] * 8) % 128, 1)
        here = (lane >= to) & (lane < to + 16)
        tiles[c] = jnp.where(here & (row < 4), low, tiles[c])
        tiles[c] = jnp.where(here & (row == 4) & (lane < to + 8), top, tiles[c])
    tiles[2] = jnp.where((row == 4) & (lane >= 64), fastest, tiles[2])
    for y in range(GY):
        for c in range(3):
            pay[y, c * 8 : c * 8 + 8] = tiles[c]
    for k in (2, 4):
        loads[k].wait()
    slabs = load_all([(u.at[:, 0:48], xlo), (u.at[:, 208:256], xhi)], sems.at[5:7])
    for f in range(NF):
        for k in range(3):
            for s in range(2):
                ylo[f, k * 16 + s * 8 : k * 16 + s * 8 + 8] = u[f, pl.ds(s * 128 + k, 8, stride=16)]
                yhi[f, k * 16 + s * 8 : k * 16 + s * 8 + 8] = u[f, pl.ds(s * 128 + 13 + k, 8, stride=16)]
    for copy in slabs:
        copy.wait()


def relay_kernel(pos, column, *rest):
    out = rest[-1]
    y = pos[1]
    tiles = [column[pl.ds(c * 8 + 4, 8, stride=24)] for c in range(3)]
    near = []
    for dy in range(3):
        here = jnp.clip(y + dy - 1, 0, GY - 1)
        inside = here == y + dy - 1
        for c in range(3):
            tile = column[pl.ds(pl.multiple_of(here * 24 + c * 8, 8), 8)]
            near.append(jnp.where(inside, tile, 0.0))
    for x in range(GX):
        for c in range(3):
            out[x, c * 8 : c * 8 + 8] = tiles[c]
        for n, tile in enumerate(near):
            out[x, 24 + n * 4 : 28 + n * 4] = tile[0:4]
        out[x, 60:64] = jnp.zeros((4, 128), F32)


def states(ol, il, l, r, ir, orr):
    face = (37.0 / 60.0) * (l + r) - (8.0 / 60.0) * (il + ir) + (1.0 / 60.0) * (ol + orr)
    low, high = jnp.minimum(l, r), jnp.maximum(l, r)
    left = jnp.minimum(jnp.maximum(face, jnp.minimum(il, low)), jnp.maximum(il, high))
    right = jnp.minimum(jnp.maximum(face, jnp.minimum(low, ir)), jnp.maximum(high, ir))
    return left, right


def fluxes(load, d, store):
    rl, rr = load(0)
    ml, mr = load(1 + d)
    sl, sr = load(5)
    il, ir = 1.0 / rl, 1.0 / rr
    vl, vr = ml * il, mr * ir
    gl, gr = power(sl), power(sr)
    cl, cr = root(GAMMA * (GAMMA - 1.0) * gl * il), root(GAMMA * (GAMMA - 1.0) * gr * ir)
    a = 4.0 * jnp.maximum(jnp.abs(vl) + cl, jnp.abs(vr) + cr)
    wl, wr = 4.0 * vl, 4.0 * vr
    kl, kr = wl + a, wr - a
    got = {0: (rl, rr), 1 + d: (ml, mr), 5: (sl, sr)}
    for f in range(NF):
        left, right = got[f] if f in got else load(f)
        flux = left * kl + right * kr
        if f == 1 + d:
            flux = flux + (4.0 * (GAMMA - 1.0)) * (gl + gr)
        if f == 4:
            flux = flux + (GAMMA - 1.0) * (gl * wl + gr * wr)
        store(f, flux)


def sweep(buf, target, d):
    def step(i, carry):
        for s in range(2):

            def load(f):
                return states(*[buf[f, pl.ds(pl.multiple_of((i + k) * 16 + s * 8, 8), 8)] for k in range(6)])

            def store(f, flux):
                target[f, pl.ds(pl.multiple_of(i * 16 + s * 8, 8), 8)] = flux

            fluxes(load, d, store)
        return carry

    lax.fori_loop(0, 17, step, 0)


def flux_z_kernel(den, mom, ene, ent, tra, out_h, u, uz, fz, turn, out, sems):
    row = row_ids((8, 128))
    loads = load_all(fields_into((den, mom, ene, ent, tra), u), sems.at[0:5])

    def into(f, carry):
        for half in range(2):
            turn[half] = u[f, half * 128 : half * 128 + 128].T
            cells = [turn[half, pl.ds(m, 8, stride=16)] for m in range(16)]
            first = jnp.broadcast_to(cells[0][0:1], (8, 128))
            last = jnp.broadcast_to(cells[15][7:8], (8, 128))
            below = [jnp.where(row == 0, first, pltpu.roll(cells[m], 1, 0)) for m in (13, 14, 15)]
            above = [jnp.where(row == 7, last, pltpu.roll(cells[m], 7, 0)) for m in (0, 1, 2)]
            for m, value in enumerate(below + cells + above):
                uz[f, m * 16 + half * 8 : m * 16 + half * 8 + 8] = value
        return carry

    for copy, (start, n) in zip(loads, PLACES):
        copy.wait()
        lax.fori_loop(start, start + n, into, 0)
    sweep(uz, fz, 2)

    def back(f, carry):
        for half in range(2):
            at = half * 8
            for m in range(16):
                low = fz[f, m * 16 + at : m * 16 + at + 8]
                high = fz[f, m * 16 + 16 + at : m * 16 + 24 + at]
                turn[half, pl.ds(m, 8, stride=16)] = low - high
            out[f, half * 128 : half * 128 + 128] = turn[half].T
        return carry

    stores = []
    for part in range(3):
        lax.fori_loop(part * 5, part * 5 + 5, back, 0)
        some = slice(part * 5, part * 5 + 5)
        stores.append(pltpu.make_async_copy(out.at[some], out_h.at[some], sems.at[5 + part]))
        stores[-1].start()
    for copy in stores:
        copy.wait()


def flux_xy_kernel(pos, den, mom, ene, ent, tra, along_z_h, xl, xr, yl, yr, out_h, ux, uy, fx, fy, along_z, out, sems):
    interior = load_all(fields_into((den, mom, ene, ent, tra), ux, rows=slice(48, 304)), sems.at[0:5])
    loads = load_all(
        [
            (yl, uy.at[:, 0:48]),
            (yr, uy.at[:, 304:352]),
            (xl, ux.at[:, 0:48]),
            (xr, ux.at[:, 304:352]),
            (along_z_h, along_z),
        ],
        sems.at[5:10],
    )
    for copy, (start, n) in zip(interior, PLACES):
        copy.wait()
        for f in range(start, start + n):
            for y in range(16):
                for s in range(2):
                    at = (3 + y) * 16 + s * 8
                    uy[f, at : at + 8] = ux[f, pl.ds(48 + s * 128 + y, 8, stride=16)]
    for copy in loads[:-1]:
        copy.wait()

    def repeat(buf, source, target):
        for f in range(NF):
            cells = buf[f, source : source + 16]
            for k in range(3):
                buf[f, target + k * 16 : target + k * 16 + 16] = cells

    pl.when(pos[0] == 0)(lambda: repeat(ux, 48, 0))
    pl.when(pos[0] == GX - 1)(lambda: repeat(ux, 288, 304))
    pl.when(pos[1] == 0)(lambda: repeat(uy, 48, 0))
    pl.when(pos[1] == GY - 1)(lambda: repeat(uy, 288, 304))
    sweep(uy, fy, 1)
    sweep(ux, fx, 0)
    loads[-1].wait()

    def gather(x, carry):
        for f in range(NF):
            for s in range(2):
                at = pl.multiple_of(x * 16 + s * 8, 8)
                change = along_z[f, pl.ds(at, 8)] + (fx[f, pl.ds(at, 8)] - fx[f, pl.ds(at + 16, 8)])
                low, high = fy[f, pl.ds(s * 128 + x, 8, stride=16)], fy[f, pl.ds(s * 128 + 16 + x, 8, stride=16)]
                out[f, pl.ds(at, 8)] = change + (low - high)
        return carry

    stores = []
    for part in range(4):
        lax.fori_loop(part * 4, part * 4 + 4, gather, 0)
        rows = slice(part * 64, part * 64 + 64)
        stores.append(pltpu.make_async_copy(out.at[:, rows], out_h.at[:, rows], sems.at[10 + part]))
        stores[-1].start()
    for copy in stores:
        copy.wait()


TREE_CONSTANTS = (
    "w_high", "w_low", "sel_zero", "lane_odd", "up", "alpha_odd", "agg", "mask", "info", "expand", "gamma_odd", "down",
    "spread", "poly",
)


def tree_kernel(
    pos, far_h, den, mom, ene, ent, tra, change_h, *args,
):
    count = len(TREE_CONSTANTS)
    section, accel, rhs, field, result, force, far, change, u, sems = args[count : count + 10]
    loaded = args[count + 10 :]
    late = fields_into((den, mom, ene, ent, tra), u) + [(change_h, change)]
    loads = load_all([(far_h, far)] + list(zip(args[:count], loaded)) + late, sems)
    for copy in loads[: 1 + count]:
        copy.wait()
    (w_high, w_low, sel_zero, lane_odd, up, alpha_odd, agg, mask, info, expand, gamma_odd, down, spread, poly) = loaded
    px, py = pos[0], pos[1]
    blocks = []
    for dx in range(3):
        here = jnp.clip(px + dx - 1, 0, GX - 1)
        inside = here == px + dx - 1
        blocks.append([jnp.where(inside, far[here, 24 + n * 4 : 28 + n * 4], 0.0) for n in range(9)])
    gap = jnp.zeros((4, 128), F32)
    around = jnp.concatenate(
        [jnp.concatenate([blocks[dx][dy * 3 + c] for dx in range(3) for dy in range(3)] + [gap], 0) for c in range(3)], 1
    )
    zero = mxu(sel_zero[...], jnp.concatenate(split(around), 1))
    zero = zero[:, :384] + zero[:, 384:]
    arrays = [zero[c * WIN : c * WIN + WIN] * lane_odd[c : c + 1] for c in range(4)]
    gathered = jnp.concatenate([far[:, c * 8 : c * 8 + 8].reshape(128, 128) for c in range(3)], 1)
    speeds = gathered[:, 256:]
    fastest = jnp.max(jnp.where(lane_ids((128, 128)) >= 64, speeds, 0.0))

    def lifted(x, x_odd, y_odd):
        sign = (1.0 - 2.0 * x_odd * alpha_odd[0:1]) * (1.0 - 2.0 * y_odd * alpha_odd[1:2])
        n = x.shape[0]
        z = mxu(jnp.concatenate(split(x * sign), 0), up[...])
        return (z[:n] + z[n:]) * sign

    def picked(matrix, x):
        y = mxu(matrix, jnp.concatenate(split(x), 1))
        return y[:, :384] + y[:, 384:]

    dev = lax.broadcasted_iota(jnp.int32, (128, 1), 0)
    raised = lifted(gathered, ((dev // 8) % 2).astype(F32), (dev % 2).astype(F32))
    two = picked(agg[...], raised)
    cell = lax.broadcasted_iota(jnp.int32, (32, 1), 0)
    raised_two = lifted(two, ((cell // 4) % 2).astype(F32), (cell % 2).astype(F32))

    def window(level, columns, count_y, shift):
        tx, ty = px >> (level - 1), py >> (level - 1)
        row = lax.broadcasted_iota(jnp.int32, (WIN, columns), 0)
        col = lax.broadcasted_iota(jnp.int32, (WIN, columns), 1)
        i, j = row // 6, row % 6
        i = jnp.where((tx & 1) == 1, 5 - i, i) + 2 * ((tx >> 1) - 1)
        j = jnp.where((ty & 1) == 1, 5 - j, j) + 2 * ((ty >> 1) - 1)
        sx, sy = (col // count_y) >> shift, (col % count_y) >> shift
        return ((row < 36) & (sx == i) & (sy == j)).astype(F32).astype(BF16)

    levels = (
        picked(window(1, 128, 8, 0), gathered)
        + picked(window(2, 128, 8, 1), raised)
        + picked(window(3, 32, 4, 1), raised_two)
    )
    sign = jnp.ones((1, 384), F32)
    for level in (1, 2, 3):
        bx = ((px >> (level - 1)) & 1).astype(F32)
        by = ((py >> (level - 1)) & 1).astype(F32)
        sign = sign * (1.0 - 2.0 * bx * lane_odd[4 + level : 5 + level])
        sign = sign * (1.0 - 2.0 * by * lane_odd[8 + level : 9 + level])
    levels = levels * sign
    wrow = lax.broadcasted_iota(jnp.int32, (WIN, 384), 0)
    wi, wj = wrow // 6, wrow % 6
    touching = (wi >= 1) & (wi <= 3) & (wj >= 1) & (wj <= 3)
    arrays += [levels, jnp.where(touching, 0.0, levels)]
    lane = lane_ids((WIN, 128)) // 16
    for a in range(NA):
        c, off = a // 8, (a % 8) * 16
        block = jnp.zeros((WIN, 128), F32)
        for g, array in enumerate(arrays):
            block = jnp.where(lane == g, pltpu.roll(array[:, c * 128 : c * 128 + 128], (16 * g - off) % 128, 1), block)
        rhs[a * WIN : a * WIN + WIN] = block
    high, low = split(rhs[...])
    y = mxu(w_high[...], jnp.concatenate([high, low], 1))
    y = y[:, :128] + y[:, 128:] + mxu(w_low[...], high)
    base = jnp.zeros((NG, 128), F32)
    for k in range(7):
        base = base + mask[k : k + 1] * pltpu.roll(y[k * NG : k * NG + NG], (3 - k) % 128, 1)
    lanes = lane_ids((NG, 128)) // 16
    base = base + jnp.where(lanes == 4, pltpu.roll(base, 112, 1), 0.0)
    bx, by = info[1:2], info[2:3]
    for level in (1, 2, 3):
        bx = bx + info[2 + 2 * level : 3 + 2 * level] * ((px >> (level - 1)) & 1).astype(F32)
        by = by + info[2 + 2 * level : 3 + 2 * level] * ((py >> (level - 1)) & 1).astype(F32)
    flip = (1.0 - 2.0 * bx * gamma_odd[0:NG]) * (1.0 - 2.0 * by * gamma_odd[NG : 2 * NG])
    base = base * info[0:1] * flip
    flip = flip * (1.0 - 2.0 * info[9:10] * gamma_odd[2 * NG :])
    total = base
    for _ in range(3):
        total = base + flip * exact(down[...], flip * exact(total, expand[...]))
    rows = jnp.concatenate([pltpu.roll(total, (128 - 16 * c) % 128, 1) for c in range(4)], 0)[:, :16]
    spreads = exact(rows, spread[...])
    terms = jnp.concatenate(
        [
            jnp.concatenate([spreads[c * NG : c * NG + NG, k * 128 : k * 128 + 128] for k in range(3)], 0)
            for c in range(4)
        ],
        1,
    )
    field[...] = exact(poly[...], terms)
    step = jnp.full((8, 128), COURANT / SUB, F32) / fastest
    for copy in loads[1 + count :]:
        copy.wait()
    stores = []
    for half in range(2):

        def finish(x, carry, half=half):
            for s in range(2):
                c = half * 2 + s
                at = pl.multiple_of(half * 128 + x * 16 + s * 8, 8)
                rows = pl.ds(at, 8)
                acc = [field[pl.ds(pl.multiple_of(i * 64 + x * 8, 8), 8), c * 128 : c * 128 + 128] for i in range(3)]
                old = [u[f, rows] for f in range(NF)]
                for i in range(3):
                    force[i, rows] = acc[i]
                for f in range(NF):
                    slope = change[f, rows]
                    if 1 <= f <= 3:
                        slope = slope + old[0] * acc[f - 1]
                    if f == 4:
                        slope = slope + (old[1] * acc[0] + old[2] * acc[1] + old[3] * acc[2])
                    result[f, rows] = old[f] + step * slope
            return carry

        lax.fori_loop(0, 8, finish, 0)
        rows = slice(half * 128, half * 128 + 128)
        for k, (source, target) in enumerate(((result, section), (force, accel))):
            stores.append(pltpu.make_async_copy(source.at[:, rows], target.at[:, rows], sems.at[2 * half + k]))
            stores[-1].start()
    for copy in stores:
        copy.wait()


ANY = pl.BlockSpec(memory_space=pl.ANY)
HBM = pl.BlockSpec(memory_space=pltpu.HBM)
VMEM = pl.BlockSpec(memory_space=pltpu.VMEM)
SMEM = pl.BlockSpec(memory_space=pltpu.SMEM)


def call(kernel, name, ins, outs, scratch, cost):
    return pl.pallas_call(
        kernel,
        out_shape=[pltpu.HBM(s, F32) if spec is HBM else jax.ShapeDtypeStruct(s, F32) for s, spec in outs],
        in_specs=[spec for _, spec in ins],
        out_specs=[spec for _, spec in outs],
        scratch_shapes=scratch,
        cost_estimate=pl.CostEstimate(flops=cost[0], bytes_accessed=cost[1], transcendentals=cost[2]),
        name=name,
        compiler_params=pltpu.CompilerParams(vmem_limit_bytes=32 << 20),
    )(*[in_hbm(x) if spec is HBM else x for x, spec in ins])


def in_hbm(x):
    return pltpu.with_memory_space_constraint(x, pltpu.HBM)


def scratch_like(x):
    return pltpu.VMEM(x.shape, x.dtype)


def shards(density, momentum, energy, entropy, tracers, leaf_flags):
    con = {k: jnp.asarray(v) for k, v in constants().items()}
    fields = [(x.reshape(-1, ROWS, 128), HBM) for x in (density, momentum, energy, entropy, tracers)]
    ix, iy = lax.axis_index("mx"), lax.axis_index("my")
    pos = (jnp.stack([ix, iy]).astype(jnp.int32), SMEM)
    first = [con[n] for n in ("left", "right", "flag")]
    whole = (NF, ROWS, 128)
    slab = ((NF, 48, 128), HBM)
    pay, xlo, xhi, ylo, yhi = call(
        prepare_kernel,
        "prepare",
        fields + [(leaf_flags, HBM)] + [(x, HBM) for x in first],
        [((GY, 24, 128), VMEM), slab, slab, ((NF, 48, 128), VMEM), ((NF, 48, 128), VMEM)],
        [pltpu.VMEM(whole, F32), pltpu.VMEM((8, 128), F32), scratch_like(leaf_flags)] + [scratch_like(x) for x in first] + [pltpu.SemaphoreType.DMA((11,))],
        (10**7, 4 * 10**6, 10**5),
    )
    up_x, down_x = [(i, i + 1) for i in range(GX - 1)], [(i + 1, i) for i in range(GX - 1)]
    up_y, down_y = [(i, i + 1) for i in range(GY - 1)], [(i + 1, i) for i in range(GY - 1)]
    column = lax.all_to_all(pay, "my", 0, 0)
    yl = lax.ppermute(yhi, "my", up_y)
    yr = lax.ppermute(ylo, "my", down_y)
    xl = lax.ppermute(xhi, "mx", up_x)
    xr = lax.ppermute(xlo, "mx", down_x)
    block = pltpu.VMEM(whole, F32)
    extended, faces = pltpu.VMEM((NF, 352, 128), F32), pltpu.VMEM((NF, 272, 128), F32)
    (along_z,) = call(
        flux_z_kernel,
        "flux_z",
        fields,
        [(whole, HBM)],
        [block, extended, faces, pltpu.VMEM((2, 128, 128), F32), block, pltpu.SemaphoreType.DMA((8,))],
        (2 * 10**7, 4 * 10**6, 3 * 10**5),
    )
    (chunks,) = call(
        relay_kernel, "relay", [pos, (column.reshape(GY * 24, 128), VMEM), (along_z, HBM)] + [(x, ANY) for x in (xl, xr, yl, yr)], [((GX, 64, 128), VMEM)], [], (10**4, 10**6, 0)
    )
    far = lax.all_to_all(chunks, "mx", 0, 0)
    (tend,) = call(
        flux_xy_kernel,
        "flux_xy",
        [pos] + fields + [(along_z, HBM)] + [(x, ANY) for x in (xl, xr, yl, yr)],
        [(whole, HBM)],
        [extended, extended, faces, faces, block, block, pltpu.SemaphoreType.DMA((14,))],
        (4 * 10**7, 6 * 10**6, 6 * 10**5),
    )
    second = [con[n] for n in TREE_CONSTANTS]
    section, accel = call(
        tree_kernel,
        "tree",
        [pos, (far, ANY)] + fields + [(tend, HBM)] + [(x, HBM) for x in second],
        [(whole, ANY), ((3, ROWS, 128), ANY)],
        [
            pltpu.VMEM((NA * WIN, 128), F32),
            pltpu.VMEM((192, 512), F32),
            pltpu.VMEM(whole, F32),
            pltpu.VMEM((3, ROWS, 128), F32),
            pltpu.VMEM((GX, 64, 128), F32),
            block,
            block,
            pltpu.SemaphoreType.DMA((7 + len(second),)),
        ]
        + [scratch_like(x) for x in second],
        (10**8, 8 * 10**6, 0),
    )
    return section.reshape(NF, 16, 16, 128), accel.reshape(3, 16, 16, 128)


def solution(mesh):
    placed = (
        P("mx", "my", None),
        P(None, "mx", "my", None),
        P("mx", "my", None),
        P("mx", "my", None),
        P(None, "mx", "my", None),
        P("mx", "my", None),
    )
    return jax.shard_map(
        shards,
        mesh=mesh,
        in_specs=placed,
        out_specs=(P(None, "mx", "my", None), P(None, "mx", "my", None)),
        check_vma=False,
    )
```

```python
import functools
import math

import jax
import jax.numpy as jnp
import ml_dtypes
import numpy as np
from jax import lax
from jax.experimental import pallas as pl
from jax.experimental.pallas import tpu as pltpu
from jax.sharding import PartitionSpec as P

F32 = jnp.float32
BF16 = jnp.bfloat16
HIGHEST = lax.Precision.HIGHEST
GRAVITY = 0.02
GAMMA = 5.0 / 3.0
COURANT = 0.3
SUB = 8
NF = 15
GX, GY = 16, 8
ROWS = 256

ALPHA = [
    (px, py, d - px - py)
    for d in range(4)
    for px in range(d, -1, -1)
    for py in range(d - px, -1, -1)
]
NA = len(ALPHA)
NG = 24
WIN = 40
PAIRS = [(px, py) for px in range(4) for py in range(4 - px)]


def factorial_of(e):
    return math.factorial(e[0]) * math.factorial(e[1]) * math.factorial(e[2])


def inverse_derivative(exponent, r):
    axes = [0] * exponent[0] + [1] * exponent[1] + [2] * exponent[2]
    norm = math.sqrt(r[0] ** 2 + r[1] ** 2 + r[2] ** 2)
    if norm == 0.0:
        return 0.0
    if not axes:
        return 1.0 / norm
    if len(axes) == 1:
        return -r[axes[0]] / norm**3
    if len(axes) == 2:
        a, b = axes
        return 3.0 * r[a] * r[b] / norm**5 - float(a == b) / norm**3
    a, b, c = axes
    crossed = float(a == b) * r[c] + float(a == c) * r[b] + float(b == c) * r[a]
    return -15.0 * r[a] * r[b] * r[c] / norm**7 + 3.0 * crossed / norm**5


def split_np(x):
    high = x.astype(np.float32).astype(ml_dtypes.bfloat16)
    low = (x - high.astype(np.float64)).astype(ml_dtypes.bfloat16)
    return high, low


@functools.cache
def constants():
    out = {}
    w = np.zeros((7, NG, NA, WIN))
    for z in range(7):
        for i in range(6):
            for j in range(6):
                r = (-(i - 2.0), -(j - 2.0), -(z - 3.0))
                for g, eg in enumerate(ALPHA):
                    for a, ea in enumerate(ALPHA):
                        if sum(eg) + sum(ea) <= 3:
                            e = tuple(eg[k] + ea[k] for k in range(3))
                            w[z, g, a, i * 6 + j] = (
                                -GRAVITY * (-1.0) ** sum(ea) / factorial_of(ea) * inverse_derivative(e, r)
                            )
    out["w_high"], out["w_low"] = split_np(w.reshape(7 * NG, NA * WIN))
    sel = np.zeros((4, WIN, 40))
    sign = np.zeros((4, 384))
    for c in range(4):
        cx, cy = c >> 1, c & 1
        for i in range(6):
            for j in range(6):
                si, sj = (5 - i if cx else i), (5 - j if cy else j)
                sel[c, i * 6 + j, ((si // 2) * 3 + sj // 2) * 4 + (si % 2) * 2 + sj % 2] = 1.0
        for a, e in enumerate(ALPHA):
            sign[c, a * 16 : a * 16 + 16] = (-1.0) ** (cx * e[0] + cy * e[1])
    out["sel_zero"] = sel.reshape(4 * WIN, 40).astype(ml_dtypes.bfloat16)
    lanes = np.zeros((16, 384), np.float32)
    lanes[0:4] = sign
    for a, e in enumerate(ALPHA):
        for r in range(16):
            lane = a * 16 + r
            level = 1 if r < 8 else 2 if r < 12 else 3
            lanes[4 + level, lane] = e[0] % 2
            lanes[8 + level, lane] = e[1] % 2
    out["lane_odd"] = lanes
    up = np.zeros((384, 384))
    for t, et in enumerate(ALPHA):
        for s, es in enumerate(ALPHA):
            if all(es[k] <= et[k] for k in range(3)):
                for base, to, count in ((0, 8, 8), (8, 12, 4)):
                    for z in range(count):
                        v = 2.0 ** -sum(et)
                        for k in range(3):
                            d = -0.5 if k < 2 or z % 2 == 0 else 0.5
                            v *= math.comb(et[k], es[k]) * d ** (et[k] - es[k])
                        up[s * 16 + base + z, t * 16 + to + z // 2] = v
    assert np.array_equal(up, up.astype(ml_dtypes.bfloat16).astype(np.float64))
    out["up"] = up.astype(ml_dtypes.bfloat16)
    odd = np.zeros((16, 384), np.float32)
    for a, e in enumerate(ALPHA):
        odd[0, a * 16 : a * 16 + 16] = e[0] % 2
        odd[1, a * 16 : a * 16 + 16] = e[1] % 2
    out["alpha_odd"] = odd
    agg = np.zeros((32, 128))
    for x in range(GX):
        for y in range(GY):
            agg[(x // 2) * 4 + y // 2, x * 8 + y] = 1.0
    out["agg"] = agg.astype(ml_dtypes.bfloat16)
    mask = np.zeros((8, 128), np.float32)
    info = np.zeros((16, 128), np.float32)
    expand = np.zeros((128, 128), np.float32)
    for lane in range(96):
        g, r = lane // 16, lane % 16
        if g < 4:
            n, z, level = 16, r, 0
        elif r < 8:
            n, z, level = 8, r, 1
        elif r < 12:
            n, z, level = 4, r - 8, 2
        elif r < 14:
            n, z, level = 2, r - 12, 3
        else:
            continue
        for k in range(7):
            o = k - 3
            ok = 0 <= z + o < n and abs((z + o) // 2 - z // 2) <= 1
            if g == 4:
                ok = ok and abs(o) > 1
            if g == 5:
                ok = ok and abs(o) <= 1
            mask[k, lane] = float(ok)
        if g < 5:
            info[0, lane] = 2.0**-level
            info[1, lane] = float(g >> 1) if level == 0 else 0.0
            info[2, lane] = float(g & 1) if level == 0 else 0.0
            info[2 + 2 * level, lane] = 1.0 if level else info[2, lane]
            info[9, lane] = float(z % 2)
            if level == 0:
                expand[64 + z // 2, lane] = 1.0
            elif level == 1:
                expand[64 + 8 + z // 2, lane] = 1.0
            elif level == 2:
                expand[64 + 12 + z // 2, lane] = 1.0
    out["mask"] = mask
    out["info"] = info
    out["expand"] = expand
    gamma_odd = np.zeros((3 * NG, 128), np.float32)
    down = np.zeros((NG, NG), np.float32)
    for g, eg in enumerate(ALPHA):
        for k in range(3):
            gamma_odd[k * NG + g] = eg[k] % 2
        for b, eb in enumerate(ALPHA):
            if all(eb[k] >= eg[k] for k in range(3)):
                v = 2.0 ** -sum(eg)
                for k in range(3):
                    n = eb[k] - eg[k]
                    v *= (-0.25) ** n / math.factorial(n)
                down[g, b] = v
    out["gamma_odd"] = gamma_odd
    out["down"] = down
    h = (np.arange(SUB) + 0.5) / SUB - 0.5
    spread = np.zeros((16, 384))
    for k in range(3):
        for z in range(128):
            spread[z // 8, k * 128 + z] = h[z % 8] ** k
    out["spread"] = spread.astype(np.float32)
    poly = np.zeros((3, 8, 8, 3, NG))
    for i in range(3):
        for g, e in enumerate(ALPHA):
            if e[i] > 0:
                low = list(e)
                low[i] -= 1
                poly[i, :, :, low[2], g] = (
                    -e[i] / factorial_of(e) * h[:, None] ** low[0] * h[None, :] ** low[1]
                )
    out["poly"] = poly.reshape(192, 72).astype(np.float32)
    cells = np.arange(16)
    near = h[cells % 8]
    far = ((cells + 0.5) / 8 - 1.0) / 2
    left = np.zeros((2, len(PAIRS), 8, 16, 16))
    for q, (px, py) in enumerate(PAIRS):
        for c in range(4):
            block = ((cells // 8 == c >> 1)[:, None] & (cells // 8 == (c & 1))[None, :]).astype(float)
            left[0, q, c] = block * near[:, None] ** px * near[None, :] ** py
            left[1, q, c] = block * far[:, None] ** px * far[None, :] ** py
    out["left"] = left.reshape(160, 256).astype(np.float32)
    right = np.zeros((128, 128))
    flag = np.zeros((128, 128))
    for z in range(128):
        s = z // 8
        f = ((z % 16 + 0.5) / 8 - 1.0) / 2
        for pz in range(4):
            right[z, pz * 16 + s] = h[z % 8] ** pz / SUB**3
            right[z, 64 + (s % 2) * 32 + pz * 8 + s // 2] = f**pz / SUB**3
    for s in range(16):
        for pz in range(4):
            flag[s, pz * 16 + s] = 1.0
            flag[s, 64 + (s % 2) * 32 + pz * 8 + s // 2] = 1.0
    out["right"] = right.astype(np.float32)
    out["flag"] = flag.astype(ml_dtypes.bfloat16)
    return out


def split(x):
    high = x.astype(BF16)
    return high, (x - high.astype(F32)).astype(BF16)


def mxu(a, b):
    return jnp.dot(a, b, preferred_element_type=F32)


def exact(a, b):
    return jnp.dot(a, b, precision=HIGHEST, preferred_element_type=F32)


def lane_ids(shape):
    return lax.broadcasted_iota(jnp.int32, shape, len(shape) - 1)


def row_ids(shape):
    return lax.broadcasted_iota(jnp.int32, shape, len(shape) - 2)


def power(s):
    return jnp.exp2(GAMMA * jnp.log2(s))


def root(x):
    return x * lax.rsqrt(x)


PLACES = ((0, 1), (1, 3), (4, 1), (5, 1), (6, 9))


def load_all(pairs, sems):
    copies = [pltpu.make_async_copy(source, target, sems.at[k]) for k, (source, target) in enumerate(pairs)]
    for copy in copies:
        copy.start()
    return copies


def fields_into(refs, target, source=slice(0, ROWS), rows=None):
    place = slice(0, source.stop - source.start) if rows is None else rows
    return [
        (ref.at[:, source], target.at[start : start + count, place]) for ref, (start, count) in zip(refs, PLACES)
    ]


def prepare_kernel(den, mom, ene, ent, tra, flags, left, right, flag, pay_h, u, xlo, xhi, ylo_h, yhi_h, pay, ylo, yhi, fl, flv, leftv, rightv, flagv, sems):
    small = load_all(zip((flags, left, right, flag), (flv, leftv, rightv, flagv)), sems.at[7:11])
    loads = load_all(fields_into((den, mom, ene, ent, tra), u), sems.at[0:5])
    for copy in loads:
        copy.wait()
    slabs = load_all([(u.at[:, 0:48], xlo), (u.at[:, 208:256], xhi)], sems.at[5:7])
    for f in range(NF):
        for k in range(3):
            for s in range(2):
                ylo[f, k * 16 + s * 8 : k * 16 + s * 8 + 8] = u[f, pl.ds(s * 128 + k, 8, stride=16)]
                yhi[f, k * 16 + s * 8 : k * 16 + s * 8 + 8] = u[f, pl.ds(s * 128 + 13 + k, 8, stride=16)]
    slabs += load_all([(ylo, ylo_h), (yhi, yhi_h)], sems.at[11:13])
    for copy in small:
        copy.wait()
    fl[...] = jnp.zeros((8, 128), F32)
    fl[0:2, 0:16] = flv[0].astype(F32)
    fl[2:4, 0:16] = flv[1].astype(F32)
    tile = mxu(fl[...].astype(BF16), flagv[...])
    rho = u[0]
    sums = exact(leftv[...], exact(rho, rightv[...]))
    inverse = 1.0 / rho
    fast = jnp.maximum(jnp.maximum(jnp.abs(u[1]), jnp.abs(u[2])), jnp.abs(u[3]))
    sound = root(GAMMA * (GAMMA - 1.0) * power(u[5]) * inverse)
    fastest = jnp.max(fast * inverse + sound)
    lane = lane_ids((8, 128))
    row = row_ids((8, 128))
    tiles = [jnp.zeros((8, 128), F32) for _ in range(3)]
    zero, one = {}, {}
    for q, pair in enumerate(PAIRS):
        zero[pair] = sums[q * 8 : q * 8 + 8] * tile
        v = jnp.sum(sums[80 + q * 8 : 88 + q * 8] * tile, axis=0, keepdims=True)
        v = jnp.broadcast_to(v, (8, 128))
        one[pair] = v + pltpu.roll(v, 96, 1)
    for a, e in enumerate(ALPHA):
        c, to = a // 8, (a % 8) * 16
        low = pltpu.roll(zero[e[0], e[1]], (to - e[2] * 16) % 128, 1)
        top = pltpu.roll(one[e[0], e[1]], (to - 64 - e[2] * 8) % 128, 1)
        here = (lane >= to) & (lane < to + 16)
        tiles[c] = jnp.where(here & (row < 4), low, tiles[c])
        tiles[c] = jnp.where(here & (row == 4) & (lane < to + 8), top, tiles[c])
    tiles[2] = jnp.where((row == 4) & (lane >= 64), fastest, tiles[2])
    for c in range(3):
        pay[c * 8 : c * 8 + 8] = tiles[c]
    slabs += load_all([(pay, pay_h.at[y]) for y in range(GY)], sems.at[13 : 13 + GY])
    for copy in slabs:
        copy.wait()


def relay_kernel(pos, column, *rest):
    out_h, out, sems = rest[-3:]
    y = pos[1]
    tiles = [column[pl.ds(c * 8 + 4, 8, stride=24)] for c in range(3)]
    near = []
    for dy in range(3):
        here = jnp.clip(y + dy - 1, 0, GY - 1)
        inside = here == y + dy - 1
        for c in range(3):
            tile = column[pl.ds(pl.multiple_of(here * 24 + c * 8, 8), 8)]
            near.append(jnp.where(inside, tile, 0.0))
    for c in range(3):
        out[c * 8 : c * 8 + 8] = tiles[c]
    for n, tile in enumerate(near):
        out[24 + n * 4 : 28 + n * 4] = tile[0:4]
    out[60:64] = jnp.zeros((4, 128), F32)
    for copy in load_all([(out, out_h.at[x]) for x in range(GX)], sems):
        copy.wait()


def states(ol, il, l, r, ir, orr):
    face = (37.0 / 60.0) * (l + r) - (8.0 / 60.0) * (il + ir) + (1.0 / 60.0) * (ol + orr)
    low, high = jnp.minimum(l, r), jnp.maximum(l, r)
    left = jnp.minimum(jnp.maximum(face, jnp.minimum(il, low)), jnp.maximum(il, high))
    right = jnp.minimum(jnp.maximum(face, jnp.minimum(low, ir)), jnp.maximum(high, ir))
    return left, right


def fluxes(load, d, store):
    rl, rr = load(0)
    ml, mr = load(1 + d)
    sl, sr = load(5)
    il, ir = 1.0 / rl, 1.0 / rr
    vl, vr = ml * il, mr * ir
    gl, gr = power(sl), power(sr)
    cl, cr = root(GAMMA * (GAMMA - 1.0) * gl * il), root(GAMMA * (GAMMA - 1.0) * gr * ir)
    a = 4.0 * jnp.maximum(jnp.abs(vl) + cl, jnp.abs(vr) + cr)
    wl, wr = 4.0 * vl, 4.0 * vr
    kl, kr = wl + a, wr - a
    got = {0: (rl, rr), 1 + d: (ml, mr), 5: (sl, sr)}
    for f in range(NF):
        left, right = got[f] if f in got else load(f)
        flux = left * kl + right * kr
        if f == 1 + d:
            flux = flux + (4.0 * (GAMMA - 1.0)) * (gl + gr)
        if f == 4:
            flux = flux + (GAMMA - 1.0) * (gl * wl + gr * wr)
        store(f, flux)


def flux_z_kernel(u, out_h, uz, fz, out, sems):
    for f in range(NF):
        for half in range(2):
            cells = u[f, half * 128 : half * 128 + 128].T
            uz[2 * f + half, 8:136] = cells
            uz[2 * f + half, 0:8] = jnp.broadcast_to(cells[0:1], (8, 128))
            uz[2 * f + half, 136:144] = jnp.broadcast_to(cells[127:128], (8, 128))

    def faces_z(i, carry):
        for half in range(2):

            def load(f):
                return states(*[uz[2 * f + half, pl.ds(i * 8 + 5 + k, 8)] for k in range(6)])

            def store(f, flux):
                fz[2 * f + half, pl.ds(pl.multiple_of(i * 8, 8), 8)] = flux

            fluxes(load, 2, store)
        return carry

    lax.fori_loop(0, 16, faces_z, 0)
    for half in range(2):

        def load_top(f, half=half):
            rows = [uz[2 * f + half, 133 + k : 141 + k] for k in range(4)]
            return states(*rows, rows[3], rows[3])

        def store_top(f, flux, half=half):
            fz[2 * f + half, 128:136] = flux

        fluxes(load_top, 2, store_top)

    stores = []
    for part in range(5):
        for f in range(part * 3, part * 3 + 3):
            for half in range(2):
                out[f, half * 128 : half * 128 + 128] = (fz[2 * f + half, 0:128] - fz[2 * f + half, 1:129]).T
        some = slice(part * 3, part * 3 + 3)
        stores += load_all([(out.at[some], out_h.at[some])], sems.at[part : part + 1])
    for copy in stores:
        copy.wait()


def flux_xy_kernel(pos, den, mom, ene, ent, tra, along_z_h, xl, xr, yl_h, yr_h, *args):
    count = len(TREE_CONSTANTS)
    out_h = args[count]
    tables = args[count + 1 : 2 * count + 1]
    ux, fx, uy, fy, yl, yr, along_z, out, sems = args[2 * count + 1 :]
    loads = load_all(
        fields_into((den, mom, ene, ent, tra), ux, rows=slice(48, 304))
        + [(xl, ux.at[:, 0:48]), (xr, ux.at[:, 304:352]), (yl_h, yl), (yr_h, yr), (along_z_h, along_z)],
        sems.at[0:10],
    )
    late = load_all(list(zip(args[:count], tables)), sems.at[10 : 10 + count])
    for copy in loads[:7]:
        copy.wait()

    def repeat(source, target):
        for f in range(NF):
            cells = ux[f, source : source + 16]
            for k in range(3):
                ux[f, target + k * 16 : target + k * 16 + 16] = cells

    pl.when(pos[0] == 0)(lambda: repeat(48, 0))
    pl.when(pos[0] == GX - 1)(lambda: repeat(288, 304))

    def faces_x(i, carry):
        for s in range(2):

            def load(f):
                return states(*[ux[f, pl.ds(pl.multiple_of((i + k) * 16 + s * 8, 8), 8)] for k in range(6)])

            def store(f, flux):
                fx[f, pl.ds(pl.multiple_of(i * 16 + s * 8, 8), 8)] = flux

            fluxes(load, 0, store)
        return carry

    lax.fori_loop(0, 17, faces_x, 0)

    def spread(x, carry):
        for f in range(NF):
            uy[f, pl.ds(pl.multiple_of(x * 32 + 8, 8), 16)] = ux[f, pl.ds(pl.multiple_of(48 + x * 16, 8), 16)]
        return carry

    lax.fori_loop(0, 16, spread, 0)
    for copy in loads[7:9]:
        copy.wait()
    first, last = pos[1] == 0, pos[1] == GY - 1
    for f in range(NF):
        for s in range(2):
            low, high = ux[f, pl.ds(48 + s * 128, 8, stride=16)], ux[f, pl.ds(63 + s * 128, 8, stride=16)]
            for k in range(3):
                at = slice(k * 16 + s * 8, k * 16 + s * 8 + 8)
                uy[f, pl.ds(s * 256 + 5 + k, 8, stride=32)] = jnp.where(first, low, yl[f, at])
                uy[f, pl.ds(s * 256 + 24 + k, 8, stride=32)] = jnp.where(last, high, yr[f, at])

    def faces_y(x, carry):
        for s in range(2):

            def load(f):
                return states(*[uy[f, pl.ds(x * 32 + s * 8 + 5 + k, 8)] for k in range(6)])

            def store(f, flux):
                fy[f, pl.ds(pl.multiple_of(x * 24 + s * 8, 8), 8)] = flux

            fluxes(load, 1, store)
        return carry

    lax.fori_loop(0, 16, faces_y, 0)
    for s in range(2):

        def load_end(f, s=s):
            return states(*[uy[f, pl.ds(s * 256 + 21 + k, 8, stride=32)] for k in range(6)])

        def store_end(f, flux, s=s):
            fy[f, pl.ds(s * 192 + 16, 8, stride=24)] = flux

        fluxes(load_end, 1, store_end)
    loads[9].wait()

    def gather(x, carry):
        for f in range(NF):
            for s in range(2):
                at = pl.multiple_of(x * 16 + s * 8, 8)
                rows = pl.ds(at, 8)
                change = along_z[f, rows] + (fx[f, rows] - fx[f, pl.ds(at + 16, 8)])
                y = x * 24 + s * 8
                out[f, rows] = change + (fy[f, pl.ds(pl.multiple_of(y, 8), 8)] - fy[f, pl.ds(y + 1, 8)])
        return carry

    for part in range(4):
        lax.fori_loop(part * 4, part * 4 + 4, gather, 0)
        rows = slice(part * 64, part * 64 + 64)
        late += load_all([(out.at[:, rows], out_h.at[:, rows])], sems.at[10 + count + part : 11 + count + part])
    for copy in late:
        copy.wait()


TREE_CONSTANTS = (
    "w_high", "w_low", "sel_zero", "lane_odd", "up", "alpha_odd", "agg", "mask", "info", "expand", "gamma_odd", "down",
    "spread", "poly",
)


def tree_kernel(pos, far, den, mom, ene, ent, tra, change_h, *args):
    count = len(TREE_CONSTANTS)
    w_high, w_low, sel_zero, lane_odd, up, alpha_odd, agg, mask, info, expand, gamma_odd, down, spread, poly = args[:count]
    section, accel, rhs, field, result, force, u, change, sems = args[count:]
    late = load_all(fields_into((den, mom, ene, ent, tra), u) + [(change_h, change)], sems.at[0:6])
    px, py = pos[0], pos[1]
    blocks = []
    for dx in range(3):
        here = jnp.clip(px + dx - 1, 0, GX - 1)
        inside = here == px + dx - 1
        blocks.append([jnp.where(inside, far[here, 24 + n * 4 : 28 + n * 4], 0.0) for n in range(9)])
    gap = jnp.zeros((4, 128), F32)
    around = jnp.concatenate(
        [jnp.concatenate([blocks[dx][dy * 3 + c] for dx in range(3) for dy in range(3)] + [gap], 0) for c in range(3)], 1
    )
    zero = mxu(sel_zero[...], jnp.concatenate(split(around), 1))
    zero = zero[:, :384] + zero[:, 384:]
    arrays = [zero[c * WIN : c * WIN + WIN] * lane_odd[c : c + 1] for c in range(4)]
    gathered = jnp.concatenate([far[:, c * 8 : c * 8 + 8].reshape(128, 128) for c in range(3)], 1)
    speeds = gathered[:, 256:]
    fastest = jnp.max(jnp.where(lane_ids((128, 128)) >= 64, speeds, 0.0))

    def lifted(x, x_odd, y_odd):
        sign = (1.0 - 2.0 * x_odd * alpha_odd[0:1]) * (1.0 - 2.0 * y_odd * alpha_odd[1:2])
        n = x.shape[0]
        z = mxu(jnp.concatenate(split(x * sign), 0), up[...])
        return (z[:n] + z[n:]) * sign

    def picked(matrix, x):
        y = mxu(matrix, jnp.concatenate(split(x), 1))
        return y[:, :384] + y[:, 384:]

    dev = lax.broadcasted_iota(jnp.int32, (128, 1), 0)
    raised = lifted(gathered, ((dev // 8) % 2).astype(F32), (dev % 2).astype(F32))
    two = picked(agg[...], raised)
    cell = lax.broadcasted_iota(jnp.int32, (32, 1), 0)
    raised_two = lifted(two, ((cell // 4) % 2).astype(F32), (cell % 2).astype(F32))

    def window(level, columns, count_y, shift):
        tx, ty = px >> (level - 1), py >> (level - 1)
        row = lax.broadcasted_iota(jnp.int32, (WIN, columns), 0)
        col = lax.broadcasted_iota(jnp.int32, (WIN, columns), 1)
        i, j = row // 6, row % 6
        i = jnp.where((tx & 1) == 1, 5 - i, i) + 2 * ((tx >> 1) - 1)
        j = jnp.where((ty & 1) == 1, 5 - j, j) + 2 * ((ty >> 1) - 1)
        sx, sy = (col // count_y) >> shift, (col % count_y) >> shift
        return ((row < 36) & (sx == i) & (sy == j)).astype(F32).astype(BF16)

    levels = (
        picked(window(1, 128, 8, 0), gathered)
        + picked(window(2, 128, 8, 1), raised)
        + picked(window(3, 32, 4, 1), raised_two)
    )
    sign = jnp.ones((1, 384), F32)
    for level in (1, 2, 3):
        bx = ((px >> (level - 1)) & 1).astype(F32)
        by = ((py >> (level - 1)) & 1).astype(F32)
        sign = sign * (1.0 - 2.0 * bx * lane_odd[4 + level : 5 + level])
        sign = sign * (1.0 - 2.0 * by * lane_odd[8 + level : 9 + level])
    levels = levels * sign
    wrow = lax.broadcasted_iota(jnp.int32, (WIN, 384), 0)
    wi, wj = wrow // 6, wrow % 6
    touching = (wi >= 1) & (wi <= 3) & (wj >= 1) & (wj <= 3)
    arrays += [levels, jnp.where(touching, 0.0, levels)]
    lane = lane_ids((WIN, 128)) // 16
    for a in range(NA):
        c, off = a // 8, (a % 8) * 16
        block = jnp.zeros((WIN, 128), F32)
        for g, array in enumerate(arrays):
            block = jnp.where(lane == g, pltpu.roll(array[:, c * 128 : c * 128 + 128], (16 * g - off) % 128, 1), block)
        rhs[a * WIN : a * WIN + WIN] = block
    high, low = split(rhs[...])
    y = mxu(w_high[...], jnp.concatenate([high, low], 1))
    y = y[:, :128] + y[:, 128:] + mxu(w_low[...], high)
    base = jnp.zeros((NG, 128), F32)
    for k in range(7):
        base = base + mask[k : k + 1] * pltpu.roll(y[k * NG : k * NG + NG], (3 - k) % 128, 1)
    lanes = lane_ids((NG, 128)) // 16
    base = base + jnp.where(lanes == 4, pltpu.roll(base, 112, 1), 0.0)
    bx, by = info[1:2], info[2:3]
    for level in (1, 2, 3):
        bx = bx + info[2 + 2 * level : 3 + 2 * level] * ((px >> (level - 1)) & 1).astype(F32)
        by = by + info[2 + 2 * level : 3 + 2 * level] * ((py >> (level - 1)) & 1).astype(F32)
    flip = (1.0 - 2.0 * bx * gamma_odd[0:NG]) * (1.0 - 2.0 * by * gamma_odd[NG : 2 * NG])
    base = base * info[0:1] * flip
    flip = flip * (1.0 - 2.0 * info[9:10] * gamma_odd[2 * NG :])
    total = base
    for _ in range(3):
        total = base + flip * exact(down[...], flip * exact(total, expand[...]))
    rows = jnp.concatenate([pltpu.roll(total, (128 - 16 * c) % 128, 1) for c in range(4)], 0)[:, :16]
    spreads = exact(rows, spread[...])
    terms = jnp.concatenate(
        [
            jnp.concatenate([spreads[c * NG : c * NG + NG, k * 128 : k * 128 + 128] for k in range(3)], 0)
            for c in range(4)
        ],
        1,
    )
    field[...] = exact(poly[...], terms)
    step = jnp.full((8, 128), COURANT / SUB, F32) / fastest
    for copy in late:
        copy.wait()
    stores = []
    for half in range(2):

        def finish(x, carry, half=half):
            for s in range(2):
                c = half * 2 + s
                at = pl.multiple_of(half * 128 + x * 16 + s * 8, 8)
                rows = pl.ds(at, 8)
                acc = [field[pl.ds(pl.multiple_of(i * 64 + x * 8, 8), 8), c * 128 : c * 128 + 128] for i in range(3)]
                old = [u[f, rows] for f in range(NF)]
                for i in range(3):
                    force[i, rows] = acc[i]
                for f in range(NF):
                    slope = change[f, rows]
                    if 1 <= f <= 3:
                        slope = slope + old[0] * acc[f - 1]
                    if f == 4:
                        slope = slope + (old[1] * acc[0] + old[2] * acc[1] + old[3] * acc[2])
                    result[f, rows] = old[f] + step * slope
            return carry

        lax.fori_loop(0, 8, finish, 0)
        rows = slice(half * 128, half * 128 + 128)
        for k, (source, target) in enumerate(((result, section), (force, accel))):
            stores.append(pltpu.make_async_copy(source.at[:, rows], target.at[:, rows], sems.at[6 + 2 * half + k]))
            stores[-1].start()
    for copy in stores:
        copy.wait()


ANY = pl.BlockSpec(memory_space=pl.ANY)
HBM = pl.BlockSpec(memory_space=pltpu.HBM)
VMEM = pl.BlockSpec(memory_space=pltpu.VMEM)
SMEM = pl.BlockSpec(memory_space=pltpu.SMEM)


def call(kernel, name, ins, outs, scratch, cost, aliases=None):
    outs = [(o[0], o[1], o[2] if len(o) > 2 else F32) for o in outs]
    return pl.pallas_call(
        kernel,
        out_shape=[pltpu.HBM(s, t) if spec is HBM else jax.ShapeDtypeStruct(s, t) for s, spec, t in outs],
        in_specs=[spec for _, spec in ins],
        out_specs=[spec for _, spec, _ in outs],
        scratch_shapes=scratch,
        input_output_aliases=aliases or {},
        cost_estimate=pl.CostEstimate(flops=cost[0], bytes_accessed=cost[1], transcendentals=cost[2]),
        name=name,
        compiler_params=pltpu.CompilerParams(vmem_limit_bytes=32 << 20),
    )(*[in_hbm(x) if spec is HBM else x for x, spec in ins])


def in_hbm(x):
    return pltpu.with_memory_space_constraint(x, pltpu.HBM)


def scratch_like(x):
    return pltpu.VMEM(x.shape, x.dtype)


def shards(density, momentum, energy, entropy, tracers, leaf_flags):
    con = {k: jnp.asarray(v) for k, v in constants().items()}
    fields = [(x.reshape(-1, ROWS, 128), HBM) for x in (density, momentum, energy, entropy, tracers)]
    ix, iy = lax.axis_index("mx"), lax.axis_index("my")
    pos = (jnp.stack([ix, iy]).astype(jnp.int32), SMEM)
    first = [con[n] for n in ("left", "right", "flag")]
    whole, slab = (NF, ROWS, 128), (NF, 48, 128)
    block, halo = pltpu.VMEM(whole, F32), pltpu.VMEM(slab, F32)
    pay, u, xlo, xhi, ylo, yhi = call(
        prepare_kernel,
        "prepare",
        fields + [(leaf_flags, HBM)] + [(x, HBM) for x in first],
        [((GY, 24, 128), HBM), (whole, VMEM)] + [(slab, HBM)] * 4,
        [pltpu.VMEM((24, 128), F32), halo, halo, pltpu.VMEM((8, 128), F32), scratch_like(leaf_flags)]
        + [scratch_like(x) for x in first]
        + [pltpu.SemaphoreType.DMA((13 + GY,))],
        (10**7, 4 * 10**6, 10**5),
    )
    up_x, down_x = [(i, i + 1) for i in range(GX - 1)], [(i + 1, i) for i in range(GX - 1)]
    up_y, down_y = [(i, i + 1) for i in range(GY - 1)], [(i + 1, i) for i in range(GY - 1)]
    column = lax.all_to_all(pay, "my", 0, 0)
    yl = lax.ppermute(yhi, "my", up_y)
    yr = lax.ppermute(ylo, "my", down_y)
    xl = lax.ppermute(xhi, "mx", up_x)
    xr = lax.ppermute(xlo, "mx", down_x)
    (along_z,) = call(
        flux_z_kernel,
        "flux_z",
        [(u, VMEM)],
        [(whole, HBM)],
        [pltpu.VMEM((2 * NF, 144, 128), F32), pltpu.VMEM((2 * NF, 136, 128), F32), block, pltpu.SemaphoreType.DMA((5,))],
        (2 * 10**7, 4 * 10**6, 3 * 10**5),
    )
    halos = [(x, ANY) for x in (xl, xr, yl, yr)]
    (chunks,) = call(
        relay_kernel,
        "relay",
        [pos, (column.reshape(GY * 24, 128), VMEM), (along_z, HBM)] + halos,
        [((GX, 64, 128), HBM)],
        [pltpu.VMEM((64, 128), F32), pltpu.SemaphoreType.DMA((GX,))],
        (10**4, 10**6, 0),
    )
    far = lax.all_to_all(chunks, "mx", 0, 0)
    second = [con[n] for n in TREE_CONSTANTS]
    tend, *tables = call(
        flux_xy_kernel,
        "flux_xy",
        [pos] + fields + [(along_z, HBM)] + halos + [(x, HBM) for x in second],
        [(whole, HBM)] + [(x.shape, VMEM, x.dtype) for x in second],
        [
            pltpu.VMEM((NF, 352, 128), F32),
            pltpu.VMEM((NF, 272, 128), F32),
            pltpu.VMEM((NF, 512, 128), F32),
            pltpu.VMEM((NF, 384, 128), F32),
            halo,
            halo,
            block,
            block,
            pltpu.SemaphoreType.DMA((14 + len(second),)),
        ],
        (4 * 10**7, 6 * 10**6, 6 * 10**5),
    )
    section, accel = call(
        tree_kernel,
        "tree",
        [pos, (far, VMEM)] + fields + [(tend, HBM)] + [(x, VMEM) for x in tables],
        [(whole, HBM), ((3, ROWS, 128), HBM)],
        [
            pltpu.VMEM((NA * WIN, 128), F32),
            pltpu.VMEM((192, 512), F32),
            block,
            pltpu.VMEM((3, ROWS, 128), F32),
            block,
            block,
            pltpu.SemaphoreType.DMA((10,)),
        ],
        (10**8, 8 * 10**6, 0),
    )
    return section.reshape(NF, 16, 16, 128), accel.reshape(3, 16, 16, 128)


def solution(mesh):
    placed = (
        P("mx", "my", None),
        P(None, "mx", "my", None),
        P("mx", "my", None),
        P("mx", "my", None),
        P(None, "mx", "my", None),
        P("mx", "my", None),
    )
    return jax.shard_map(
        shards,
        mesh=mesh,
        in_specs=placed,
        out_specs=(P(None, "mx", "my", None), P(None, "mx", "my", None)),
        check_vma=False,
    )
```

```python
import functools
import math

import jax
import jax.numpy as jnp
import ml_dtypes
import numpy as np
from jax import lax
from jax.experimental import pallas as pl
from jax.experimental.pallas import tpu as pltpu
from jax.sharding import PartitionSpec as P

F32 = jnp.float32
BF16 = jnp.bfloat16
HIGHEST = lax.Precision.HIGHEST
GRAVITY = 0.02
GAMMA = 5.0 / 3.0
COURANT = 0.3
SUB = 8
NF = 15
GX, GY = 16, 8
ROWS = 256

ALPHA = [
    (px, py, d - px - py)
    for d in range(4)
    for px in range(d, -1, -1)
    for py in range(d - px, -1, -1)
]
NA = len(ALPHA)
NG = 24
WIN = 40
PAIRS = [(px, py) for px in range(4) for py in range(4 - px)]


def factorial_of(e):
    return math.factorial(e[0]) * math.factorial(e[1]) * math.factorial(e[2])


def inverse_derivative(exponent, r):
    axes = [0] * exponent[0] + [1] * exponent[1] + [2] * exponent[2]
    norm = math.sqrt(r[0] ** 2 + r[1] ** 2 + r[2] ** 2)
    if norm == 0.0:
        return 0.0
    if not axes:
        return 1.0 / norm
    if len(axes) == 1:
        return -r[axes[0]] / norm**3
    if len(axes) == 2:
        a, b = axes
        return 3.0 * r[a] * r[b] / norm**5 - float(a == b) / norm**3
    a, b, c = axes
    crossed = float(a == b) * r[c] + float(a == c) * r[b] + float(b == c) * r[a]
    return -15.0 * r[a] * r[b] * r[c] / norm**7 + 3.0 * crossed / norm**5


def split_np(x):
    high = x.astype(np.float32).astype(ml_dtypes.bfloat16)
    low = (x - high.astype(np.float64)).astype(ml_dtypes.bfloat16)
    return high, low


def exact_np(x):
    y = x.astype(ml_dtypes.bfloat16)
    assert np.array_equal(x, y.astype(np.float64))
    return y


@functools.cache
def constants():
    out = {}
    w = np.zeros((7, NG, NA, WIN))
    for z in range(7):
        for i in range(6):
            for j in range(6):
                r = (-(i - 2.0), -(j - 2.0), -(z - 3.0))
                for g, eg in enumerate(ALPHA):
                    for a, ea in enumerate(ALPHA):
                        if sum(eg) + sum(ea) <= 3:
                            e = tuple(eg[k] + ea[k] for k in range(3))
                            w[z, g, a, i * 6 + j] = (
                                -GRAVITY
                                * (-1.0) ** sum(ea)
                                / (factorial_of(ea) * factorial_of(eg))
                                * inverse_derivative(e, r)
                            )
    out["w_high"], out["w_low"] = split_np(w.reshape(7 * NG, NA * WIN))
    sel = np.zeros((4, WIN, 40))
    sign = np.zeros((4, 384))
    for c in range(4):
        cx, cy = c >> 1, c & 1
        for i in range(6):
            for j in range(6):
                si, sj = (5 - i if cx else i), (5 - j if cy else j)
                sel[c, i * 6 + j, ((si // 2) * 3 + sj // 2) * 4 + (si % 2) * 2 + sj % 2] = 1.0
        for a, e in enumerate(ALPHA):
            sign[c, a * 16 : a * 16 + 16] = (-1.0) ** (cx * e[0] + cy * e[1])
    out["sel_zero"] = sel.reshape(4 * WIN, 40).astype(ml_dtypes.bfloat16)
    lanes = np.zeros((16, 384), np.float32)
    lanes[0:4] = sign
    for a, e in enumerate(ALPHA):
        for r in range(16):
            lane = a * 16 + r
            level = 1 if r < 8 else 2 if r < 12 else 3
            lanes[4 + level, lane] = e[0] % 2
            lanes[8 + level, lane] = e[1] % 2
    out["lane_odd"] = lanes
    up = np.zeros((384, 384))
    for t, et in enumerate(ALPHA):
        for s, es in enumerate(ALPHA):
            if all(es[k] <= et[k] for k in range(3)):
                for base, to, count in ((0, 8, 8), (8, 12, 4)):
                    for z in range(count):
                        v = 2.0 ** -sum(et)
                        for k in range(3):
                            d = -0.5 if k < 2 or z % 2 == 0 else 0.5
                            v *= math.comb(et[k], es[k]) * d ** (et[k] - es[k])
                        up[s * 16 + base + z, t * 16 + to + z // 2] = v
    out["up"] = exact_np(up)
    odd = np.zeros((16, 384), np.float32)
    for a, e in enumerate(ALPHA):
        odd[0, a * 16 : a * 16 + 16] = e[0] % 2
        odd[1, a * 16 : a * 16 + 16] = e[1] % 2
    out["alpha_odd"] = odd
    agg = np.zeros((32, 128))
    for x in range(GX):
        for y in range(GY):
            agg[(x // 2) * 4 + y // 2, (y % 2) * 64 + x * 4 + y // 2] = 1.0
    out["agg"] = agg.astype(ml_dtypes.bfloat16)
    mask = np.zeros((8, 128), np.float32)
    info = np.zeros((16, 128), np.float32)
    expand = np.zeros((128, 128), np.float32)
    for lane in range(96):
        g, r = lane // 16, lane % 16
        if g < 4:
            n, z, level = 16, r, 0
        elif r < 8:
            n, z, level = 8, r, 1
        elif r < 12:
            n, z, level = 4, r - 8, 2
        elif r < 14:
            n, z, level = 2, r - 12, 3
        else:
            continue
        for k in range(7):
            o = k - 3
            ok = 0 <= z + o < n and abs((z + o) // 2 - z // 2) <= 1
            if g == 4:
                ok = ok and abs(o) > 1
            if g == 5:
                ok = ok and abs(o) <= 1
            mask[k, lane] = float(ok)
        if g < 5:
            info[0, lane] = 2.0**-level
            info[1, lane] = float(g >> 1) if level == 0 else 0.0
            info[2, lane] = float(g & 1) if level == 0 else 0.0
            info[2 + 2 * level, lane] = 1.0 if level else info[2, lane]
            info[9, lane] = float(z % 2)
            if level == 0:
                expand[64 + z // 2, lane] = 1.0
            elif level == 1:
                expand[64 + 8 + z // 2, lane] = 1.0
            elif level == 2:
                expand[64 + 12 + z // 2, lane] = 1.0
    out["mask"] = mask
    out["info"] = info
    out["expand"] = exact_np(expand)
    gamma_odd = np.zeros((3 * NG, 128), np.float32)
    down = np.zeros((NG, NG))
    for g, eg in enumerate(ALPHA):
        for k in range(3):
            gamma_odd[k * NG + g] = eg[k] % 2
        for b, eb in enumerate(ALPHA):
            if all(eb[k] >= eg[k] for k in range(3)):
                v = 2.0 ** -sum(eg)
                for k in range(3):
                    n = eb[k] - eg[k]
                    v *= (-0.25) ** n * math.comb(eb[k], eg[k])
                down[g, b] = v
    out["gamma_odd"] = gamma_odd
    out["down"] = exact_np(down)
    h = (np.arange(SUB) + 0.5) / SUB - 0.5
    spread = np.zeros((16, 384))
    for k in range(3):
        for z in range(128):
            spread[z // 8, k * 128 + z] = h[z % 8] ** k
    out["spread"] = exact_np(spread)
    poly = np.zeros((3, 8, 8, 3, NG))
    for i in range(3):
        for g, e in enumerate(ALPHA):
            if e[i] > 0:
                low = list(e)
                low[i] -= 1
                poly[i, :, :, low[2], g] = (
                    -e[i] * h[:, None] ** low[0] * h[None, :] ** low[1]
                )
    out["poly"] = exact_np(poly.reshape(192, 72))
    cells = np.arange(16)
    near = h[cells % 8]
    far = ((cells + 0.5) / 8 - 1.0) / 2
    left = np.zeros((2, len(PAIRS), 8, 16, 16))
    for q, (px, py) in enumerate(PAIRS):
        for c in range(4):
            block = ((cells // 8 == c >> 1)[:, None] & (cells // 8 == (c & 1))[None, :]).astype(float)
            left[0, q, c] = block * near[:, None] ** px * near[None, :] ** py
            left[1, q, c] = block * far[:, None] ** px * far[None, :] ** py
    out["left"] = left.reshape(160, 256).astype(np.float32)
    right = np.zeros((128, 128))
    flag = np.zeros((128, 128))
    for z in range(128):
        s = z // 8
        f = ((z % 16 + 0.5) / 8 - 1.0) / 2
        for pz in range(4):
            right[z, pz * 16 + s] = h[z % 8] ** pz / SUB**3
            right[z, 64 + (s % 2) * 32 + pz * 8 + s // 2] = f**pz / SUB**3
    for s in range(16):
        for pz in range(4):
            flag[s, pz * 16 + s] = 1.0
            flag[s, 64 + (s % 2) * 32 + pz * 8 + s // 2] = 1.0
    out["right"] = right.astype(np.float32)
    out["flag"] = flag.astype(ml_dtypes.bfloat16)
    return out


def split(x):
    high = x.astype(BF16)
    return high, (x - high.astype(F32)).astype(BF16)


def split_rows(x):
    high = x.astype(BF16).astype(F32)
    return jnp.concatenate([high, x - high], 0).astype(BF16)


def mxu(a, b):
    return jnp.dot(a, b, preferred_element_type=F32)


def exact(a, b):
    return jnp.dot(a, b, precision=HIGHEST, preferred_element_type=F32)


def lane_ids(shape):
    return lax.broadcasted_iota(jnp.int32, shape, len(shape) - 1)


def row_ids(shape):
    return lax.broadcasted_iota(jnp.int32, shape, len(shape) - 2)


def power(s):
    return jnp.exp2(GAMMA * jnp.log2(s))


def root(x):
    return x * lax.rsqrt(x)


PLACES = ((0, 1), (1, 3), (4, 1), (5, 1), (6, 9))


def load_all(pairs, sems):
    copies = [pltpu.make_async_copy(source, target, sems.at[k]) for k, (source, target) in enumerate(pairs)]
    for copy in copies:
        copy.start()
    return copies


def fields_into(refs, target, source=slice(0, ROWS), rows=None):
    place = slice(0, source.stop - source.start) if rows is None else rows
    return [
        (ref.at[:, source], target.at[start : start + count, place]) for ref, (start, count) in zip(refs, PLACES)
    ]


def prepare_kernel(den, mom, ene, ent, tra, flags, left, right, flag, pay_h, u, xlo, xhi, ylo_h, yhi_h, pay, ylo, yhi, fl, flv, leftv, rightv, flagv, sems):
    small = load_all(zip((flags, left, right, flag), (flv, leftv, rightv, flagv)), sems.at[7:11])
    loads = load_all(fields_into((den, mom, ene, ent, tra), u), sems.at[0:5])
    for copy in loads:
        copy.wait()
    slabs = load_all([(u.at[:, 0:48], xlo), (u.at[:, 208:256], xhi)], sems.at[5:7])
    for f in range(NF):
        for k in range(3):
            for s in range(2):
                ylo[f, k * 16 + s * 8 : k * 16 + s * 8 + 8] = u[f, pl.ds(s * 128 + k, 8, stride=16)]
                yhi[f, k * 16 + s * 8 : k * 16 + s * 8 + 8] = u[f, pl.ds(s * 128 + 13 + k, 8, stride=16)]
    slabs += load_all([(ylo, ylo_h), (yhi, yhi_h)], sems.at[11:13])
    for copy in small:
        copy.wait()
    fl[...] = jnp.zeros((8, 128), F32)
    fl[0:2, 0:16] = flv[0].astype(F32)
    fl[2:4, 0:16] = flv[1].astype(F32)
    tile = mxu(fl[...].astype(BF16), flagv[...])
    rho = u[0]
    sums = exact(leftv[...], exact(rho, rightv[...]))
    inverse = 1.0 / rho
    fast = jnp.maximum(jnp.maximum(jnp.abs(u[1]), jnp.abs(u[2])), jnp.abs(u[3]))
    sound = root(GAMMA * (GAMMA - 1.0) * power(u[5]) * inverse)
    fastest = jnp.max(fast * inverse + sound)
    lane = lane_ids((8, 128))
    row = row_ids((8, 128))
    tiles = [jnp.zeros((8, 128), F32) for _ in range(3)]
    zero, one = {}, {}
    for q, pair in enumerate(PAIRS):
        zero[pair] = sums[q * 8 : q * 8 + 8] * tile
        v = jnp.sum(sums[80 + q * 8 : 88 + q * 8] * tile, axis=0, keepdims=True)
        v = jnp.broadcast_to(v, (8, 128))
        one[pair] = v + pltpu.roll(v, 96, 1)
    for a, e in enumerate(ALPHA):
        c, to = a // 8, (a % 8) * 16
        low = pltpu.roll(zero[e[0], e[1]], (to - e[2] * 16) % 128, 1)
        top = pltpu.roll(one[e[0], e[1]], (to - 64 - e[2] * 8) % 128, 1)
        here = (lane >= to) & (lane < to + 16)
        tiles[c] = jnp.where(here & (row < 4), low, tiles[c])
        tiles[c] = jnp.where(here & (row == 4) & (lane < to + 8), top, tiles[c])
    tiles[2] = jnp.where((row == 4) & (lane >= 64) & (lane < 72), fastest, tiles[2])
    for c in range(3):
        pay[c * 8 : c * 8 + 8] = tiles[c]
    slabs += load_all([(pay, pay_h.at[y]) for y in range(GY)], sems.at[13 : 13 + GY])
    for copy in slabs:
        copy.wait()


def relay_kernel(pos, column, *rest):
    out_h, out, sems = rest[-3:]
    y = pos[1]
    even = [column[pl.ds(c * 8 + 4, 4, stride=48)] for c in range(3)]
    odd = [column[pl.ds(c * 8 + 28, 4, stride=48)] for c in range(3)]
    near = []
    for dy in range(3):
        here = jnp.clip(y + dy - 1, 0, GY - 1)
        inside = here == y + dy - 1
        for c in range(3):
            tile = column[pl.ds(pl.multiple_of(here * 24 + c * 8, 8), 8)]
            near.append(jnp.where(inside, tile, 0.0))
    for c in range(3):
        out[c * 4 : c * 4 + 4] = even[c] + pltpu.roll(odd[c], 8, 1)
    for n, tile in enumerate(near):
        out[12 + n * 4 : 16 + n * 4] = tile[0:4]
    for copy in load_all([(out, out_h.at[x]) for x in range(GX)], sems):
        copy.wait()


def states(ol, il, l, r, ir, orr):
    face = (37.0 / 60.0) * (l + r) - (8.0 / 60.0) * (il + ir) + (1.0 / 60.0) * (ol + orr)
    low, high = jnp.minimum(l, r), jnp.maximum(l, r)
    left = jnp.minimum(jnp.maximum(face, jnp.minimum(il, low)), jnp.maximum(il, high))
    right = jnp.minimum(jnp.maximum(face, jnp.minimum(low, ir)), jnp.maximum(high, ir))
    return left, right


def fluxes(load, d, store):
    rl, rr = load(0)
    ml, mr = load(1 + d)
    sl, sr = load(5)
    il, ir = 1.0 / rl, 1.0 / rr
    vl, vr = ml * il, mr * ir
    gl, gr = power(sl), power(sr)
    cl, cr = root(GAMMA * (GAMMA - 1.0) * gl * il), root(GAMMA * (GAMMA - 1.0) * gr * ir)
    a = 4.0 * jnp.maximum(jnp.abs(vl) + cl, jnp.abs(vr) + cr)
    wl, wr = 4.0 * vl, 4.0 * vr
    kl, kr = wl + a, wr - a
    got = {0: (rl, rr), 1 + d: (ml, mr), 5: (sl, sr)}
    for f in range(NF):
        left, right = got[f] if f in got else load(f)
        flux = left * kl + right * kr
        if f == 1 + d:
            flux = flux + (4.0 * (GAMMA - 1.0)) * (gl + gr)
        if f == 4:
            flux = flux + (GAMMA - 1.0) * (gl * wl + gr * wr)
        store(f, flux)


def flux_z_kernel(u, out_h, uz, fz, out, sems):
    for f in range(NF):
        for half in range(2):
            cells = u[f, half * 128 : half * 128 + 128].T
            uz[2 * f + half, 8:136] = cells
            uz[2 * f + half, 0:8] = jnp.broadcast_to(cells[0:1], (8, 128))
            uz[2 * f + half, 136:144] = jnp.broadcast_to(cells[127:128], (8, 128))

    def faces_z(i, carry):
        for half in range(2):

            def load(f):
                return states(*[uz[2 * f + half, pl.ds(i * 8 + 5 + k, 8)] for k in range(6)])

            def store(f, flux):
                fz[2 * f + half, pl.ds(pl.multiple_of(i * 8, 8), 8)] = flux

            fluxes(load, 2, store)
        return carry

    lax.fori_loop(0, 16, faces_z, 0)
    for half in range(2):

        def load_top(f, half=half):
            rows = [uz[2 * f + half, 133 + k : 141 + k] for k in range(4)]
            return states(*rows, rows[3], rows[3])

        def store_top(f, flux, half=half):
            fz[2 * f + half, 128:136] = flux

        fluxes(load_top, 2, store_top)

    stores = []
    for part in range(5):
        for f in range(part * 3, part * 3 + 3):
            for half in range(2):
                out[f, half * 128 : half * 128 + 128] = (fz[2 * f + half, 0:128] - fz[2 * f + half, 1:129]).T
        some = slice(part * 3, part * 3 + 3)
        stores += load_all([(out.at[some], out_h.at[some])], sems.at[part : part + 1])
    for copy in stores:
        copy.wait()


def flux_xy_kernel(pos, den, mom, ene, ent, tra, along_z_h, xl, xr, yl_h, yr_h, *args):
    count = len(TREE_CONSTANTS)
    out_h = args[count]
    tables = args[count + 1 : 2 * count + 1]
    ux, fx, uy, fy, yl, yr, along_z, out, sems = args[2 * count + 1 :]
    loads = load_all(
        fields_into((den, mom, ene, ent, tra), ux, rows=slice(48, 304))
        + [(xl, ux.at[:, 0:48]), (xr, ux.at[:, 304:352]), (yl_h, yl), (yr_h, yr), (along_z_h, along_z)],
        sems.at[0:10],
    )
    late = load_all(list(zip(args[:count], tables)), sems.at[10 : 10 + count])
    for copy in loads[:7]:
        copy.wait()

    def repeat(source, target):
        for f in range(NF):
            cells = ux[f, source : source + 16]
            for k in range(3):
                ux[f, target + k * 16 : target + k * 16 + 16] = cells

    pl.when(pos[0] == 0)(lambda: repeat(48, 0))
    pl.when(pos[0] == GX - 1)(lambda: repeat(288, 304))

    def faces_x(i, carry):
        for s in range(2):

            def load(f):
                return states(*[ux[f, pl.ds(pl.multiple_of((i + k) * 16 + s * 8, 8), 8)] for k in range(6)])

            def store(f, flux):
                fx[f, pl.ds(pl.multiple_of(i * 16 + s * 8, 8), 8)] = flux

            fluxes(load, 0, store)
        return carry

    lax.fori_loop(0, 17, faces_x, 0)

    def spread(x, carry):
        for f in range(NF):
            uy[f, pl.ds(pl.multiple_of(x * 32 + 8, 8), 16)] = ux[f, pl.ds(pl.multiple_of(48 + x * 16, 8), 16)]
        return carry

    lax.fori_loop(0, 16, spread, 0)
    for copy in loads[7:9]:
        copy.wait()
    first, last = pos[1] == 0, pos[1] == GY - 1
    for f in range(NF):
        for s in range(2):
            low, high = ux[f, pl.ds(48 + s * 128, 8, stride=16)], ux[f, pl.ds(63 + s * 128, 8, stride=16)]
            for k in range(3):
                at = slice(k * 16 + s * 8, k * 16 + s * 8 + 8)
                uy[f, pl.ds(s * 256 + 5 + k, 8, stride=32)] = jnp.where(first, low, yl[f, at])
                uy[f, pl.ds(s * 256 + 24 + k, 8, stride=32)] = jnp.where(last, high, yr[f, at])

    for s in range(2):

        def load_end(f, s=s):
            return states(*[uy[f, pl.ds(s * 256 + 21 + k, 8, stride=32)] for k in range(6)])

        def store_end(f, flux, s=s):
            fy[f, pl.ds(s * 192 + 16, 8, stride=24)] = flux

        fluxes(load_end, 1, store_end)
    def faces_y(x):
        for s in range(2):

            def load(f):
                return states(*[uy[f, pl.ds(x * 32 + s * 8 + 5 + k, 8)] for k in range(6)])

            def store(f, flux):
                fy[f, pl.ds(pl.multiple_of(x * 24 + s * 8, 8), 8)] = flux

            fluxes(load, 1, store)

    loads[9].wait()

    def gather(x):
        for f in range(NF):
            for s in range(2):
                at = pl.multiple_of(x * 16 + s * 8, 8)
                rows = pl.ds(at, 8)
                change = along_z[f, rows] + (fx[f, rows] - fx[f, pl.ds(pl.multiple_of(at + 16, 8), 8)])
                y = pl.multiple_of(x * 24 + s * 8, 8)
                out[f, rows] = change + (fy[f, pl.ds(y, 8)] - fy[f, pl.ds(y + 1, 8)])

    def both(x, carry):
        gather(x - 1)
        faces_y(x)
        return carry

    faces_y(0)
    for part in range(4):
        lax.fori_loop(part * 4 + 1, min(part * 4 + 5, 16), both, 0)
        if part == 3:
            gather(15)
        rows = slice(part * 64, part * 64 + 64)
        late += load_all([(out.at[:, rows], out_h.at[:, rows])], sems.at[10 + count + part : 11 + count + part])
    for copy in late:
        copy.wait()


TREE_CONSTANTS = (
    "w_high", "w_low", "sel_zero", "lane_odd", "up", "alpha_odd", "agg", "mask", "info", "expand", "gamma_odd", "down",
    "spread", "poly",
)


def tree_kernel(pos, far, den, mom, ene, ent, tra, change_h, *args):
    count = len(TREE_CONSTANTS)
    w_high, w_low, sel_zero, lane_odd, up, alpha_odd, agg, mask, info, expand, gamma_odd, down, spread, poly = args[:count]
    section, accel, rhs, field, result, force, u, change, sems = args[count:]
    late = load_all(fields_into((den, mom, ene, ent, tra), u) + [(change_h, change)], sems.at[0:6])
    px, py = pos[0], pos[1]
    blocks = []
    for dx in range(3):
        here = jnp.clip(px + dx - 1, 0, GX - 1)
        inside = here == px + dx - 1
        blocks.append([jnp.where(inside, far[here, 12 + n * 4 : 16 + n * 4], 0.0) for n in range(9)])
    gap = jnp.zeros((4, 128), F32)
    around = jnp.concatenate(
        [jnp.concatenate([blocks[dx][dy * 3 + c] for dx in range(3) for dy in range(3)] + [gap], 0) for c in range(3)], 1
    )
    zero = mxu(sel_zero[...], jnp.concatenate(split(around), 1))
    zero = zero[:, :384] + zero[:, 384:]
    arrays = [zero[c * WIN : c * WIN + WIN] * lane_odd[c : c + 1] for c in range(4)]
    packed = [jnp.concatenate([far[x, c * 4 : c * 4 + 4] for x in range(GX)], 0) for c in range(3)]
    lower = lane_ids((128, 128)) % 16 < 8
    gathered = jnp.concatenate(
        [jnp.where(lower, jnp.concatenate([rows, pltpu.roll(rows, 120, 1)], 0), 0.0) for rows in packed], 1
    )
    speeds = gathered[:, 256:]
    fastest = jnp.max(jnp.where(lane_ids((128, 128)) >= 64, speeds, 0.0))

    def lifted(x, x_odd, y_odd):
        sign = (1.0 - 2.0 * x_odd * alpha_odd[0:1]) * (1.0 - 2.0 * y_odd * alpha_odd[1:2])
        n = x.shape[0]
        z = mxu(jnp.concatenate(split(x * sign), 0), up[...])
        return (z[:n] + z[n:]) * sign

    def picked(matrix, x):
        y = mxu(matrix, jnp.concatenate(split(x), 1))
        return y[:, :384] + y[:, 384:]

    dev = lax.broadcasted_iota(jnp.int32, (128, 1), 0)
    raised = lifted(gathered, ((dev // 4) % 2).astype(F32), (dev // 64).astype(F32))
    two = picked(agg[...], raised)
    cell = lax.broadcasted_iota(jnp.int32, (32, 1), 0)
    raised_two = lifted(two, ((cell // 4) % 2).astype(F32), (cell % 2).astype(F32))

    def window(level, columns, shift):
        tx, ty = px >> (level - 1), py >> (level - 1)
        row = lax.broadcasted_iota(jnp.int32, (WIN, columns), 0)
        col = lax.broadcasted_iota(jnp.int32, (WIN, columns), 1)
        i, j = row // 6, row % 6
        i = jnp.where((tx & 1) == 1, 5 - i, i) + 2 * ((tx >> 1) - 1)
        j = jnp.where((ty & 1) == 1, 5 - j, j) + 2 * ((ty >> 1) - 1)
        if columns == 128:
            sx, sy = (col % 64) // 4, 2 * (col % 4) + col // 64
        else:
            sx, sy = col // 4, col % 4
        sx, sy = sx >> shift, sy >> shift
        return ((row < 36) & (sx == i) & (sy == j)).astype(F32).astype(BF16)

    levels = (
        picked(window(1, 128, 0), gathered)
        + picked(window(2, 128, 1), raised)
        + picked(window(3, 32, 1), raised_two)
    )
    sign = jnp.ones((1, 384), F32)
    for level in (1, 2, 3):
        bx = ((px >> (level - 1)) & 1).astype(F32)
        by = ((py >> (level - 1)) & 1).astype(F32)
        sign = sign * (1.0 - 2.0 * bx * lane_odd[4 + level : 5 + level])
        sign = sign * (1.0 - 2.0 * by * lane_odd[8 + level : 9 + level])
    levels = levels * sign
    wrow = lax.broadcasted_iota(jnp.int32, (WIN, 384), 0)
    wi, wj = wrow // 6, wrow % 6
    touching = (wi >= 1) & (wi <= 3) & (wj >= 1) & (wj <= 3)
    arrays += [levels, jnp.where(touching, 0.0, levels)]
    lane = lane_ids((WIN, 128)) // 16
    for a in range(NA):
        c, off = a // 8, (a % 8) * 16
        block = jnp.zeros((WIN, 128), F32)
        for g, array in enumerate(arrays):
            block = jnp.where(lane == g, pltpu.roll(array[:, c * 128 : c * 128 + 128], (16 * g - off) % 128, 1), block)
        rhs[a * WIN : a * WIN + WIN] = block
    high, low = split(rhs[...])
    y = mxu(w_high[...], jnp.concatenate([high, low], 1))
    y = y[:, :128] + y[:, 128:] + mxu(w_low[...], high)
    base = jnp.zeros((NG, 128), F32)
    for k in range(7):
        base = base + mask[k : k + 1] * pltpu.roll(y[k * NG : k * NG + NG], (3 - k) % 128, 1)
    lanes = lane_ids((NG, 128)) // 16
    base = base + jnp.where(lanes == 4, pltpu.roll(base, 112, 1), 0.0)
    bx, by = info[1:2], info[2:3]
    for level in (1, 2, 3):
        bx = bx + info[2 + 2 * level : 3 + 2 * level] * ((px >> (level - 1)) & 1).astype(F32)
        by = by + info[2 + 2 * level : 3 + 2 * level] * ((py >> (level - 1)) & 1).astype(F32)
    flip = (1.0 - 2.0 * bx * gamma_odd[0:NG]) * (1.0 - 2.0 * by * gamma_odd[NG : 2 * NG])
    base = base * info[0:1] * flip
    flip = flip * (1.0 - 2.0 * info[9:10] * gamma_odd[2 * NG :])
    total = base
    for _ in range(3):
        parents = mxu(split_rows(total), expand[...])
        pieces = jnp.concatenate(split(flip * (parents[:NG] + parents[NG:])), 1)
        carried = mxu(down[...], pieces)
        total = base + flip * (carried[:, :128] + carried[:, 128:])
    rows = jnp.concatenate([pltpu.roll(total, (128 - 16 * c) % 128, 1) for c in range(4)], 0)[:, :16]
    spreads = mxu(split_rows(rows), spread[...])
    spreads = spreads[: 4 * NG] + spreads[4 * NG :]
    terms = jnp.concatenate(
        [
            jnp.concatenate([spreads[c * NG : c * NG + NG, k * 128 : k * 128 + 128] for k in range(3)], 0)
            for c in range(4)
        ],
        1,
    )
    values = mxu(poly[...], jnp.concatenate(split(terms), 1))
    field[...] = values[:, :512] + values[:, 512:]
    step = jnp.full((8, 128), COURANT / SUB, F32) / fastest
    for copy in late:
        copy.wait()
    stores = []
    for part in range(4):
        half = part // 2

        def finish(x, carry, half=half):
            for s in range(2):
                c = half * 2 + s
                at = pl.multiple_of(half * 128 + x * 16 + s * 8, 8)
                rows = pl.ds(at, 8)
                acc = [field[pl.ds(pl.multiple_of(i * 64 + x * 8, 8), 8), c * 128 : c * 128 + 128] for i in range(3)]
                old = [u[f, rows] for f in range(NF)]
                for i in range(3):
                    force[i, rows] = acc[i]
                for f in range(NF):
                    slope = change[f, rows]
                    if 1 <= f <= 3:
                        slope = slope + old[0] * acc[f - 1]
                    if f == 4:
                        slope = slope + (old[1] * acc[0] + old[2] * acc[1] + old[3] * acc[2])
                    result[f, rows] = old[f] + step * slope
            return carry

        lax.fori_loop((part % 2) * 4, (part % 2) * 4 + 4, finish, 0)
        rows = slice(part * 64, part * 64 + 64)
        stores += load_all(
            [(result.at[:, rows], section.at[:, rows]), (force.at[:, rows], accel.at[:, rows])],
            sems.at[6 + 2 * part : 8 + 2 * part],
        )
    for copy in stores:
        copy.wait()


ANY = pl.BlockSpec(memory_space=pl.ANY)
HBM = pl.BlockSpec(memory_space=pltpu.HBM)
VMEM = pl.BlockSpec(memory_space=pltpu.VMEM)
SMEM = pl.BlockSpec(memory_space=pltpu.SMEM)


def call(kernel, name, ins, outs, scratch, cost, aliases=None):
    outs = [(o[0], o[1], o[2] if len(o) > 2 else F32) for o in outs]
    return pl.pallas_call(
        kernel,
        out_shape=[pltpu.HBM(s, t) if spec is HBM else jax.ShapeDtypeStruct(s, t) for s, spec, t in outs],
        in_specs=[spec for _, spec in ins],
        out_specs=[spec for _, spec, _ in outs],
        scratch_shapes=scratch,
        input_output_aliases=aliases or {},
        cost_estimate=pl.CostEstimate(flops=cost[0], bytes_accessed=cost[1], transcendentals=cost[2]),
        name=name,
        compiler_params=pltpu.CompilerParams(vmem_limit_bytes=32 << 20),
    )(*[in_hbm(x) if spec is HBM else x for x, spec in ins])


def in_hbm(x):
    return pltpu.with_memory_space_constraint(x, pltpu.HBM)


def scratch_like(x):
    return pltpu.VMEM(x.shape, x.dtype)


def shards(density, momentum, energy, entropy, tracers, leaf_flags):
    con = {k: jnp.asarray(v) for k, v in constants().items()}
    fields = [(x.reshape(-1, ROWS, 128), HBM) for x in (density, momentum, energy, entropy, tracers)]
    ix, iy = lax.axis_index("mx"), lax.axis_index("my")
    pos = (jnp.stack([ix, iy]).astype(jnp.int32), SMEM)
    first = [con[n] for n in ("left", "right", "flag")]
    whole, slab = (NF, ROWS, 128), (NF, 48, 128)
    block, halo = pltpu.VMEM(whole, F32), pltpu.VMEM(slab, F32)
    pay, u, xlo, xhi, ylo, yhi = call(
        prepare_kernel,
        "prepare",
        fields + [(leaf_flags, HBM)] + [(x, HBM) for x in first],
        [((GY, 24, 128), HBM), (whole, VMEM)] + [(slab, HBM)] * 4,
        [pltpu.VMEM((24, 128), F32), halo, halo, pltpu.VMEM((8, 128), F32), scratch_like(leaf_flags)]
        + [scratch_like(x) for x in first]
        + [pltpu.SemaphoreType.DMA((13 + GY,))],
        (10**7, 4 * 10**6, 10**5),
    )
    up_x, down_x = [(i, i + 1) for i in range(GX - 1)], [(i + 1, i) for i in range(GX - 1)]
    up_y, down_y = [(i, i + 1) for i in range(GY - 1)], [(i + 1, i) for i in range(GY - 1)]
    column = lax.all_to_all(pay, "my", 0, 0)
    yl = lax.ppermute(yhi, "my", up_y)
    yr = lax.ppermute(ylo, "my", down_y)
    xl = lax.ppermute(xhi, "mx", up_x)
    xr = lax.ppermute(xlo, "mx", down_x)
    (along_z,) = call(
        flux_z_kernel,
        "flux_z",
        [(u, VMEM)],
        [(whole, HBM)],
        [pltpu.VMEM((2 * NF, 144, 128), F32), pltpu.VMEM((2 * NF, 136, 128), F32), block, pltpu.SemaphoreType.DMA((5,))],
        (2 * 10**7, 4 * 10**6, 3 * 10**5),
    )
    halos = [(x, ANY) for x in (xl, xr, yl, yr)]
    (chunks,) = call(
        relay_kernel,
        "relay",
        [pos, (column.reshape(GY * 24, 128), VMEM), (along_z, HBM)] + halos,
        [((GX, 48, 128), HBM)],
        [pltpu.VMEM((48, 128), F32), pltpu.SemaphoreType.DMA((GX,))],
        (10**4, 10**6, 0),
    )
    far = lax.all_to_all(chunks, "mx", 0, 0)
    second = [con[n] for n in TREE_CONSTANTS]
    tend, *tables = call(
        flux_xy_kernel,
        "flux_xy",
        [pos] + fields + [(along_z, HBM)] + halos + [(x, HBM) for x in second],
        [(whole, HBM)] + [(x.shape, VMEM, x.dtype) for x in second],
        [
            pltpu.VMEM((NF, 352, 128), F32),
            pltpu.VMEM((NF, 272, 128), F32),
            pltpu.VMEM((NF, 512, 128), F32),
            pltpu.VMEM((NF, 384, 128), F32),
            halo,
            halo,
            block,
            block,
            pltpu.SemaphoreType.DMA((14 + len(second),)),
        ],
        (4 * 10**7, 6 * 10**6, 6 * 10**5),
    )
    section, accel = call(
        tree_kernel,
        "tree",
        [pos, (far, VMEM)] + fields + [(tend, HBM)] + [(x, VMEM) for x in tables],
        [(whole, HBM), ((3, ROWS, 128), HBM)],
        [
            pltpu.VMEM((NA * WIN, 128), F32),
            pltpu.VMEM((192, 512), F32),
            block,
            pltpu.VMEM((3, ROWS, 128), F32),
            block,
            block,
            pltpu.SemaphoreType.DMA((14,)),
        ],
        (10**8, 8 * 10**6, 0),
    )
    return section.reshape(NF, 16, 16, 128), accel.reshape(3, 16, 16, 128)


def solution(mesh):
    placed = (
        P("mx", "my", None),
        P(None, "mx", "my", None),
        P("mx", "my", None),
        P("mx", "my", None),
        P(None, "mx", "my", None),
        P("mx", "my", None),
    )
    return jax.shard_map(
        shards,
        mesh=mesh,
        in_specs=placed,
        out_specs=(P(None, "mx", "my", None), P(None, "mx", "my", None)),
        check_vma=False,
    )
```

```python
import functools
import math

import jax
import jax.numpy as jnp
import ml_dtypes
import numpy as np
from jax import lax
from jax.experimental import pallas as pl
from jax.experimental.pallas import tpu as pltpu
from jax.sharding import PartitionSpec as P

F32 = jnp.float32
BF16 = jnp.bfloat16
HIGHEST = lax.Precision.HIGHEST
GRAVITY = 0.02
GAMMA = 5.0 / 3.0
COURANT = 0.3
SUB = 8
NF = 15
GX, GY = 16, 8
ROWS = 256

ALPHA = [
    (px, py, d - px - py)
    for d in range(4)
    for px in range(d, -1, -1)
    for py in range(d - px, -1, -1)
]
NA = len(ALPHA)
NG = 24
WIN = 40
PAIRS = [(px, py) for px in range(4) for py in range(4 - px)]


def factorial_of(e):
    return math.factorial(e[0]) * math.factorial(e[1]) * math.factorial(e[2])


def inverse_derivative(exponent, r):
    axes = [0] * exponent[0] + [1] * exponent[1] + [2] * exponent[2]
    norm = math.sqrt(r[0] ** 2 + r[1] ** 2 + r[2] ** 2)
    if norm == 0.0:
        return 0.0
    if not axes:
        return 1.0 / norm
    if len(axes) == 1:
        return -r[axes[0]] / norm**3
    if len(axes) == 2:
        a, b = axes
        return 3.0 * r[a] * r[b] / norm**5 - float(a == b) / norm**3
    a, b, c = axes
    crossed = float(a == b) * r[c] + float(a == c) * r[b] + float(b == c) * r[a]
    return -15.0 * r[a] * r[b] * r[c] / norm**7 + 3.0 * crossed / norm**5


def split_np(x):
    high = x.astype(np.float32).astype(ml_dtypes.bfloat16)
    low = (x - high.astype(np.float64)).astype(ml_dtypes.bfloat16)
    return high, low


def exact_np(x):
    y = x.astype(ml_dtypes.bfloat16)
    assert np.array_equal(x, y.astype(np.float64))
    return y


@functools.cache
def constants():
    out = {}
    w = np.zeros((7, NG, NA, WIN))
    for z in range(7):
        for i in range(6):
            for j in range(6):
                r = (-(i - 2.0), -(j - 2.0), -(z - 3.0))
                for g, eg in enumerate(ALPHA):
                    for a, ea in enumerate(ALPHA):
                        if sum(eg) + sum(ea) <= 3:
                            e = tuple(eg[k] + ea[k] for k in range(3))
                            w[z, g, a, i * 6 + j] = (
                                -GRAVITY
                                * (-1.0) ** sum(ea)
                                / (factorial_of(ea) * factorial_of(eg))
                                * inverse_derivative(e, r)
                            )
    out["w_high"], out["w_low"] = split_np(w.reshape(7 * NG, NA * WIN))
    sel = np.zeros((4, WIN, 40))
    sign = np.zeros((4, 384))
    for c in range(4):
        cx, cy = c >> 1, c & 1
        for i in range(6):
            for j in range(6):
                si, sj = (5 - i if cx else i), (5 - j if cy else j)
                sel[c, i * 6 + j, ((si // 2) * 3 + sj // 2) * 4 + (si % 2) * 2 + sj % 2] = 1.0
        for a, e in enumerate(ALPHA):
            sign[c, a * 16 : a * 16 + 16] = (-1.0) ** (cx * e[0] + cy * e[1])
    out["sel_zero"] = sel.reshape(4 * WIN, 40).astype(ml_dtypes.bfloat16)
    lanes = np.zeros((16, 384), np.float32)
    lanes[0:4] = sign
    for a, e in enumerate(ALPHA):
        for r in range(16):
            lane = a * 16 + r
            level = 1 if r < 8 else 2 if r < 12 else 3
            lanes[4 + level, lane] = e[0] % 2
            lanes[8 + level, lane] = e[1] % 2
    out["lane_odd"] = lanes
    up = np.zeros((384, 384))
    for t, et in enumerate(ALPHA):
        for s, es in enumerate(ALPHA):
            if all(es[k] <= et[k] for k in range(3)):
                for base, to, count in ((0, 8, 8), (8, 12, 4)):
                    for z in range(count):
                        v = 2.0 ** -sum(et)
                        for k in range(3):
                            d = -0.5 if k < 2 or z % 2 == 0 else 0.5
                            v *= math.comb(et[k], es[k]) * d ** (et[k] - es[k])
                        up[s * 16 + base + z, t * 16 + to + z // 2] = v
    out["up"] = exact_np(up)
    odd = np.zeros((16, 384), np.float32)
    for a, e in enumerate(ALPHA):
        odd[0, a * 16 : a * 16 + 16] = e[0] % 2
        odd[1, a * 16 : a * 16 + 16] = e[1] % 2
    out["alpha_odd"] = odd
    agg = np.zeros((32, 128))
    for x in range(GX):
        for y in range(GY):
            agg[(x // 2) * 4 + y // 2, (y % 2) * 64 + x * 4 + y // 2] = 1.0
    out["agg"] = agg.astype(ml_dtypes.bfloat16)
    mask = np.zeros((8, 128), np.float32)
    info = np.zeros((16, 128), np.float32)
    expand = np.zeros((128, 128), np.float32)
    for lane in range(96):
        g, r = lane // 16, lane % 16
        if g < 4:
            n, z, level = 16, r, 0
        elif r < 8:
            n, z, level = 8, r, 1
        elif r < 12:
            n, z, level = 4, r - 8, 2
        elif r < 14:
            n, z, level = 2, r - 12, 3
        else:
            continue
        for k in range(7):
            o = k - 3
            ok = 0 <= z + o < n and abs((z + o) // 2 - z // 2) <= 1
            if g == 4:
                ok = ok and abs(o) > 1
            if g == 5:
                ok = ok and abs(o) <= 1
            mask[k, lane] = float(ok)
        if g < 5:
            info[0, lane] = 2.0**-level
            info[1, lane] = float(g >> 1) if level == 0 else 0.0
            info[2, lane] = float(g & 1) if level == 0 else 0.0
            info[2 + 2 * level, lane] = 1.0 if level else info[2, lane]
            info[9, lane] = float(z % 2)
            if level == 0:
                expand[64 + z // 2, lane] = 1.0
            elif level == 1:
                expand[64 + 8 + z // 2, lane] = 1.0
            elif level == 2:
                expand[64 + 12 + z // 2, lane] = 1.0
    out["mask"] = mask
    out["info"] = info
    out["expand"] = exact_np(expand)
    gamma_odd = np.zeros((3 * NG, 128), np.float32)
    down = np.zeros((NG, NG))
    for g, eg in enumerate(ALPHA):
        for k in range(3):
            gamma_odd[k * NG + g] = eg[k] % 2
        for b, eb in enumerate(ALPHA):
            if all(eb[k] >= eg[k] for k in range(3)):
                v = 2.0 ** -sum(eg)
                for k in range(3):
                    n = eb[k] - eg[k]
                    v *= (-0.25) ** n * math.comb(eb[k], eg[k])
                down[g, b] = v
    out["gamma_odd"] = gamma_odd
    out["down"] = exact_np(down)
    h = (np.arange(SUB) + 0.5) / SUB - 0.5
    spread = np.zeros((16, 384))
    for k in range(3):
        for z in range(128):
            spread[z // 8, k * 128 + z] = h[z % 8] ** k
    out["spread"] = exact_np(spread)
    poly = np.zeros((3, 8, 8, 3, NG))
    for i in range(3):
        for g, e in enumerate(ALPHA):
            if e[i] > 0:
                low = list(e)
                low[i] -= 1
                poly[i, :, :, low[2], g] = (
                    -e[i] * h[:, None] ** low[0] * h[None, :] ** low[1]
                )
    out["poly"] = exact_np(poly.reshape(192, 72))
    cells = np.arange(16)
    near = h[cells % 8]
    far = ((cells + 0.5) / 8 - 1.0) / 2
    left = np.zeros((2, len(PAIRS), 8, 16, 16))
    for q, (px, py) in enumerate(PAIRS):
        for c in range(4):
            block = ((cells // 8 == c >> 1)[:, None] & (cells // 8 == (c & 1))[None, :]).astype(float)
            left[0, q, c] = block * near[:, None] ** px * near[None, :] ** py
            left[1, q, c] = block * far[:, None] ** px * far[None, :] ** py
    out["left"] = left.reshape(160, 256).astype(np.float32)
    right = np.zeros((128, 128))
    flag = np.zeros((128, 128))
    for z in range(128):
        s = z // 8
        f = ((z % 16 + 0.5) / 8 - 1.0) / 2
        for pz in range(4):
            right[z, pz * 16 + s] = h[z % 8] ** pz / SUB**3
            right[z, 64 + (s % 2) * 32 + pz * 8 + s // 2] = f**pz / SUB**3
    for s in range(16):
        for pz in range(4):
            flag[s, pz * 16 + s] = 1.0
            flag[s, 64 + (s % 2) * 32 + pz * 8 + s // 2] = 1.0
    out["right"] = right.astype(np.float32)
    out["flag"] = flag.astype(ml_dtypes.bfloat16)
    return out


def split(x):
    high = x.astype(BF16)
    return high, (x - high.astype(F32)).astype(BF16)


def split_rows(x):
    high = x.astype(BF16).astype(F32)
    return jnp.concatenate([high, x - high], 0).astype(BF16)


def mxu(a, b):
    return jnp.dot(a, b, preferred_element_type=F32)


def exact(a, b):
    return jnp.dot(a, b, precision=HIGHEST, preferred_element_type=F32)


def lane_ids(shape):
    return lax.broadcasted_iota(jnp.int32, shape, len(shape) - 1)


def row_ids(shape):
    return lax.broadcasted_iota(jnp.int32, shape, len(shape) - 2)


def power(s):
    return jnp.exp2(GAMMA * jnp.log2(s))


def root(x):
    return x * lax.rsqrt(x)


PLACES = ((0, 1), (1, 3), (4, 1), (5, 1), (6, 9))


def load_all(pairs, sems):
    copies = [pltpu.make_async_copy(source, target, sems.at[k]) for k, (source, target) in enumerate(pairs)]
    for copy in copies:
        copy.start()
    return copies


def fields_into(refs, target, source=slice(0, ROWS), rows=None):
    place = slice(0, source.stop - source.start) if rows is None else rows
    return [
        (ref.at[:, source], target.at[start : start + count, place]) for ref, (start, count) in zip(refs, PLACES)
    ]


def prepare_kernel(pos, den, mom, ene, ent, tra, flags, left, right, flag, pay_h, u, xa, xb, ya_h, yb_h, *scratch):
    pay, ya, yb, fl, flv, leftv, rightv, flagv, sems = scratch
    small = load_all(zip((flags, left, right, flag), (flv, leftv, rightv, flagv)), sems.at[7:11])
    loads = load_all(fields_into((den, mom, ene, ent, tra), u), sems.at[0:5])
    even_x, even_y = pos[0] % 2 == 0, pos[1] % 2 == 0
    for copy in small:
        copy.wait()
    fl[...] = jnp.zeros((8, 128), F32)
    fl[0:2, 0:16] = flv[0].astype(F32)
    fl[2:4, 0:16] = flv[1].astype(F32)
    tile = mxu(fl[...].astype(BF16), flagv[...])
    for k in (0, 1, 3):
        loads[k].wait()
    rho = u[0]
    sums = exact(leftv[...], exact(rho, rightv[...]))
    inverse = 1.0 / rho
    fast = jnp.maximum(jnp.maximum(jnp.abs(u[1]), jnp.abs(u[2])), jnp.abs(u[3]))
    sound = root(GAMMA * (GAMMA - 1.0) * power(u[5]) * inverse)
    fastest = jnp.max(fast * inverse + sound)
    lane = lane_ids((8, 128))
    row = row_ids((8, 128))
    tiles = [jnp.zeros((8, 128), F32) for _ in range(3)]
    zero, one = {}, {}
    for q, pair in enumerate(PAIRS):
        zero[pair] = sums[q * 8 : q * 8 + 8] * tile
        v = jnp.sum(sums[80 + q * 8 : 88 + q * 8] * tile, axis=0, keepdims=True)
        v = jnp.broadcast_to(v, (8, 128))
        one[pair] = v + pltpu.roll(v, 96, 1)
    for a, e in enumerate(ALPHA):
        c, to = a // 8, (a % 8) * 16
        low = pltpu.roll(zero[e[0], e[1]], (to - e[2] * 16) % 128, 1)
        top = pltpu.roll(one[e[0], e[1]], (to - 64 - e[2] * 8) % 128, 1)
        here = (lane >= to) & (lane < to + 16)
        tiles[c] = jnp.where(here & (row < 4), low, tiles[c])
        tiles[c] = jnp.where(here & (row == 4) & (lane < to + 8), top, tiles[c])
    tiles[2] = jnp.where((row == 4) & (lane >= 64) & (lane < 72), fastest, tiles[2])
    for c in range(3):
        pay[c * 8 : c * 8 + 8] = tiles[c]
    slabs = load_all([(pay, pay_h.at[y]) for y in range(GY)], sems.at[13 : 13 + GY])
    for k in (2, 4):
        loads[k].wait()
    row_a, row_b = jnp.where(even_x, 208, 0), jnp.where(even_x, 0, 208)
    slabs += load_all(
        [(u.at[:, pl.ds(pl.multiple_of(r, 8), 48)], slab) for r, slab in ((row_a, xa), (row_b, xb))], sems.at[5:7]
    )
    for k in range(3):
        for s in range(2):
            at = slice(k * 16 + s * 8, k * 16 + s * 8 + 8)
            for f in range(NF):
                low, high = u[f, pl.ds(s * 128 + k, 8, stride=16)], u[f, pl.ds(s * 128 + 13 + k, 8, stride=16)]
                ya[f, at] = jnp.where(even_y, high, low)
                yb[f, at] = jnp.where(even_y, low, high)
    slabs += load_all([(ya, ya_h), (yb, yb_h)], sems.at[11:13])
    for copy in slabs:
        copy.wait()


def relay_kernel(pos, column, *rest):
    out_h, out, sems = rest[-3:]
    y = pos[1]
    even = [column[pl.ds(c * 8 + 4, 4, stride=48)] for c in range(3)]
    odd = [column[pl.ds(c * 8 + 28, 4, stride=48)] for c in range(3)]
    near = []
    for dy in range(3):
        here = jnp.clip(y + dy - 1, 0, GY - 1)
        inside = here == y + dy - 1
        for c in range(3):
            tile = column[pl.ds(pl.multiple_of(here * 24 + c * 8, 8), 8)]
            near.append(jnp.where(inside, tile, 0.0))
    for c in range(3):
        out[c * 4 : c * 4 + 4] = even[c] + pltpu.roll(odd[c], 8, 1)
    for n, tile in enumerate(near):
        out[12 + n * 4 : 16 + n * 4] = tile[0:4]
    for copy in load_all([(out, out_h.at[x]) for x in range(GX)], sems):
        copy.wait()


def states(ol, il, l, r, ir, orr):
    face = (37.0 / 60.0) * (l + r) - (8.0 / 60.0) * (il + ir) + (1.0 / 60.0) * (ol + orr)
    low, high = jnp.minimum(l, r), jnp.maximum(l, r)
    left = jnp.minimum(jnp.maximum(face, jnp.minimum(il, low)), jnp.maximum(il, high))
    right = jnp.minimum(jnp.maximum(face, jnp.minimum(low, ir)), jnp.maximum(high, ir))
    return left, right


def fluxes(load, d, store):
    rl, rr = load(0)
    ml, mr = load(1 + d)
    sl, sr = load(5)
    il, ir = 1.0 / rl, 1.0 / rr
    vl, vr = ml * il, mr * ir
    gl, gr = power(sl), power(sr)
    cl, cr = root(GAMMA * (GAMMA - 1.0) * gl * il), root(GAMMA * (GAMMA - 1.0) * gr * ir)
    a = 4.0 * jnp.maximum(jnp.abs(vl) + cl, jnp.abs(vr) + cr)
    wl, wr = 4.0 * vl, 4.0 * vr
    kl, kr = wl + a, wr - a
    got = {0: (rl, rr), 1 + d: (ml, mr), 5: (sl, sr)}
    for f in range(NF):
        left, right = got[f] if f in got else load(f)
        flux = left * kl + right * kr
        if f == 1 + d:
            flux = flux + (4.0 * (GAMMA - 1.0)) * (gl + gr)
        if f == 4:
            flux = flux + (GAMMA - 1.0) * (gl * wl + gr * wr)
        store(f, flux)


def flux_z_kernel(u, out_h, uz, fz, out, sems):
    for f in range(NF):
        for half in range(2):
            cells = u[f, half * 128 : half * 128 + 128].T
            uz[2 * f + half, 8:136] = cells
            uz[2 * f + half, 0:8] = jnp.broadcast_to(cells[0:1], (8, 128))
            uz[2 * f + half, 136:144] = jnp.broadcast_to(cells[127:128], (8, 128))

    def faces_z(i, carry):
        for half in range(2):

            def load(f):
                return states(*[uz[2 * f + half, pl.ds(i * 8 + 5 + k, 8)] for k in range(6)])

            def store(f, flux):
                fz[2 * f + half, pl.ds(pl.multiple_of(i * 8, 8), 8)] = flux

            fluxes(load, 2, store)
        return carry

    lax.fori_loop(0, 16, faces_z, 0)
    for half in range(2):

        def load_top(f, half=half):
            rows = [uz[2 * f + half, 133 + k : 141 + k] for k in range(4)]
            return states(*rows, rows[3], rows[3])

        def store_top(f, flux, half=half):
            fz[2 * f + half, 128:136] = flux

        fluxes(load_top, 2, store_top)

    stores = []
    for part in range(5):
        for f in range(part * 3, part * 3 + 3):
            for half in range(2):
                out[f, half * 128 : half * 128 + 128] = (fz[2 * f + half, 0:128] - fz[2 * f + half, 1:129]).T
        some = slice(part * 3, part * 3 + 3)
        stores += load_all([(out.at[some], out_h.at[some])], sems.at[part : part + 1])
    for copy in stores:
        copy.wait()


def flux_xy_kernel(pos, den, mom, ene, ent, tra, along_z_h, xa, xb, ya_h, yb_h, *args):
    count = len(TREE_CONSTANTS)
    out_h = args[count]
    tables = args[count + 1 : 2 * count + 1]
    ux, fx, uy, fy, ya, yb, along_z, out, sems = args[2 * count + 1 :]
    even_x, even_y = pos[0] % 2 == 0, pos[1] % 2 == 0
    row_a, row_b = [pl.ds(pl.multiple_of(jnp.where(even_x, p, q), 8), 48) for p, q in ((304, 0), (0, 304))]
    loads = load_all(
        fields_into((den, mom, ene, ent, tra), ux, rows=slice(48, 304))
        + [(xa, ux.at[:, row_a]), (xb, ux.at[:, row_b]), (ya_h, ya), (yb_h, yb), (along_z_h, along_z)],
        sems.at[0:10],
    )
    late = load_all(list(zip(args[:count], tables)), sems.at[10 : 10 + count])
    for copy in loads[:7]:
        copy.wait()

    def repeat(source, target):
        for f in range(NF):
            cells = ux[f, source : source + 16]
            for k in range(3):
                ux[f, target + k * 16 : target + k * 16 + 16] = cells

    pl.when(pos[0] == 0)(lambda: repeat(48, 0))
    pl.when(pos[0] == GX - 1)(lambda: repeat(288, 304))

    def faces_x(i, carry):
        for s in range(2):

            def load(f):
                return states(*[ux[f, pl.ds(pl.multiple_of((i + k) * 16 + s * 8, 8), 8)] for k in range(6)])

            def store(f, flux):
                fx[f, pl.ds(pl.multiple_of(i * 16 + s * 8, 8), 8)] = flux

            fluxes(load, 0, store)
        return carry

    lax.fori_loop(0, 17, faces_x, 0)

    def spread(x, carry):
        for f in range(NF):
            uy[f, pl.ds(pl.multiple_of(x * 32 + 8, 8), 16)] = ux[f, pl.ds(pl.multiple_of(48 + x * 16, 8), 16)]
        return carry

    lax.fori_loop(0, 16, spread, 0)
    for copy in loads[7:9]:
        copy.wait()
    first, last = pos[1] == 0, pos[1] == GY - 1
    for f in range(NF):
        for s in range(2):
            low, high = ux[f, pl.ds(48 + s * 128, 8, stride=16)], ux[f, pl.ds(63 + s * 128, 8, stride=16)]
            for k in range(3):
                at = slice(k * 16 + s * 8, k * 16 + s * 8 + 8)
                uy[f, pl.ds(s * 256 + 5 + k, 8, stride=32)] = jnp.where(first, low, jnp.where(even_y, yb[f, at], ya[f, at]))
                uy[f, pl.ds(s * 256 + 24 + k, 8, stride=32)] = jnp.where(last, high, jnp.where(even_y, ya[f, at], yb[f, at]))

    for s in range(2):

        def load_end(f, s=s):
            return states(*[uy[f, pl.ds(s * 256 + 21 + k, 8, stride=32)] for k in range(6)])

        def store_end(f, flux, s=s):
            fy[f, pl.ds(s * 192 + 16, 8, stride=24)] = flux

        fluxes(load_end, 1, store_end)
    def faces_y(x):
        for s in range(2):

            def load(f):
                return states(*[uy[f, pl.ds(x * 32 + s * 8 + 5 + k, 8)] for k in range(6)])

            def store(f, flux):
                fy[f, pl.ds(pl.multiple_of(x * 24 + s * 8, 8), 8)] = flux

            fluxes(load, 1, store)

    loads[9].wait()

    def gather(x):
        for f in range(NF):
            for s in range(2):
                at = pl.multiple_of(x * 16 + s * 8, 8)
                rows = pl.ds(at, 8)
                change = along_z[f, rows] + (fx[f, rows] - fx[f, pl.ds(pl.multiple_of(at + 16, 8), 8)])
                y = pl.multiple_of(x * 24 + s * 8, 8)
                out[f, rows] = change + (fy[f, pl.ds(y, 8)] - fy[f, pl.ds(y + 1, 8)])

    def both(x, carry):
        gather(x - 1)
        faces_y(x)
        return carry

    faces_y(0)
    for part in range(4):
        lax.fori_loop(part * 4 + 1, min(part * 4 + 5, 16), both, 0)
        if part == 3:
            gather(15)
        rows = slice(part * 64, part * 64 + 64)
        late += load_all([(out.at[:, rows], out_h.at[:, rows])], sems.at[10 + count + part : 11 + count + part])
    for copy in late:
        copy.wait()


TREE_CONSTANTS = (
    "w_high", "w_low", "sel_zero", "lane_odd", "up", "alpha_odd", "agg", "mask", "info", "expand", "gamma_odd", "down",
    "spread", "poly",
)


def tree_kernel(pos, far, den, mom, ene, ent, tra, change_h, *args):
    count = len(TREE_CONSTANTS)
    w_high, w_low, sel_zero, lane_odd, up, alpha_odd, agg, mask, info, expand, gamma_odd, down, spread, poly = args[:count]
    section, accel, rhs, field, result, force, u, change, sems = args[count:]
    late = []
    for q in range(4):
        rows = slice(q * 64, q * 64 + 64)
        pairs = fields_into((den, mom, ene, ent, tra), u, rows, rows) + [(change_h.at[:, rows], change.at[:, rows])]
        late.append(load_all(pairs, sems.at[8 + 6 * q : 14 + 6 * q]))
    px, py = pos[0], pos[1]
    blocks = []
    for dx in range(3):
        here = jnp.clip(px + dx - 1, 0, GX - 1)
        inside = here == px + dx - 1
        blocks.append([jnp.where(inside, far[here, 12 + n * 4 : 16 + n * 4], 0.0) for n in range(9)])
    gap = jnp.zeros((4, 128), F32)
    around = jnp.concatenate(
        [jnp.concatenate([blocks[dx][dy * 3 + c] for dx in range(3) for dy in range(3)] + [gap], 0) for c in range(3)], 1
    )
    zero = mxu(sel_zero[...], jnp.concatenate(split(around), 1))
    zero = zero[:, :384] + zero[:, 384:]
    arrays = [zero[c * WIN : c * WIN + WIN] * lane_odd[c : c + 1] for c in range(4)]
    packed = [jnp.concatenate([far[x, c * 4 : c * 4 + 4] for x in range(GX)], 0) for c in range(3)]
    lower = lane_ids((128, 128)) % 16 < 8
    gathered = jnp.concatenate(
        [jnp.where(lower, jnp.concatenate([rows, pltpu.roll(rows, 120, 1)], 0), 0.0) for rows in packed], 1
    )
    speeds = gathered[:, 256:]
    fastest = jnp.max(jnp.where(lane_ids((128, 128)) >= 64, speeds, 0.0))

    def lifted(x, x_odd, y_odd):
        sign = (1.0 - 2.0 * x_odd * alpha_odd[0:1]) * (1.0 - 2.0 * y_odd * alpha_odd[1:2])
        n = x.shape[0]
        z = mxu(jnp.concatenate(split(x * sign), 0), up[...])
        return (z[:n] + z[n:]) * sign

    def picked(matrix, x):
        y = mxu(matrix, jnp.concatenate(split(x), 1))
        return y[:, :384] + y[:, 384:]

    dev = lax.broadcasted_iota(jnp.int32, (128, 1), 0)
    raised = lifted(gathered, ((dev // 4) % 2).astype(F32), (dev // 64).astype(F32))
    two = picked(agg[...], raised)
    cell = lax.broadcasted_iota(jnp.int32, (32, 1), 0)
    raised_two = lifted(two, ((cell // 4) % 2).astype(F32), (cell % 2).astype(F32))

    def window(level, columns, shift):
        tx, ty = px >> (level - 1), py >> (level - 1)
        row = lax.broadcasted_iota(jnp.int32, (WIN, columns), 0)
        col = lax.broadcasted_iota(jnp.int32, (WIN, columns), 1)
        i, j = row // 6, row % 6
        i = jnp.where((tx & 1) == 1, 5 - i, i) + 2 * ((tx >> 1) - 1)
        j = jnp.where((ty & 1) == 1, 5 - j, j) + 2 * ((ty >> 1) - 1)
        if columns == 128:
            sx, sy = (col % 64) // 4, 2 * (col % 4) + col // 64
        else:
            sx, sy = col // 4, col % 4
        sx, sy = sx >> shift, sy >> shift
        return ((row < 36) & (sx == i) & (sy == j)).astype(F32).astype(BF16)

    levels = (
        picked(window(1, 128, 0), gathered)
        + picked(window(2, 128, 1), raised)
        + picked(window(3, 32, 1), raised_two)
    )
    sign = jnp.ones((1, 384), F32)
    for level in (1, 2, 3):
        bx = ((px >> (level - 1)) & 1).astype(F32)
        by = ((py >> (level - 1)) & 1).astype(F32)
        sign = sign * (1.0 - 2.0 * bx * lane_odd[4 + level : 5 + level])
        sign = sign * (1.0 - 2.0 * by * lane_odd[8 + level : 9 + level])
    levels = levels * sign
    wrow = lax.broadcasted_iota(jnp.int32, (WIN, 384), 0)
    wi, wj = wrow // 6, wrow % 6
    touching = (wi >= 1) & (wi <= 3) & (wj >= 1) & (wj <= 3)
    arrays += [levels, jnp.where(touching, 0.0, levels)]
    lane = lane_ids((WIN, 128)) // 16
    for a in range(NA):
        c, off = a // 8, (a % 8) * 16
        block = jnp.zeros((WIN, 128), F32)
        for g, array in enumerate(arrays):
            block = jnp.where(lane == g, pltpu.roll(array[:, c * 128 : c * 128 + 128], (16 * g - off) % 128, 1), block)
        rhs[a * WIN : a * WIN + WIN] = block
    high, low = split(rhs[...])
    y = mxu(w_high[...], jnp.concatenate([high, low], 1))
    y = y[:, :128] + y[:, 128:] + mxu(w_low[...], high)
    base = jnp.zeros((NG, 128), F32)
    for k in range(7):
        base = base + mask[k : k + 1] * pltpu.roll(y[k * NG : k * NG + NG], (3 - k) % 128, 1)
    lanes = lane_ids((NG, 128)) // 16
    base = base + jnp.where(lanes == 4, pltpu.roll(base, 112, 1), 0.0)
    bx, by = info[1:2], info[2:3]
    for level in (1, 2, 3):
        bx = bx + info[2 + 2 * level : 3 + 2 * level] * ((px >> (level - 1)) & 1).astype(F32)
        by = by + info[2 + 2 * level : 3 + 2 * level] * ((py >> (level - 1)) & 1).astype(F32)
    flip = (1.0 - 2.0 * bx * gamma_odd[0:NG]) * (1.0 - 2.0 * by * gamma_odd[NG : 2 * NG])
    base = base * info[0:1] * flip
    flip = flip * (1.0 - 2.0 * info[9:10] * gamma_odd[2 * NG :])
    total = base
    for _ in range(3):
        parents = mxu(split_rows(total), expand[...])
        pieces = jnp.concatenate(split(flip * (parents[:NG] + parents[NG:])), 1)
        carried = mxu(down[...], pieces)
        total = base + flip * (carried[:, :128] + carried[:, 128:])
    rows = jnp.concatenate([pltpu.roll(total, (128 - 16 * c) % 128, 1) for c in range(4)], 0)[:, :16]
    spreads = mxu(split_rows(rows), spread[...])
    spreads = spreads[: 4 * NG] + spreads[4 * NG :]
    terms = jnp.concatenate(
        [
            jnp.concatenate([spreads[c * NG : c * NG + NG, k * 128 : k * 128 + 128] for k in range(3)], 0)
            for c in range(4)
        ],
        1,
    )
    values = mxu(poly[...], jnp.concatenate(split(terms), 1))
    field[...] = values[:, :512] + values[:, 512:]
    step = jnp.full((8, 128), COURANT / SUB, F32) / fastest
    stores = []
    for part in range(4):
        half = part // 2
        for copy in late[part]:
            copy.wait()

        def finish(x, carry, half=half):
            for s in range(2):
                c = half * 2 + s
                at = pl.multiple_of(half * 128 + x * 16 + s * 8, 8)
                rows = pl.ds(at, 8)
                acc = [field[pl.ds(pl.multiple_of(i * 64 + x * 8, 8), 8), c * 128 : c * 128 + 128] for i in range(3)]
                old = [u[f, rows] for f in range(NF)]
                for i in range(3):
                    force[i, rows] = acc[i]
                for f in range(NF):
                    slope = change[f, rows]
                    if 1 <= f <= 3:
                        slope = slope + old[0] * acc[f - 1]
                    if f == 4:
                        slope = slope + (old[1] * acc[0] + old[2] * acc[1] + old[3] * acc[2])
                    result[f, rows] = old[f] + step * slope
            return carry

        lax.fori_loop((part % 2) * 4, (part % 2) * 4 + 4, finish, 0)
        rows = slice(part * 64, part * 64 + 64)
        stores += load_all(
            [(result.at[:, rows], section.at[:, rows]), (force.at[:, rows], accel.at[:, rows])],
            sems.at[2 * part : 2 * part + 2],
        )
    for copy in stores:
        copy.wait()


ANY = pl.BlockSpec(memory_space=pl.ANY)
HBM = pl.BlockSpec(memory_space=pltpu.HBM)
VMEM = pl.BlockSpec(memory_space=pltpu.VMEM)
SMEM = pl.BlockSpec(memory_space=pltpu.SMEM)


def call(kernel, name, ins, outs, scratch, cost, aliases=None):
    outs = [(o[0], o[1], o[2] if len(o) > 2 else F32) for o in outs]
    return pl.pallas_call(
        kernel,
        out_shape=[pltpu.HBM(s, t) if spec is HBM else jax.ShapeDtypeStruct(s, t) for s, spec, t in outs],
        in_specs=[spec for _, spec in ins],
        out_specs=[spec for _, spec, _ in outs],
        scratch_shapes=scratch,
        input_output_aliases=aliases or {},
        cost_estimate=pl.CostEstimate(flops=cost[0], bytes_accessed=cost[1], transcendentals=cost[2]),
        name=name,
        compiler_params=pltpu.CompilerParams(vmem_limit_bytes=32 << 20),
    )(*[in_hbm(x) if spec is HBM else x for x, spec in ins])


def in_hbm(x):
    return pltpu.with_memory_space_constraint(x, pltpu.HBM)


def scratch_like(x):
    return pltpu.VMEM(x.shape, x.dtype)


def shards(density, momentum, energy, entropy, tracers, leaf_flags):
    con = {k: jnp.asarray(v) for k, v in constants().items()}
    fields = [(x.reshape(-1, ROWS, 128), HBM) for x in (density, momentum, energy, entropy, tracers)]
    ix, iy = lax.axis_index("mx"), lax.axis_index("my")
    pos = (jnp.stack([ix, iy]).astype(jnp.int32), SMEM)
    first = [con[n] for n in ("left", "right", "flag")]
    whole, slab = (NF, ROWS, 128), (NF, 48, 128)
    block, halo = pltpu.VMEM(whole, F32), pltpu.VMEM(slab, F32)
    pay, u, xa, xb, ya, yb = call(
        prepare_kernel,
        "prepare",
        [pos] + fields + [(leaf_flags, HBM)] + [(x, HBM) for x in first],
        [((GY, 24, 128), HBM), (whole, VMEM)] + [(slab, HBM)] * 4,
        [pltpu.VMEM((24, 128), F32), halo, halo, pltpu.VMEM((8, 128), F32), scratch_like(leaf_flags)]
        + [scratch_like(x) for x in first]
        + [pltpu.SemaphoreType.DMA((13 + GY,))],
        (10**7, 4 * 10**6, 10**5),
    )

    def pairs(count, start):
        lows = range(start, count - 1, 2)
        return [(i, i + 1) for i in lows] + [(i + 1, i) for i in lows]

    column = lax.all_to_all(pay, "my", 0, 0)
    halos = [
        (lax.ppermute(slab, axis, pairs(count, start)), ANY)
        for slab, axis, count, start in ((xa, "mx", GX, 0), (xb, "mx", GX, 1), (ya, "my", GY, 0), (yb, "my", GY, 1))
    ]
    (along_z,) = call(
        flux_z_kernel,
        "flux_z",
        [(u, VMEM)],
        [(whole, HBM)],
        [pltpu.VMEM((2 * NF, 144, 128), F32), pltpu.VMEM((2 * NF, 136, 128), F32), block, pltpu.SemaphoreType.DMA((5,))],
        (2 * 10**7, 4 * 10**6, 3 * 10**5),
    )
    (chunks,) = call(
        relay_kernel,
        "relay",
        [pos, (column.reshape(GY * 24, 128), VMEM), (along_z, HBM)] + halos,
        [((GX, 48, 128), HBM)],
        [pltpu.VMEM((48, 128), F32), pltpu.SemaphoreType.DMA((GX,))],
        (10**4, 10**6, 0),
    )
    far = lax.all_to_all(chunks, "mx", 0, 0)
    second = [con[n] for n in TREE_CONSTANTS]
    tend, *tables = call(
        flux_xy_kernel,
        "flux_xy",
        [pos] + fields + [(along_z, HBM)] + halos + [(x, HBM) for x in second],
        [(whole, HBM)] + [(x.shape, VMEM, x.dtype) for x in second],
        [
            pltpu.VMEM((NF, 352, 128), F32),
            pltpu.VMEM((NF, 272, 128), F32),
            pltpu.VMEM((NF, 512, 128), F32),
            pltpu.VMEM((NF, 384, 128), F32),
            halo,
            halo,
            block,
            block,
            pltpu.SemaphoreType.DMA((14 + len(second),)),
        ],
        (4 * 10**7, 6 * 10**6, 6 * 10**5),
    )
    section, accel = call(
        tree_kernel,
        "tree",
        [pos, (far, VMEM)] + fields + [(tend, HBM)] + [(x, VMEM) for x in tables],
        [(whole, HBM), ((3, ROWS, 128), HBM)],
        [
            pltpu.VMEM((NA * WIN, 128), F32),
            pltpu.VMEM((192, 512), F32),
            block,
            pltpu.VMEM((3, ROWS, 128), F32),
            block,
            block,
            pltpu.SemaphoreType.DMA((32,)),
        ],
        (10**8, 8 * 10**6, 0),
    )
    return section.reshape(NF, 16, 16, 128), accel.reshape(3, 16, 16, 128)


def solution(mesh):
    placed = (
        P("mx", "my", None),
        P(None, "mx", "my", None),
        P("mx", "my", None),
        P("mx", "my", None),
        P(None, "mx", "my", None),
        P("mx", "my", None),
    )
    return jax.shard_map(
        shards,
        mesh=mesh,
        in_specs=placed,
        out_specs=(P(None, "mx", "my", None), P(None, "mx", "my", None)),
        check_vma=False,
    )
```

```python
import functools
import math

import jax
import jax.numpy as jnp
import ml_dtypes
import numpy as np
from jax import lax
from jax.experimental import pallas as pl
from jax.experimental.pallas import tpu as pltpu
from jax.sharding import PartitionSpec as P

F32 = jnp.float32
BF16 = jnp.bfloat16
HIGHEST = lax.Precision.HIGHEST
GRAVITY = 0.02
GAMMA = 5.0 / 3.0
COURANT = 0.3
SUB = 8
NF = 15
GX, GY = 16, 8
ROWS = 256

ALPHA = [
    (px, py, d - px - py)
    for d in range(4)
    for px in range(d, -1, -1)
    for py in range(d - px, -1, -1)
]
NA = len(ALPHA)
NG = 24
WIN = 40
PAIRS = [(px, py) for px in range(4) for py in range(4 - px)]


def factorial_of(e):
    return math.factorial(e[0]) * math.factorial(e[1]) * math.factorial(e[2])


def inverse_derivative(exponent, r):
    axes = [0] * exponent[0] + [1] * exponent[1] + [2] * exponent[2]
    norm = math.sqrt(r[0] ** 2 + r[1] ** 2 + r[2] ** 2)
    if norm == 0.0:
        return 0.0
    if not axes:
        return 1.0 / norm
    if len(axes) == 1:
        return -r[axes[0]] / norm**3
    if len(axes) == 2:
        a, b = axes
        return 3.0 * r[a] * r[b] / norm**5 - float(a == b) / norm**3
    a, b, c = axes
    crossed = float(a == b) * r[c] + float(a == c) * r[b] + float(b == c) * r[a]
    return -15.0 * r[a] * r[b] * r[c] / norm**7 + 3.0 * crossed / norm**5


def split_np(x):
    high = x.astype(np.float32).astype(ml_dtypes.bfloat16)
    low = (x - high.astype(np.float64)).astype(ml_dtypes.bfloat16)
    return high, low


def exact_np(x):
    y = x.astype(ml_dtypes.bfloat16)
    assert np.array_equal(x, y.astype(np.float64))
    return y


@functools.cache
def constants():
    out = {}
    w = np.zeros((7, NG, NA, WIN))
    for z in range(7):
        for i in range(6):
            for j in range(6):
                r = (-(i - 2.0), -(j - 2.0), -(z - 3.0))
                for g, eg in enumerate(ALPHA):
                    for a, ea in enumerate(ALPHA):
                        if sum(eg) + sum(ea) <= 3:
                            e = tuple(eg[k] + ea[k] for k in range(3))
                            w[z, g, a, i * 6 + j] = (
                                -GRAVITY
                                * (-1.0) ** sum(ea)
                                / (factorial_of(ea) * factorial_of(eg))
                                * inverse_derivative(e, r)
                            )
    out["w_high"], out["w_low"] = split_np(w.reshape(7 * NG, NA * WIN))
    sel = np.zeros((4, WIN, 40))
    sign = np.zeros((4, 384))
    for c in range(4):
        cx, cy = c >> 1, c & 1
        for i in range(6):
            for j in range(6):
                si, sj = (5 - i if cx else i), (5 - j if cy else j)
                sel[c, i * 6 + j, ((si // 2) * 3 + sj // 2) * 4 + (si % 2) * 2 + sj % 2] = 1.0
        for a, e in enumerate(ALPHA):
            sign[c, a * 16 : a * 16 + 16] = (-1.0) ** (cx * e[0] + cy * e[1])
    out["sel_zero"] = sel.reshape(4 * WIN, 40).astype(ml_dtypes.bfloat16)
    lanes = np.zeros((16, 384), np.float32)
    lanes[0:4] = sign
    for a, e in enumerate(ALPHA):
        for r in range(16):
            lane = a * 16 + r
            level = 1 if r < 8 else 2 if r < 12 else 3
            lanes[4 + level, lane] = e[0] % 2
            lanes[8 + level, lane] = e[1] % 2
    out["lane_odd"] = lanes
    up = np.zeros((384, 384))
    for t, et in enumerate(ALPHA):
        for s, es in enumerate(ALPHA):
            if all(es[k] <= et[k] for k in range(3)):
                for base, to, count in ((0, 8, 8), (8, 12, 4)):
                    for z in range(count):
                        v = 2.0 ** -sum(et)
                        for k in range(3):
                            d = -0.5 if k < 2 or z % 2 == 0 else 0.5
                            v *= math.comb(et[k], es[k]) * d ** (et[k] - es[k])
                        up[s * 16 + base + z, t * 16 + to + z // 2] = v
    out["up"] = exact_np(up)
    odd = np.zeros((16, 384), np.float32)
    for a, e in enumerate(ALPHA):
        odd[0, a * 16 : a * 16 + 16] = e[0] % 2
        odd[1, a * 16 : a * 16 + 16] = e[1] % 2
    out["alpha_odd"] = odd
    agg = np.zeros((32, 128))
    for x in range(GX):
        for y in range(GY):
            agg[(x // 2) * 4 + y // 2, (y % 2) * 64 + x * 4 + y // 2] = 1.0
    out["agg"] = agg.astype(ml_dtypes.bfloat16)
    mask = np.zeros((8, 128), np.float32)
    info = np.zeros((16, 128), np.float32)
    expand = np.zeros((128, 128), np.float32)
    for lane in range(96):
        g, r = lane // 16, lane % 16
        if g < 4:
            n, z, level = 16, r, 0
        elif r < 8:
            n, z, level = 8, r, 1
        elif r < 12:
            n, z, level = 4, r - 8, 2
        elif r < 14:
            n, z, level = 2, r - 12, 3
        else:
            continue
        for k in range(7):
            o = k - 3
            ok = 0 <= z + o < n and abs((z + o) // 2 - z // 2) <= 1
            if g == 4:
                ok = ok and abs(o) > 1
            if g == 5:
                ok = ok and abs(o) <= 1
            mask[k, lane] = float(ok)
        if g < 5:
            info[0, lane] = 2.0**-level
            info[1, lane] = float(g >> 1) if level == 0 else 0.0
            info[2, lane] = float(g & 1) if level == 0 else 0.0
            info[2 + 2 * level, lane] = 1.0 if level else info[2, lane]
            info[9, lane] = float(z % 2)
            if level == 0:
                expand[64 + z // 2, lane] = 1.0
            elif level == 1:
                expand[64 + 8 + z // 2, lane] = 1.0
            elif level == 2:
                expand[64 + 12 + z // 2, lane] = 1.0
    out["mask"] = mask
    out["info"] = info
    out["expand"] = exact_np(expand)
    gamma_odd = np.zeros((3 * NG, 128), np.float32)
    down = np.zeros((NG, NG))
    for g, eg in enumerate(ALPHA):
        for k in range(3):
            gamma_odd[k * NG + g] = eg[k] % 2
        for b, eb in enumerate(ALPHA):
            if all(eb[k] >= eg[k] for k in range(3)):
                v = 2.0 ** -sum(eg)
                for k in range(3):
                    n = eb[k] - eg[k]
                    v *= (-0.25) ** n * math.comb(eb[k], eg[k])
                down[g, b] = v
    out["gamma_odd"] = gamma_odd
    out["down"] = exact_np(down)
    h = (np.arange(SUB) + 0.5) / SUB - 0.5
    spread = np.zeros((16, 384))
    for k in range(3):
        for z in range(128):
            spread[z // 8, k * 128 + z] = h[z % 8] ** k
    out["spread"] = exact_np(spread)
    poly = np.zeros((3, 8, 8, 3, NG))
    for i in range(3):
        for g, e in enumerate(ALPHA):
            if e[i] > 0:
                low = list(e)
                low[i] -= 1
                poly[i, :, :, low[2], g] = (
                    -e[i] * h[:, None] ** low[0] * h[None, :] ** low[1]
                )
    out["poly"] = exact_np(poly.reshape(192, 72))
    cells = np.arange(16)
    near = h[cells % 8]
    far = ((cells + 0.5) / 8 - 1.0) / 2
    left = np.zeros((2, len(PAIRS), 8, 16, 16))
    for q, (px, py) in enumerate(PAIRS):
        for c in range(4):
            block = ((cells // 8 == c >> 1)[:, None] & (cells // 8 == (c & 1))[None, :]).astype(float)
            left[0, q, c] = block * near[:, None] ** px * near[None, :] ** py
            left[1, q, c] = block * far[:, None] ** px * far[None, :] ** py
    out["left"] = left.reshape(160, 256).astype(np.float32)
    right = np.zeros((128, 128))
    flag = np.zeros((128, 128))
    for z in range(128):
        s = z // 8
        f = ((z % 16 + 0.5) / 8 - 1.0) / 2
        for pz in range(4):
            right[z, pz * 16 + s] = h[z % 8] ** pz / SUB**3
            right[z, 64 + (s % 2) * 32 + pz * 8 + s // 2] = f**pz / SUB**3
    for s in range(16):
        for pz in range(4):
            flag[s, pz * 16 + s] = 1.0
            flag[s, 64 + (s % 2) * 32 + pz * 8 + s // 2] = 1.0
    out["right"] = right.astype(np.float32)
    out["flag"] = flag.astype(ml_dtypes.bfloat16)
    return out


def split(x):
    high = x.astype(BF16)
    return high, (x - high.astype(F32)).astype(BF16)


def split_rows(x):
    high = x.astype(BF16).astype(F32)
    return jnp.concatenate([high, x - high], 0).astype(BF16)


def mxu(a, b):
    return jnp.dot(a, b, preferred_element_type=F32)


def exact(a, b):
    return jnp.dot(a, b, precision=HIGHEST, preferred_element_type=F32)


def lane_ids(shape):
    return lax.broadcasted_iota(jnp.int32, shape, len(shape) - 1)


def row_ids(shape):
    return lax.broadcasted_iota(jnp.int32, shape, len(shape) - 2)


def power(s):
    return jnp.exp2(GAMMA * jnp.log2(s))


def root(x):
    return x * lax.rsqrt(x)


PLACES = ((0, 1), (1, 3), (4, 1), (5, 1), (6, 9))


def position():
    return lax.axis_index("mx"), lax.axis_index("my")


def load_all(pairs, sems):
    copies = [pltpu.make_async_copy(source, target, sems.at[k]) for k, (source, target) in enumerate(pairs)]
    for copy in copies:
        copy.start()
    return copies


def fields_into(refs, target, source=slice(0, ROWS), rows=None):
    place = slice(0, source.stop - source.start) if rows is None else rows
    return [
        (ref.at[:, source], target.at[start : start + count, place]) for ref, (start, count) in zip(refs, PLACES)
    ]


def prepare_kernel(den, mom, ene, ent, tra, flags, left, right, flag, pay_h, u, xa, xb, ya, yb, *scratch):
    pos = position()
    pay, sides, fl, flv, leftv, rightv, flagv, sems = scratch
    small = load_all(zip((flags, left, right, flag), (flv, leftv, rightv, flagv)), sems.at[7:11])
    loads = load_all(fields_into((den, mom, ene, ent, tra), u), sems.at[0:5])
    even_x, even_y = pos[0] % 2 == 0, pos[1] % 2 == 0
    for copy in loads:
        copy.wait()
    row_a, row_b = jnp.where(even_x, 208, 0), jnp.where(even_x, 0, 208)
    slabs = load_all(
        [(u.at[:, pl.ds(pl.multiple_of(r, 8), 48)], slab) for r, slab in ((row_a, xa), (row_b, xb))], sems.at[5:7]
    )
    for f in range(NF):
        for k in range(3):
            for s in range(2):
                at = slice(k * 16 + s * 8, k * 16 + s * 8 + 8)
                sides[0, f, at] = u[f, pl.ds(s * 128 + k, 8, stride=16)]
                sides[1, f, at] = u[f, pl.ds(s * 128 + 13 + k, 8, stride=16)]
    side_a, side_b = jnp.where(even_y, 1, 0), jnp.where(even_y, 0, 1)
    slabs += load_all([(sides.at[side_a], ya), (sides.at[side_b], yb)], sems.at[11:13])
    for copy in small:
        copy.wait()
    fl[...] = jnp.zeros((8, 128), F32)
    fl[0:2, 0:16] = flv[0].astype(F32)
    fl[2:4, 0:16] = flv[1].astype(F32)
    tile = mxu(fl[...].astype(BF16), flagv[...])
    rho = u[0]
    sums = exact(leftv[...], exact(rho, rightv[...]))
    inverse = 1.0 / rho
    fast = jnp.maximum(jnp.maximum(jnp.abs(u[1]), jnp.abs(u[2])), jnp.abs(u[3]))
    sound = root(GAMMA * (GAMMA - 1.0) * power(u[5]) * inverse)
    fastest = jnp.max(fast * inverse + sound)
    lane = lane_ids((8, 128))
    row = row_ids((8, 128))
    tiles = [jnp.zeros((8, 128), F32) for _ in range(3)]
    zero, one = {}, {}
    for q, pair in enumerate(PAIRS):
        zero[pair] = sums[q * 8 : q * 8 + 8] * tile
        v = jnp.sum(sums[80 + q * 8 : 88 + q * 8] * tile, axis=0, keepdims=True)
        v = jnp.broadcast_to(v, (8, 128))
        one[pair] = v + pltpu.roll(v, 96, 1)
    for a, e in enumerate(ALPHA):
        c, to = a // 8, (a % 8) * 16
        low = pltpu.roll(zero[e[0], e[1]], (to - e[2] * 16) % 128, 1)
        top = pltpu.roll(one[e[0], e[1]], (to - 64 - e[2] * 8) % 128, 1)
        here = (lane >= to) & (lane < to + 16)
        tiles[c] = jnp.where(here & (row < 4), low, tiles[c])
        tiles[c] = jnp.where(here & (row == 4) & (lane < to + 8), top, tiles[c])
    tiles[2] = jnp.where((row == 4) & (lane >= 64) & (lane < 72), fastest, tiles[2])
    for c in range(3):
        pay[c * 8 : c * 8 + 8] = tiles[c]
    slabs += load_all([(pay, pay_h.at[y]) for y in range(GY)], sems.at[13 : 13 + GY])
    for copy in slabs:
        copy.wait()


def relay_kernel(column, *rest):
    out_h, out, sems = rest[-3:]
    y = position()[1]
    even = [column[pl.ds(c * 8 + 4, 4, stride=48)] for c in range(3)]
    odd = [column[pl.ds(c * 8 + 28, 4, stride=48)] for c in range(3)]
    near = []
    for dy in range(3):
        here = jnp.clip(y + dy - 1, 0, GY - 1)
        inside = here == y + dy - 1
        for c in range(3):
            tile = column[pl.ds(pl.multiple_of(here * 24 + c * 8, 8), 8)]
            near.append(jnp.where(inside, tile, 0.0))
    for c in range(3):
        out[c * 4 : c * 4 + 4] = even[c] + pltpu.roll(odd[c], 8, 1)
    for n, tile in enumerate(near):
        out[12 + n * 4 : 16 + n * 4] = tile[0:4]
    for copy in load_all([(out, out_h.at[x]) for x in range(GX)], sems):
        copy.wait()


def states(ol, il, l, r, ir, orr):
    face = (37.0 / 60.0) * (l + r) - (8.0 / 60.0) * (il + ir) + (1.0 / 60.0) * (ol + orr)
    low, high = jnp.minimum(l, r), jnp.maximum(l, r)
    left = jnp.minimum(jnp.maximum(face, jnp.minimum(il, low)), jnp.maximum(il, high))
    right = jnp.minimum(jnp.maximum(face, jnp.minimum(low, ir)), jnp.maximum(high, ir))
    return left, right


def fluxes(load, d, store):
    rl, rr = load(0)
    ml, mr = load(1 + d)
    sl, sr = load(5)
    il, ir = 1.0 / rl, 1.0 / rr
    vl, vr = ml * il, mr * ir
    gl, gr = power(sl), power(sr)
    cl, cr = root(GAMMA * (GAMMA - 1.0) * gl * il), root(GAMMA * (GAMMA - 1.0) * gr * ir)
    a = 4.0 * jnp.maximum(jnp.abs(vl) + cl, jnp.abs(vr) + cr)
    wl, wr = 4.0 * vl, 4.0 * vr
    kl, kr = wl + a, wr - a
    got = {0: (rl, rr), 1 + d: (ml, mr), 5: (sl, sr)}
    for f in range(NF):
        left, right = got[f] if f in got else load(f)
        flux = left * kl + right * kr
        if f == 1 + d:
            flux = flux + (4.0 * (GAMMA - 1.0)) * (gl + gr)
        if f == 4:
            flux = flux + (GAMMA - 1.0) * (gl * wl + gr * wr)
        store(f, flux)


def flux_z_kernel(u, out_h, uz, fz, out, sems):
    for f in range(NF):
        for half in range(2):
            cells = u[f, half * 128 : half * 128 + 128].T
            uz[2 * f + half, 8:136] = cells
            uz[2 * f + half, 0:8] = jnp.broadcast_to(cells[0:1], (8, 128))
            uz[2 * f + half, 136:144] = jnp.broadcast_to(cells[127:128], (8, 128))

    def faces_z(i, carry):
        for half in range(2):

            def load(f):
                return states(*[uz[2 * f + half, pl.ds(i * 8 + 5 + k, 8)] for k in range(6)])

            def store(f, flux):
                fz[2 * f + half, pl.ds(pl.multiple_of(i * 8, 8), 8)] = flux

            fluxes(load, 2, store)
        return carry

    lax.fori_loop(0, 16, faces_z, 0)
    for half in range(2):

        def load_top(f, half=half):
            rows = [uz[2 * f + half, 133 + k : 141 + k] for k in range(4)]
            return states(*rows, rows[3], rows[3])

        def store_top(f, flux, half=half):
            fz[2 * f + half, 128:136] = flux

        fluxes(load_top, 2, store_top)

    stores = []
    for part in range(5):
        for f in range(part * 3, part * 3 + 3):
            for half in range(2):
                out[f, half * 128 : half * 128 + 128] = (fz[2 * f + half, 0:128] - fz[2 * f + half, 1:129]).T
        some = slice(part * 3, part * 3 + 3)
        stores += load_all([(out.at[some], out_h.at[some])], sems.at[part : part + 1])
    for copy in stores:
        copy.wait()


def flux_xy_kernel(den, mom, ene, ent, tra, along_z_h, xa, xb, ya_h, yb_h, *args):
    pos = position()
    count = len(TREE_CONSTANTS)
    out_h = args[count]
    tables = args[count + 1 : 2 * count + 1]
    ux, fx, uy, fy, ya, yb, along_z, out, sems = args[2 * count + 1 :]
    even_x, even_y = pos[0] % 2 == 0, pos[1] % 2 == 0
    row_a, row_b = [pl.ds(pl.multiple_of(jnp.where(even_x, p, q), 8), 48) for p, q in ((304, 0), (0, 304))]
    loads = load_all(
        fields_into((den, mom, ene, ent, tra), ux, rows=slice(48, 304))
        + [(xa, ux.at[:, row_a]), (xb, ux.at[:, row_b]), (ya_h, ya), (yb_h, yb), (along_z_h, along_z)],
        sems.at[0:10],
    )
    late = load_all(list(zip(args[:count], tables)), sems.at[10 : 10 + count])
    for copy in loads[:7]:
        copy.wait()

    def repeat(source, target):
        for f in range(NF):
            cells = ux[f, source : source + 16]
            for k in range(3):
                ux[f, target + k * 16 : target + k * 16 + 16] = cells

    pl.when(pos[0] == 0)(lambda: repeat(48, 0))
    pl.when(pos[0] == GX - 1)(lambda: repeat(288, 304))

    def faces_x(i, carry):
        for s in range(2):

            def load(f):
                return states(*[ux[f, pl.ds(pl.multiple_of((i + k) * 16 + s * 8, 8), 8)] for k in range(6)])

            def store(f, flux):
                fx[f, pl.ds(pl.multiple_of(i * 16 + s * 8, 8), 8)] = flux

            fluxes(load, 0, store)
        return carry

    lax.fori_loop(0, 17, faces_x, 0)

    def spread(x, carry):
        for f in range(NF):
            uy[f, pl.ds(pl.multiple_of(x * 32 + 8, 8), 16)] = ux[f, pl.ds(pl.multiple_of(48 + x * 16, 8), 16)]
        return carry

    lax.fori_loop(0, 16, spread, 0)
    for copy in loads[7:9]:
        copy.wait()
    first, last = pos[1] == 0, pos[1] == GY - 1
    for f in range(NF):
        for s in range(2):
            low, high = ux[f, pl.ds(48 + s * 128, 8, stride=16)], ux[f, pl.ds(63 + s * 128, 8, stride=16)]
            for k in range(3):
                at = slice(k * 16 + s * 8, k * 16 + s * 8 + 8)
                uy[f, pl.ds(s * 256 + 5 + k, 8, stride=32)] = jnp.where(first, low, jnp.where(even_y, yb[f, at], ya[f, at]))
                uy[f, pl.ds(s * 256 + 24 + k, 8, stride=32)] = jnp.where(last, high, jnp.where(even_y, ya[f, at], yb[f, at]))

    for s in range(2):

        def load_end(f, s=s):
            return states(*[uy[f, pl.ds(s * 256 + 21 + k, 8, stride=32)] for k in range(6)])

        def store_end(f, flux, s=s):
            fy[f, pl.ds(s * 192 + 16, 8, stride=24)] = flux

        fluxes(load_end, 1, store_end)
    def faces_y(x):
        for s in range(2):

            def load(f):
                return states(*[uy[f, pl.ds(x * 32 + s * 8 + 5 + k, 8)] for k in range(6)])

            def store(f, flux):
                fy[f, pl.ds(pl.multiple_of(x * 24 + s * 8, 8), 8)] = flux

            fluxes(load, 1, store)

    loads[9].wait()

    def gather(x):
        for f in range(NF):
            for s in range(2):
                at = pl.multiple_of(x * 16 + s * 8, 8)
                rows = pl.ds(at, 8)
                change = along_z[f, rows] + (fx[f, rows] - fx[f, pl.ds(pl.multiple_of(at + 16, 8), 8)])
                y = pl.multiple_of(x * 24 + s * 8, 8)
                out[f, rows] = change + (fy[f, pl.ds(y, 8)] - fy[f, pl.ds(y + 1, 8)])

    def both(x, carry):
        gather(x - 1)
        faces_y(x)
        return carry

    faces_y(0)
    for part in range(4):
        lax.fori_loop(part * 4 + 1, min(part * 4 + 5, 16), both, 0)
        if part == 3:
            gather(15)
        rows = slice(part * 64, part * 64 + 64)
        late += load_all([(out.at[:, rows], out_h.at[:, rows])], sems.at[10 + count + part : 11 + count + part])
    for copy in late:
        copy.wait()


TREE_CONSTANTS = (
    "w_high", "w_low", "sel_zero", "lane_odd", "up", "alpha_odd", "agg", "mask", "info", "expand", "gamma_odd", "down",
    "spread", "poly",
)


def tree_kernel(far, den, mom, ene, ent, tra, change_h, *args):
    count = len(TREE_CONSTANTS)
    w_high, w_low, sel_zero, lane_odd, up, alpha_odd, agg, mask, info, expand, gamma_odd, down, spread, poly = args[:count]
    section, accel, rhs, field, result, force, u, change, sems = args[count:]
    late = []
    for q in range(4):
        rows = slice(q * 64, q * 64 + 64)
        pairs = fields_into((den, mom, ene, ent, tra), u, rows, rows) + [(change_h.at[:, rows], change.at[:, rows])]
        late.append(load_all(pairs, sems.at[8 + 6 * q : 14 + 6 * q]))
    px, py = position()
    blocks = []
    for dx in range(3):
        here = jnp.clip(px + dx - 1, 0, GX - 1)
        inside = here == px + dx - 1
        blocks.append([jnp.where(inside, far[here, 12 + n * 4 : 16 + n * 4], 0.0) for n in range(9)])
    gap = jnp.zeros((4, 128), F32)
    around = jnp.concatenate(
        [jnp.concatenate([blocks[dx][dy * 3 + c] for dx in range(3) for dy in range(3)] + [gap], 0) for c in range(3)], 1
    )
    zero = mxu(sel_zero[...], jnp.concatenate(split(around), 1))
    zero = zero[:, :384] + zero[:, 384:]
    arrays = [zero[c * WIN : c * WIN + WIN] * lane_odd[c : c + 1] for c in range(4)]
    packed = [jnp.concatenate([far[x, c * 4 : c * 4 + 4] for x in range(GX)], 0) for c in range(3)]
    lower = lane_ids((128, 128)) % 16 < 8
    gathered = jnp.concatenate(
        [jnp.where(lower, jnp.concatenate([rows, pltpu.roll(rows, 120, 1)], 0), 0.0) for rows in packed], 1
    )
    speeds = gathered[:, 256:]
    fastest = jnp.max(jnp.where(lane_ids((128, 128)) >= 64, speeds, 0.0))

    def lifted(x, x_odd, y_odd):
        sign = (1.0 - 2.0 * x_odd * alpha_odd[0:1]) * (1.0 - 2.0 * y_odd * alpha_odd[1:2])
        n = x.shape[0]
        z = mxu(jnp.concatenate(split(x * sign), 0), up[...])
        return (z[:n] + z[n:]) * sign

    def picked(matrix, x):
        y = mxu(matrix, jnp.concatenate(split(x), 1))
        return y[:, :384] + y[:, 384:]

    dev = lax.broadcasted_iota(jnp.int32, (128, 1), 0)
    raised = lifted(gathered, ((dev // 4) % 2).astype(F32), (dev // 64).astype(F32))
    two = picked(agg[...], raised)
    cell = lax.broadcasted_iota(jnp.int32, (32, 1), 0)
    raised_two = lifted(two, ((cell // 4) % 2).astype(F32), (cell % 2).astype(F32))

    def window(level, columns, shift):
        tx, ty = px >> (level - 1), py >> (level - 1)
        row = lax.broadcasted_iota(jnp.int32, (WIN, columns), 0)
        col = lax.broadcasted_iota(jnp.int32, (WIN, columns), 1)
        i, j = row // 6, row % 6
        i = jnp.where((tx & 1) == 1, 5 - i, i) + 2 * ((tx >> 1) - 1)
        j = jnp.where((ty & 1) == 1, 5 - j, j) + 2 * ((ty >> 1) - 1)
        if columns == 128:
            sx, sy = (col % 64) // 4, 2 * (col % 4) + col // 64
        else:
            sx, sy = col // 4, col % 4
        sx, sy = sx >> shift, sy >> shift
        return ((row < 36) & (sx == i) & (sy == j)).astype(F32).astype(BF16)

    levels = (
        picked(window(1, 128, 0), gathered)
        + picked(window(2, 128, 1), raised)
        + picked(window(3, 32, 1), raised_two)
    )
    sign = jnp.ones((1, 384), F32)
    for level in (1, 2, 3):
        bx = ((px >> (level - 1)) & 1).astype(F32)
        by = ((py >> (level - 1)) & 1).astype(F32)
        sign = sign * (1.0 - 2.0 * bx * lane_odd[4 + level : 5 + level])
        sign = sign * (1.0 - 2.0 * by * lane_odd[8 + level : 9 + level])
    levels = levels * sign
    wrow = lax.broadcasted_iota(jnp.int32, (WIN, 384), 0)
    wi, wj = wrow // 6, wrow % 6
    touching = (wi >= 1) & (wi <= 3) & (wj >= 1) & (wj <= 3)
    arrays += [levels, jnp.where(touching, 0.0, levels)]
    lane = lane_ids((WIN, 128)) // 16
    for a in range(NA):
        c, off = a // 8, (a % 8) * 16
        block = jnp.zeros((WIN, 128), F32)
        for g, array in enumerate(arrays):
            block = jnp.where(lane == g, pltpu.roll(array[:, c * 128 : c * 128 + 128], (16 * g - off) % 128, 1), block)
        rhs[a * WIN : a * WIN + WIN] = block
    high, low = split(rhs[...])
    y = mxu(w_high[...], jnp.concatenate([high, low], 1))
    y = y[:, :128] + y[:, 128:] + mxu(w_low[...], high)
    base = jnp.zeros((NG, 128), F32)
    for k in range(7):
        base = base + mask[k : k + 1] * pltpu.roll(y[k * NG : k * NG + NG], (3 - k) % 128, 1)
    lanes = lane_ids((NG, 128)) // 16
    base = base + jnp.where(lanes == 4, pltpu.roll(base, 112, 1), 0.0)
    bx, by = info[1:2], info[2:3]
    for level in (1, 2, 3):
        bx = bx + info[2 + 2 * level : 3 + 2 * level] * ((px >> (level - 1)) & 1).astype(F32)
        by = by + info[2 + 2 * level : 3 + 2 * level] * ((py >> (level - 1)) & 1).astype(F32)
    flip = (1.0 - 2.0 * bx * gamma_odd[0:NG]) * (1.0 - 2.0 * by * gamma_odd[NG : 2 * NG])
    base = base * info[0:1] * flip
    flip = flip * (1.0 - 2.0 * info[9:10] * gamma_odd[2 * NG :])
    total = base
    for _ in range(3):
        parents = mxu(split_rows(total), expand[...])
        pieces = jnp.concatenate(split(flip * (parents[:NG] + parents[NG:])), 1)
        carried = mxu(down[...], pieces)
        total = base + flip * (carried[:, :128] + carried[:, 128:])
    rows = jnp.concatenate([pltpu.roll(total, (128 - 16 * c) % 128, 1) for c in range(4)], 0)[:, :16]
    spreads = mxu(split_rows(rows), spread[...])
    spreads = spreads[: 4 * NG] + spreads[4 * NG :]
    terms = jnp.concatenate(
        [
            jnp.concatenate([spreads[c * NG : c * NG + NG, k * 128 : k * 128 + 128] for k in range(3)], 0)
            for c in range(4)
        ],
        1,
    )
    values = mxu(poly[...], jnp.concatenate(split(terms), 1))
    field[...] = values[:, :512] + values[:, 512:]
    step = jnp.full((8, 128), COURANT / SUB, F32) / fastest
    stores = []
    for part in range(4):
        half = part // 2
        for copy in late[part]:
            copy.wait()

        def finish(x, carry, half=half):
            for s in range(2):
                c = half * 2 + s
                at = pl.multiple_of(half * 128 + x * 16 + s * 8, 8)
                rows = pl.ds(at, 8)
                acc = [field[pl.ds(pl.multiple_of(i * 64 + x * 8, 8), 8), c * 128 : c * 128 + 128] for i in range(3)]
                old = [u[f, rows] for f in range(NF)]
                for i in range(3):
                    force[i, rows] = acc[i]
                for f in range(NF):
                    slope = change[f, rows]
                    if 1 <= f <= 3:
                        slope = slope + old[0] * acc[f - 1]
                    if f == 4:
                        slope = slope + (old[1] * acc[0] + old[2] * acc[1] + old[3] * acc[2])
                    result[f, rows] = old[f] + step * slope
            return carry

        lax.fori_loop((part % 2) * 4, (part % 2) * 4 + 4, finish, 0)
        rows = slice(part * 64, part * 64 + 64)
        stores += load_all(
            [(result.at[:, rows], section.at[:, rows]), (force.at[:, rows], accel.at[:, rows])],
            sems.at[2 * part : 2 * part + 2],
        )
    for copy in stores:
        copy.wait()


ANY = pl.BlockSpec(memory_space=pl.ANY)
HBM = pl.BlockSpec(memory_space=pltpu.HBM)
VMEM = pl.BlockSpec(memory_space=pltpu.VMEM)


def call(kernel, name, ins, outs, scratch, cost, aliases=None):
    outs = [(o[0], o[1], o[2] if len(o) > 2 else F32) for o in outs]
    return pl.pallas_call(
        kernel,
        out_shape=[pltpu.HBM(s, t) if spec is HBM else jax.ShapeDtypeStruct(s, t) for s, spec, t in outs],
        in_specs=[spec for _, spec in ins],
        out_specs=[spec for _, spec, _ in outs],
        scratch_shapes=scratch,
        input_output_aliases=aliases or {},
        cost_estimate=pl.CostEstimate(flops=cost[0], bytes_accessed=cost[1], transcendentals=cost[2]),
        name=name,
        compiler_params=pltpu.CompilerParams(vmem_limit_bytes=32 << 20),
    )(*[in_hbm(x) if spec is HBM else x for x, spec in ins])


def in_hbm(x):
    return pltpu.with_memory_space_constraint(x, pltpu.HBM)


def scratch_like(x):
    return pltpu.VMEM(x.shape, x.dtype)


def shards(density, momentum, energy, entropy, tracers, leaf_flags):
    con = {k: jnp.asarray(v) for k, v in constants().items()}
    fields = [(x.reshape(-1, ROWS, 128), HBM) for x in (density, momentum, energy, entropy, tracers)]
    first = [con[n] for n in ("left", "right", "flag")]
    whole, slab = (NF, ROWS, 128), (NF, 48, 128)
    block, halo = pltpu.VMEM(whole, F32), pltpu.VMEM(slab, F32)
    pay, u, xa, xb, ya, yb = call(
        prepare_kernel,
        "prepare",
        fields + [(leaf_flags, HBM)] + [(x, HBM) for x in first],
        [((GY, 24, 128), HBM), (whole, VMEM)] + [(slab, HBM)] * 4,
        [pltpu.VMEM((24, 128), F32), pltpu.VMEM((2, *slab), F32), pltpu.VMEM((8, 128), F32), scratch_like(leaf_flags)]
        + [scratch_like(x) for x in first]
        + [pltpu.SemaphoreType.DMA((13 + GY,))],
        (10**7, 4 * 10**6, 10**5),
    )

    def pairs(count, start):
        lows = range(start, count, 2)
        return [(i, (i + 1) % count) for i in lows] + [((i + 1) % count, i) for i in lows]

    column = lax.all_to_all(pay, "my", 0, 0)
    halos = [
        (lax.ppermute(slab, axis, pairs(count, start)), ANY)
        for slab, axis, count, start in ((xa, "mx", GX, 0), (xb, "mx", GX, 1), (ya, "my", GY, 0), (yb, "my", GY, 1))
    ]
    (along_z,) = call(
        flux_z_kernel,
        "flux_z",
        [(u, VMEM)],
        [(whole, HBM)],
        [pltpu.VMEM((2 * NF, 144, 128), F32), pltpu.VMEM((2 * NF, 136, 128), F32), block, pltpu.SemaphoreType.DMA((5,))],
        (2 * 10**7, 4 * 10**6, 3 * 10**5),
    )
    (chunks,) = call(
        relay_kernel,
        "relay",
        [(column.reshape(GY * 24, 128), VMEM), (along_z, HBM)] + halos,
        [((GX, 48, 128), HBM)],
        [pltpu.VMEM((48, 128), F32), pltpu.SemaphoreType.DMA((GX,))],
        (10**4, 10**6, 0),
    )
    far = lax.all_to_all(chunks, "mx", 0, 0)
    second = [con[n] for n in TREE_CONSTANTS]
    tend, *tables = call(
        flux_xy_kernel,
        "flux_xy",
        fields + [(along_z, HBM)] + halos + [(x, HBM) for x in second],
        [(whole, HBM)] + [(x.shape, VMEM, x.dtype) for x in second],
        [
            pltpu.VMEM((NF, 352, 128), F32),
            pltpu.VMEM((NF, 272, 128), F32),
            pltpu.VMEM((NF, 512, 128), F32),
            pltpu.VMEM((NF, 384, 128), F32),
            halo,
            halo,
            block,
            block,
            pltpu.SemaphoreType.DMA((14 + len(second),)),
        ],
        (4 * 10**7, 6 * 10**6, 6 * 10**5),
    )
    section, accel = call(
        tree_kernel,
        "tree",
        [(far, VMEM)] + fields + [(tend, HBM)] + [(x, VMEM) for x in tables],
        [(whole, HBM), ((3, ROWS, 128), HBM)],
        [
            pltpu.VMEM((NA * WIN, 128), F32),
            pltpu.VMEM((192, 512), F32),
            block,
            pltpu.VMEM((3, ROWS, 128), F32),
            block,
            block,
            pltpu.SemaphoreType.DMA((32,)),
        ],
        (10**8, 8 * 10**6, 0),
    )
    return section.reshape(NF, 16, 16, 128), accel.reshape(3, 16, 16, 128)


def solution(mesh):
    placed = (
        P("mx", "my", None),
        P(None, "mx", "my", None),
        P("mx", "my", None),
        P("mx", "my", None),
        P(None, "mx", "my", None),
        P("mx", "my", None),
    )
    return jax.shard_map(
        shards,
        mesh=mesh,
        in_specs=placed,
        out_specs=(P(None, "mx", "my", None), P(None, "mx", "my", None)),
        check_vma=False,
    )
```

```python
import functools
import math

import jax
import jax.numpy as jnp
import ml_dtypes
import numpy as np
from jax import lax
from jax.experimental import pallas as pl
from jax.experimental.pallas import tpu as pltpu
from jax.sharding import PartitionSpec as P

F32 = jnp.float32
BF16 = jnp.bfloat16
HIGHEST = lax.Precision.HIGHEST
GRAVITY = 0.02
GAMMA = 5.0 / 3.0
COURANT = 0.3
SUB = 8
NF = 15
GX, GY = 16, 8
ROWS = 256

ALPHA = [
    (px, py, d - px - py)
    for d in range(4)
    for px in range(d, -1, -1)
    for py in range(d - px, -1, -1)
]
NA = len(ALPHA)
NG = 24
WIN = 40
PAIRS = [(px, py) for px in range(4) for py in range(4 - px)]


def factorial_of(e):
    return math.factorial(e[0]) * math.factorial(e[1]) * math.factorial(e[2])


def inverse_derivative(exponent, r):
    axes = [0] * exponent[0] + [1] * exponent[1] + [2] * exponent[2]
    norm = math.sqrt(r[0] ** 2 + r[1] ** 2 + r[2] ** 2)
    if norm == 0.0:
        return 0.0
    if not axes:
        return 1.0 / norm
    if len(axes) == 1:
        return -r[axes[0]] / norm**3
    if len(axes) == 2:
        a, b = axes
        return 3.0 * r[a] * r[b] / norm**5 - float(a == b) / norm**3
    a, b, c = axes
    crossed = float(a == b) * r[c] + float(a == c) * r[b] + float(b == c) * r[a]
    return -15.0 * r[a] * r[b] * r[c] / norm**7 + 3.0 * crossed / norm**5


def split_np(x):
    high = x.astype(np.float32).astype(ml_dtypes.bfloat16)
    low = (x - high.astype(np.float64)).astype(ml_dtypes.bfloat16)
    return high, low


def exact_np(x):
    y = x.astype(ml_dtypes.bfloat16)
    assert np.array_equal(x, y.astype(np.float64))
    return y


@functools.cache
def constants():
    out = {}
    w = np.zeros((7, NG, NA, WIN))
    for z in range(7):
        for i in range(6):
            for j in range(6):
                r = (-(i - 2.0), -(j - 2.0), -(z - 3.0))
                for g, eg in enumerate(ALPHA):
                    for a, ea in enumerate(ALPHA):
                        if sum(eg) + sum(ea) <= 3:
                            e = tuple(eg[k] + ea[k] for k in range(3))
                            w[z, g, a, i * 6 + j] = (
                                -GRAVITY
                                * (-1.0) ** sum(ea)
                                / (factorial_of(ea) * factorial_of(eg))
                                * inverse_derivative(e, r)
                            )
    out["w_high"], out["w_low"] = split_np(w.reshape(7 * NG, NA * WIN))
    sel = np.zeros((4, WIN, 40))
    sign = np.zeros((4, 384))
    for c in range(4):
        cx, cy = c >> 1, c & 1
        for i in range(6):
            for j in range(6):
                si, sj = (5 - i if cx else i), (5 - j if cy else j)
                sel[c, i * 6 + j, ((si // 2) * 3 + sj // 2) * 4 + (si % 2) * 2 + sj % 2] = 1.0
        for a, e in enumerate(ALPHA):
            sign[c, a * 16 : a * 16 + 16] = (-1.0) ** (cx * e[0] + cy * e[1])
    out["sel_zero"] = sel.reshape(4 * WIN, 40).astype(ml_dtypes.bfloat16)
    lanes = np.zeros((16, 384), np.float32)
    lanes[0:4] = sign
    for a, e in enumerate(ALPHA):
        for r in range(16):
            lane = a * 16 + r
            level = 1 if r < 8 else 2 if r < 12 else 3
            lanes[4 + level, lane] = e[0] % 2
            lanes[8 + level, lane] = e[1] % 2
    out["lane_odd"] = lanes
    up = np.zeros((384, 384))
    for t, et in enumerate(ALPHA):
        for s, es in enumerate(ALPHA):
            if all(es[k] <= et[k] for k in range(3)):
                for base, to, count in ((0, 8, 8), (8, 12, 4)):
                    for z in range(count):
                        v = 2.0 ** -sum(et)
                        for k in range(3):
                            d = -0.5 if k < 2 or z % 2 == 0 else 0.5
                            v *= math.comb(et[k], es[k]) * d ** (et[k] - es[k])
                        up[s * 16 + base + z, t * 16 + to + z // 2] = v
    out["up"] = exact_np(up)
    odd = np.zeros((16, 384), np.float32)
    for a, e in enumerate(ALPHA):
        odd[0, a * 16 : a * 16 + 16] = e[0] % 2
        odd[1, a * 16 : a * 16 + 16] = e[1] % 2
    out["alpha_odd"] = odd
    agg = np.zeros((32, 128))
    for x in range(GX):
        for y in range(GY):
            agg[(x // 2) * 4 + y // 2, (y % 2) * 64 + x * 4 + y // 2] = 1.0
    out["agg"] = agg.astype(ml_dtypes.bfloat16)
    mask = np.zeros((8, 128), np.float32)
    info = np.zeros((16, 128), np.float32)
    expand = np.zeros((128, 128), np.float32)
    for lane in range(96):
        g, r = lane // 16, lane % 16
        if g < 4:
            n, z, level = 16, r, 0
        elif r < 8:
            n, z, level = 8, r, 1
        elif r < 12:
            n, z, level = 4, r - 8, 2
        elif r < 14:
            n, z, level = 2, r - 12, 3
        else:
            continue
        for k in range(7):
            o = k - 3
            ok = 0 <= z + o < n and abs((z + o) // 2 - z // 2) <= 1
            if g == 4:
                ok = ok and abs(o) > 1
            if g == 5:
                ok = ok and abs(o) <= 1
            mask[k, lane] = float(ok)
        if g < 5:
            info[0, lane] = 2.0**-level
            info[1, lane] = float(g >> 1) if level == 0 else 0.0
            info[2, lane] = float(g & 1) if level == 0 else 0.0
            info[2 + 2 * level, lane] = 1.0 if level else info[2, lane]
            info[9, lane] = float(z % 2)
            if level == 0:
                expand[64 + z // 2, lane] = 1.0
            elif level == 1:
                expand[64 + 8 + z // 2, lane] = 1.0
            elif level == 2:
                expand[64 + 12 + z // 2, lane] = 1.0
    out["mask"] = mask
    out["info"] = info
    out["expand"] = exact_np(expand)
    gamma_odd = np.zeros((3 * NG, 128), np.float32)
    down = np.zeros((NG, NG))
    for g, eg in enumerate(ALPHA):
        for k in range(3):
            gamma_odd[k * NG + g] = eg[k] % 2
        for b, eb in enumerate(ALPHA):
            if all(eb[k] >= eg[k] for k in range(3)):
                v = 2.0 ** -sum(eg)
                for k in range(3):
                    n = eb[k] - eg[k]
                    v *= (-0.25) ** n * math.comb(eb[k], eg[k])
                down[g, b] = v
    out["gamma_odd"] = gamma_odd
    out["down"] = exact_np(down)
    h = (np.arange(SUB) + 0.5) / SUB - 0.5
    spread = np.zeros((16, 384))
    for k in range(3):
        for z in range(128):
            spread[z // 8, k * 128 + z] = h[z % 8] ** k
    out["spread"] = exact_np(spread)
    poly = np.zeros((3, 8, 8, 3, NG))
    for i in range(3):
        for g, e in enumerate(ALPHA):
            if e[i] > 0:
                low = list(e)
                low[i] -= 1
                poly[i, :, :, low[2], g] = (
                    -e[i] * h[:, None] ** low[0] * h[None, :] ** low[1]
                )
    out["poly"] = exact_np(poly.reshape(192, 72))
    cells = np.arange(16)
    near = h[cells % 8]
    far = ((cells + 0.5) / 8 - 1.0) / 2
    left = np.zeros((2, len(PAIRS), 8, 16, 16))
    for q, (px, py) in enumerate(PAIRS):
        for c in range(4):
            block = ((cells // 8 == c >> 1)[:, None] & (cells // 8 == (c & 1))[None, :]).astype(float)
            left[0, q, c] = block * near[:, None] ** px * near[None, :] ** py
            left[1, q, c] = block * far[:, None] ** px * far[None, :] ** py
    out["left"] = left.reshape(160, 256).astype(np.float32)
    right = np.zeros((128, 128))
    flag = np.zeros((128, 128))
    for z in range(128):
        s = z // 8
        f = ((z % 16 + 0.5) / 8 - 1.0) / 2
        for pz in range(4):
            right[z, pz * 16 + s] = h[z % 8] ** pz / SUB**3
            right[z, 64 + (s % 2) * 32 + pz * 8 + s // 2] = f**pz / SUB**3
    for s in range(16):
        for pz in range(4):
            flag[s, pz * 16 + s] = 1.0
            flag[s, 64 + (s % 2) * 32 + pz * 8 + s // 2] = 1.0
    out["right"] = right.astype(np.float32)
    out["flag"] = flag.astype(ml_dtypes.bfloat16)
    return out


def split(x):
    high = x.astype(BF16)
    return high, (x - high.astype(F32)).astype(BF16)


def split_rows(x):
    high = x.astype(BF16).astype(F32)
    return jnp.concatenate([high, x - high], 0).astype(BF16)


def mxu(a, b):
    return jnp.dot(a, b, preferred_element_type=F32)


def exact(a, b):
    return jnp.dot(a, b, precision=HIGHEST, preferred_element_type=F32)


def lane_ids(shape):
    return lax.broadcasted_iota(jnp.int32, shape, len(shape) - 1)


def row_ids(shape):
    return lax.broadcasted_iota(jnp.int32, shape, len(shape) - 2)


def power(s):
    return jnp.exp2(GAMMA * jnp.log2(s))


def root(x):
    return x * lax.rsqrt(x)


PLACES = ((0, 1), (1, 3), (4, 1), (5, 1), (6, 9))


def position():
    return lax.axis_index("mx"), lax.axis_index("my")


def load_all(pairs, sems):
    copies = [pltpu.make_async_copy(source, target, sems.at[k]) for k, (source, target) in enumerate(pairs)]
    for copy in copies:
        copy.start()
    return copies


def fields_into(refs, target, source=slice(0, ROWS), rows=None):
    place = slice(0, source.stop - source.start) if rows is None else rows
    return [
        (ref.at[:, source], target.at[start : start + count, place]) for ref, (start, count) in zip(refs, PLACES)
    ]


def prepare_kernel(den, mom, ene, ent, tra, flags, left, right, flag, pay_h, u, xa, xb, ya, yb, *scratch):
    pos = position()
    pay, sides, fl, flv, leftv, rightv, flagv, sems = scratch
    small = load_all(zip((flags, left, right, flag), (flv, leftv, rightv, flagv)), sems.at[7:11])
    loads = load_all(fields_into((den, mom, ene, ent, tra), u), sems.at[0:5])
    even_x, even_y = pos[0] % 2 == 0, pos[1] % 2 == 0
    for copy in loads:
        copy.wait()
    row_a, row_b = jnp.where(even_x, 208, 0), jnp.where(even_x, 0, 208)
    slabs = load_all(
        [(u.at[:, pl.ds(pl.multiple_of(r, 8), 48)], slab) for r, slab in ((row_a, xa), (row_b, xb))], sems.at[5:7]
    )
    for f in range(NF):
        for k in range(3):
            for s in range(2):
                at = slice(k * 16 + s * 8, k * 16 + s * 8 + 8)
                sides[0, f, at] = u[f, pl.ds(s * 128 + k, 8, stride=16)]
                sides[1, f, at] = u[f, pl.ds(s * 128 + 13 + k, 8, stride=16)]
    side_a, side_b = jnp.where(even_y, 1, 0), jnp.where(even_y, 0, 1)
    slabs += load_all([(sides.at[side_a], ya), (sides.at[side_b], yb)], sems.at[11:13])
    for copy in small:
        copy.wait()
    fl[...] = jnp.zeros((8, 128), F32)
    fl[0:2, 0:16] = flv[0].astype(F32)
    fl[2:4, 0:16] = flv[1].astype(F32)
    tile = mxu(fl[...].astype(BF16), flagv[...])
    rho = u[0]
    sums = exact(leftv[...], exact(rho, rightv[...]))
    inverse = 1.0 / rho
    fast = jnp.maximum(jnp.maximum(jnp.abs(u[1]), jnp.abs(u[2])), jnp.abs(u[3]))
    sound = root(GAMMA * (GAMMA - 1.0) * power(u[5]) * inverse)
    fastest = jnp.max(fast * inverse + sound)
    lane = lane_ids((8, 128))
    row = row_ids((8, 128))
    tiles = [jnp.zeros((8, 128), F32) for _ in range(3)]
    zero, one = {}, {}
    for q, pair in enumerate(PAIRS):
        zero[pair] = sums[q * 8 : q * 8 + 8] * tile
        v = jnp.sum(sums[80 + q * 8 : 88 + q * 8] * tile, axis=0, keepdims=True)
        v = jnp.broadcast_to(v, (8, 128))
        one[pair] = v + pltpu.roll(v, 96, 1)
    for a, e in enumerate(ALPHA):
        c, to = a // 8, (a % 8) * 16
        low = pltpu.roll(zero[e[0], e[1]], (to - e[2] * 16) % 128, 1)
        top = pltpu.roll(one[e[0], e[1]], (to - 64 - e[2] * 8) % 128, 1)
        here = (lane >= to) & (lane < to + 16)
        tiles[c] = jnp.where(here & (row < 4), low, tiles[c])
        tiles[c] = jnp.where(here & (row == 4) & (lane < to + 8), top, tiles[c])
    tiles[2] = jnp.where((row == 4) & (lane >= 64) & (lane < 72), fastest, tiles[2])
    pay[8:16] = jnp.zeros((8, 128), F32)
    for c in range(3):
        pay[c * 5 : c * 5 + 5] = tiles[c][0:5]
    slabs += load_all([(pay, pay_h.at[y]) for y in range(GY)], sems.at[13 : 13 + GY])
    for copy in slabs:
        copy.wait()


def relay_kernel(column, *rest):
    out_h, out, sems = rest[-3:]
    y = position()[1]
    even = [column[pl.ds(c * 5 + 4, 4, stride=32)] for c in range(3)]
    odd = [column[pl.ds(c * 5 + 20, 4, stride=32)] for c in range(3)]
    near = []
    for dy in range(3):
        here = jnp.clip(y + dy - 1, 0, GY - 1)
        inside = here == y + dy - 1
        for c in range(3):
            tile = column[pl.ds(here * 16 + c * 5, 4)]
            near.append(jnp.where(inside, tile, 0.0))
    for c in range(3):
        out[c * 4 : c * 4 + 4] = even[c] + pltpu.roll(odd[c], 8, 1)
    for n, tile in enumerate(near):
        out[12 + n * 4 : 16 + n * 4] = tile
    for copy in load_all([(out, out_h.at[x]) for x in range(GX)], sems):
        copy.wait()


def states(ol, il, l, r, ir, orr):
    face = (37.0 / 60.0) * (l + r) - (8.0 / 60.0) * (il + ir) + (1.0 / 60.0) * (ol + orr)
    low, high = jnp.minimum(l, r), jnp.maximum(l, r)
    left = jnp.minimum(jnp.maximum(face, jnp.minimum(il, low)), jnp.maximum(il, high))
    right = jnp.minimum(jnp.maximum(face, jnp.minimum(low, ir)), jnp.maximum(high, ir))
    return left, right


def fluxes(load, d, store):
    rl, rr = load(0)
    ml, mr = load(1 + d)
    sl, sr = load(5)
    il, ir = 1.0 / rl, 1.0 / rr
    vl, vr = ml * il, mr * ir
    gl, gr = power(sl), power(sr)
    cl, cr = root(GAMMA * (GAMMA - 1.0) * gl * il), root(GAMMA * (GAMMA - 1.0) * gr * ir)
    a = 4.0 * jnp.maximum(jnp.abs(vl) + cl, jnp.abs(vr) + cr)
    wl, wr = 4.0 * vl, 4.0 * vr
    kl, kr = wl + a, wr - a
    got = {0: (rl, rr), 1 + d: (ml, mr), 5: (sl, sr)}
    for f in range(NF):
        left, right = got[f] if f in got else load(f)
        flux = left * kl + right * kr
        if f == 1 + d:
            flux = flux + (4.0 * (GAMMA - 1.0)) * (gl + gr)
        if f == 4:
            flux = flux + (GAMMA - 1.0) * (gl * wl + gr * wr)
        store(f, flux)


def flux_z_kernel(u, out_h, uz, fz, out, sems):
    for f in range(NF):
        for half in range(2):
            cells = u[f, half * 128 : half * 128 + 128].T
            uz[2 * f + half, 8:136] = cells
            uz[2 * f + half, 0:8] = jnp.broadcast_to(cells[0:1], (8, 128))
            uz[2 * f + half, 136:144] = jnp.broadcast_to(cells[127:128], (8, 128))

    def faces_z(i, carry):
        for half in range(2):

            def load(f):
                return states(*[uz[2 * f + half, pl.ds(i * 8 + 5 + k, 8)] for k in range(6)])

            def store(f, flux):
                fz[2 * f + half, pl.ds(pl.multiple_of(i * 8, 8), 8)] = flux

            fluxes(load, 2, store)
        return carry

    lax.fori_loop(0, 16, faces_z, 0)
    for half in range(2):

        def load_top(f, half=half):
            rows = [uz[2 * f + half, 133 + k : 141 + k] for k in range(4)]
            return states(*rows, rows[3], rows[3])

        def store_top(f, flux, half=half):
            fz[2 * f + half, 128:136] = flux

        fluxes(load_top, 2, store_top)

    stores = []
    for part in range(5):
        for f in range(part * 3, part * 3 + 3):
            for half in range(2):
                out[f, half * 128 : half * 128 + 128] = (fz[2 * f + half, 0:128] - fz[2 * f + half, 1:129]).T
        some = slice(part * 3, part * 3 + 3)
        stores += load_all([(out.at[some], out_h.at[some])], sems.at[part : part + 1])
    for copy in stores:
        copy.wait()


def flux_xy_kernel(den, mom, ene, ent, tra, along_z_h, xa, xb, ya_h, yb_h, *args):
    pos = position()
    count = len(TREE_CONSTANTS)
    out_h = args[count]
    tables = args[count + 1 : 2 * count + 1]
    ux, fx, uy, fy, ya, yb, along_z, out, sems = args[2 * count + 1 :]
    even_x, even_y = pos[0] % 2 == 0, pos[1] % 2 == 0
    row_a, row_b = [pl.ds(pl.multiple_of(jnp.where(even_x, p, q), 8), 48) for p, q in ((304, 0), (0, 304))]
    loads = load_all(
        fields_into((den, mom, ene, ent, tra), ux, rows=slice(48, 304))
        + [(xa, ux.at[:, row_a]), (xb, ux.at[:, row_b]), (ya_h, ya), (yb_h, yb), (along_z_h, along_z)],
        sems.at[0:10],
    )
    late = load_all(list(zip(args[:count], tables)), sems.at[10 : 10 + count])
    for copy in loads[:7]:
        copy.wait()

    def repeat(source, target):
        for f in range(NF):
            cells = ux[f, source : source + 16]
            for k in range(3):
                ux[f, target + k * 16 : target + k * 16 + 16] = cells

    pl.when(pos[0] == 0)(lambda: repeat(48, 0))
    pl.when(pos[0] == GX - 1)(lambda: repeat(288, 304))

    def faces_x(i, carry):
        for s in range(2):

            def load(f):
                return states(*[ux[f, pl.ds(pl.multiple_of((i + k) * 16 + s * 8, 8), 8)] for k in range(6)])

            def store(f, flux):
                fx[f, pl.ds(pl.multiple_of(i * 16 + s * 8, 8), 8)] = flux

            fluxes(load, 0, store)
        return carry

    lax.fori_loop(0, 17, faces_x, 0)

    def spread(x, carry):
        for f in range(NF):
            uy[f, pl.ds(pl.multiple_of(x * 32 + 8, 8), 16)] = ux[f, pl.ds(pl.multiple_of(48 + x * 16, 8), 16)]
        return carry

    lax.fori_loop(0, 16, spread, 0)
    for copy in loads[7:9]:
        copy.wait()
    first, last = pos[1] == 0, pos[1] == GY - 1
    for f in range(NF):
        for s in range(2):
            low, high = ux[f, pl.ds(48 + s * 128, 8, stride=16)], ux[f, pl.ds(63 + s * 128, 8, stride=16)]
            for k in range(3):
                at = slice(k * 16 + s * 8, k * 16 + s * 8 + 8)
                uy[f, pl.ds(s * 256 + 5 + k, 8, stride=32)] = jnp.where(first, low, jnp.where(even_y, yb[f, at], ya[f, at]))
                uy[f, pl.ds(s * 256 + 24 + k, 8, stride=32)] = jnp.where(last, high, jnp.where(even_y, ya[f, at], yb[f, at]))

    for s in range(2):

        def load_end(f, s=s):
            return states(*[uy[f, pl.ds(s * 256 + 21 + k, 8, stride=32)] for k in range(6)])

        def store_end(f, flux, s=s):
            fy[f, pl.ds(s * 192 + 16, 8, stride=24)] = flux

        fluxes(load_end, 1, store_end)
    def faces_y(x):
        for s in range(2):

            def load(f):
                return states(*[uy[f, pl.ds(x * 32 + s * 8 + 5 + k, 8)] for k in range(6)])

            def store(f, flux):
                fy[f, pl.ds(pl.multiple_of(x * 24 + s * 8, 8), 8)] = flux

            fluxes(load, 1, store)

    loads[9].wait()

    def gather(x):
        for f in range(NF):
            for s in range(2):
                at = pl.multiple_of(x * 16 + s * 8, 8)
                rows = pl.ds(at, 8)
                change = along_z[f, rows] + (fx[f, rows] - fx[f, pl.ds(pl.multiple_of(at + 16, 8), 8)])
                y = pl.multiple_of(x * 24 + s * 8, 8)
                out[f, rows] = change + (fy[f, pl.ds(y, 8)] - fy[f, pl.ds(y + 1, 8)])

    def both(x, carry):
        gather(x - 1)
        faces_y(x)
        return carry

    faces_y(0)
    for part in range(4):
        lax.fori_loop(part * 4 + 1, min(part * 4 + 5, 16), both, 0)
        if part == 3:
            gather(15)
        rows = slice(part * 64, part * 64 + 64)
        late += load_all([(out.at[:, rows], out_h.at[:, rows])], sems.at[10 + count + part : 11 + count + part])
    for copy in late:
        copy.wait()


TREE_CONSTANTS = (
    "w_high", "w_low", "sel_zero", "lane_odd", "up", "alpha_odd", "agg", "mask", "info", "expand", "gamma_odd", "down",
    "spread", "poly",
)


def tree_kernel(far, den, mom, ene, ent, tra, change_h, *args):
    count = len(TREE_CONSTANTS)
    w_high, w_low, sel_zero, lane_odd, up, alpha_odd, agg, mask, info, expand, gamma_odd, down, spread, poly = args[:count]
    section, accel, rhs, field, result, force, u, change, sems = args[count:]
    late = []
    for q in range(4):
        rows = slice(q * 64, q * 64 + 64)
        pairs = fields_into((den, mom, ene, ent, tra), u, rows, rows) + [(change_h.at[:, rows], change.at[:, rows])]
        late.append(load_all(pairs, sems.at[8 + 6 * q : 14 + 6 * q]))
    px, py = position()
    blocks = []
    for dx in range(3):
        here = jnp.clip(px + dx - 1, 0, GX - 1)
        inside = here == px + dx - 1
        blocks.append([jnp.where(inside, far[here, 12 + n * 4 : 16 + n * 4], 0.0) for n in range(9)])
    gap = jnp.zeros((4, 128), F32)
    around = jnp.concatenate(
        [jnp.concatenate([blocks[dx][dy * 3 + c] for dx in range(3) for dy in range(3)] + [gap], 0) for c in range(3)], 1
    )
    zero = mxu(sel_zero[...], jnp.concatenate(split(around), 1))
    zero = zero[:, :384] + zero[:, 384:]
    arrays = [zero[c * WIN : c * WIN + WIN] * lane_odd[c : c + 1] for c in range(4)]
    packed = [jnp.concatenate([far[x, c * 4 : c * 4 + 4] for x in range(GX)], 0) for c in range(3)]
    lower = lane_ids((128, 128)) % 16 < 8
    gathered = jnp.concatenate(
        [jnp.where(lower, jnp.concatenate([rows, pltpu.roll(rows, 120, 1)], 0), 0.0) for rows in packed], 1
    )
    speeds = gathered[:, 256:]
    fastest = jnp.max(jnp.where(lane_ids((128, 128)) >= 64, speeds, 0.0))

    def lifted(x, x_odd, y_odd):
        sign = (1.0 - 2.0 * x_odd * alpha_odd[0:1]) * (1.0 - 2.0 * y_odd * alpha_odd[1:2])
        n = x.shape[0]
        z = mxu(jnp.concatenate(split(x * sign), 0), up[...])
        return (z[:n] + z[n:]) * sign

    def picked(matrix, x):
        y = mxu(matrix, jnp.concatenate(split(x), 1))
        return y[:, :384] + y[:, 384:]

    dev = lax.broadcasted_iota(jnp.int32, (128, 1), 0)
    raised = lifted(gathered, ((dev // 4) % 2).astype(F32), (dev // 64).astype(F32))
    two = picked(agg[...], raised)
    cell = lax.broadcasted_iota(jnp.int32, (32, 1), 0)
    raised_two = lifted(two, ((cell // 4) % 2).astype(F32), (cell % 2).astype(F32))

    def window(level, columns, shift):
        tx, ty = px >> (level - 1), py >> (level - 1)
        row = lax.broadcasted_iota(jnp.int32, (WIN, columns), 0)
        col = lax.broadcasted_iota(jnp.int32, (WIN, columns), 1)
        i, j = row // 6, row % 6
        i = jnp.where((tx & 1) == 1, 5 - i, i) + 2 * ((tx >> 1) - 1)
        j = jnp.where((ty & 1) == 1, 5 - j, j) + 2 * ((ty >> 1) - 1)
        if columns == 128:
            sx, sy = (col % 64) // 4, 2 * (col % 4) + col // 64
        else:
            sx, sy = col // 4, col % 4
        sx, sy = sx >> shift, sy >> shift
        return ((row < 36) & (sx == i) & (sy == j)).astype(F32).astype(BF16)

    levels = (
        picked(window(1, 128, 0), gathered)
        + picked(window(2, 128, 1), raised)
        + picked(window(3, 32, 1), raised_two)
    )
    sign = jnp.ones((1, 384), F32)
    for level in (1, 2, 3):
        bx = ((px >> (level - 1)) & 1).astype(F32)
        by = ((py >> (level - 1)) & 1).astype(F32)
        sign = sign * (1.0 - 2.0 * bx * lane_odd[4 + level : 5 + level])
        sign = sign * (1.0 - 2.0 * by * lane_odd[8 + level : 9 + level])
    levels = levels * sign
    wrow = lax.broadcasted_iota(jnp.int32, (WIN, 384), 0)
    wi, wj = wrow // 6, wrow % 6
    touching = (wi >= 1) & (wi <= 3) & (wj >= 1) & (wj <= 3)
    arrays += [levels, jnp.where(touching, 0.0, levels)]
    lane = lane_ids((WIN, 128)) // 16
    for a in range(NA):
        c, off = a // 8, (a % 8) * 16
        block = jnp.zeros((WIN, 128), F32)
        for g, array in enumerate(arrays):
            block = jnp.where(lane == g, pltpu.roll(array[:, c * 128 : c * 128 + 128], (16 * g - off) % 128, 1), block)
        rhs[a * WIN : a * WIN + WIN] = block
    high, low = split(rhs[...])
    y = mxu(w_high[...], jnp.concatenate([high, low], 1))
    y = y[:, :128] + y[:, 128:] + mxu(w_low[...], high)
    base = jnp.zeros((NG, 128), F32)
    for k in range(7):
        base = base + mask[k : k + 1] * pltpu.roll(y[k * NG : k * NG + NG], (3 - k) % 128, 1)
    lanes = lane_ids((NG, 128)) // 16
    base = base + jnp.where(lanes == 4, pltpu.roll(base, 112, 1), 0.0)
    bx, by = info[1:2], info[2:3]
    for level in (1, 2, 3):
        bx = bx + info[2 + 2 * level : 3 + 2 * level] * ((px >> (level - 1)) & 1).astype(F32)
        by = by + info[2 + 2 * level : 3 + 2 * level] * ((py >> (level - 1)) & 1).astype(F32)
    flip = (1.0 - 2.0 * bx * gamma_odd[0:NG]) * (1.0 - 2.0 * by * gamma_odd[NG : 2 * NG])
    base = base * info[0:1] * flip
    flip = flip * (1.0 - 2.0 * info[9:10] * gamma_odd[2 * NG :])
    total = base
    for _ in range(3):
        parents = mxu(split_rows(total), expand[...])
        pieces = jnp.concatenate(split(flip * (parents[:NG] + parents[NG:])), 1)
        carried = mxu(down[...], pieces)
        total = base + flip * (carried[:, :128] + carried[:, 128:])
    rows = jnp.concatenate([pltpu.roll(total, (128 - 16 * c) % 128, 1) for c in range(4)], 0)[:, :16]
    spreads = mxu(split_rows(rows), spread[...])
    spreads = spreads[: 4 * NG] + spreads[4 * NG :]
    terms = jnp.concatenate(
        [
            jnp.concatenate([spreads[c * NG : c * NG + NG, k * 128 : k * 128 + 128] for k in range(3)], 0)
            for c in range(4)
        ],
        1,
    )
    values = mxu(poly[...], jnp.concatenate(split(terms), 1))
    field[...] = values[:, :512] + values[:, 512:]
    step = jnp.full((8, 128), COURANT / SUB, F32) / fastest
    stores = []
    for part in range(4):
        half = part // 2
        for copy in late[part]:
            copy.wait()

        def finish(x, carry, half=half):
            for s in range(2):
                c = half * 2 + s
                at = pl.multiple_of(half * 128 + x * 16 + s * 8, 8)
                rows = pl.ds(at, 8)
                acc = [field[pl.ds(pl.multiple_of(i * 64 + x * 8, 8), 8), c * 128 : c * 128 + 128] for i in range(3)]
                old = [u[f, rows] for f in range(NF)]
                for i in range(3):
                    force[i, rows] = acc[i]
                for f in range(NF):
                    slope = change[f, rows]
                    if 1 <= f <= 3:
                        slope = slope + old[0] * acc[f - 1]
                    if f == 4:
                        slope = slope + (old[1] * acc[0] + old[2] * acc[1] + old[3] * acc[2])
                    result[f, rows] = old[f] + step * slope
            return carry

        lax.fori_loop((part % 2) * 4, (part % 2) * 4 + 4, finish, 0)
        rows = slice(part * 64, part * 64 + 64)
        stores += load_all(
            [(result.at[:, rows], section.at[:, rows]), (force.at[:, rows], accel.at[:, rows])],
            sems.at[2 * part : 2 * part + 2],
        )
    for copy in stores:
        copy.wait()


ANY = pl.BlockSpec(memory_space=pl.ANY)
HBM = pl.BlockSpec(memory_space=pltpu.HBM)
VMEM = pl.BlockSpec(memory_space=pltpu.VMEM)


def call(kernel, name, ins, outs, scratch, cost, aliases=None):
    outs = [(o[0], o[1], o[2] if len(o) > 2 else F32) for o in outs]
    return pl.pallas_call(
        kernel,
        out_shape=[pltpu.HBM(s, t) if spec is HBM else jax.ShapeDtypeStruct(s, t) for s, spec, t in outs],
        in_specs=[spec for _, spec in ins],
        out_specs=[spec for _, spec, _ in outs],
        scratch_shapes=scratch,
        input_output_aliases=aliases or {},
        cost_estimate=pl.CostEstimate(flops=cost[0], bytes_accessed=cost[1], transcendentals=cost[2]),
        name=name,
        compiler_params=pltpu.CompilerParams(vmem_limit_bytes=32 << 20),
    )(*[in_hbm(x) if spec is HBM else x for x, spec in ins])


def in_hbm(x):
    return pltpu.with_memory_space_constraint(x, pltpu.HBM)


def scratch_like(x):
    return pltpu.VMEM(x.shape, x.dtype)


def shards(density, momentum, energy, entropy, tracers, leaf_flags):
    con = {k: jnp.asarray(v) for k, v in constants().items()}
    fields = [(x.reshape(-1, ROWS, 128), HBM) for x in (density, momentum, energy, entropy, tracers)]
    first = [con[n] for n in ("left", "right", "flag")]
    whole, slab = (NF, ROWS, 128), (NF, 48, 128)
    block, halo = pltpu.VMEM(whole, F32), pltpu.VMEM(slab, F32)
    pay, u, xa, xb, ya, yb = call(
        prepare_kernel,
        "prepare",
        fields + [(leaf_flags, HBM)] + [(x, HBM) for x in first],
        [((GY, 16, 128), HBM), (whole, VMEM)] + [(slab, HBM)] * 4,
        [pltpu.VMEM((16, 128), F32), pltpu.VMEM((2, *slab), F32), pltpu.VMEM((8, 128), F32), scratch_like(leaf_flags)]
        + [scratch_like(x) for x in first]
        + [pltpu.SemaphoreType.DMA((13 + GY,))],
        (10**7, 4 * 10**6, 10**5),
    )

    def pairs(count, start):
        lows = range(start, count, 2)
        return [(i, (i + 1) % count) for i in lows] + [((i + 1) % count, i) for i in lows]

    column = lax.all_to_all(pay, "my", 0, 0)
    swaps = [
        (lax.ppermute(slab, axis, pairs(count, start)), ANY)
        for slab, axis, count, start in ((xb, "mx", GX, 1), (yb, "my", GY, 1), (xa, "mx", GX, 0), (ya, "my", GY, 0))
    ]
    halos = [swaps[i] for i in (2, 0, 3, 1)]
    (along_z,) = call(
        flux_z_kernel,
        "flux_z",
        [(u, VMEM)],
        [(whole, HBM)],
        [pltpu.VMEM((2 * NF, 144, 128), F32), pltpu.VMEM((2 * NF, 136, 128), F32), block, pltpu.SemaphoreType.DMA((5,))],
        (2 * 10**7, 4 * 10**6, 3 * 10**5),
    )
    (chunks,) = call(
        relay_kernel,
        "relay",
        [(column.reshape(GY * 16, 128), VMEM), (along_z, HBM)] + swaps,
        [((GX, 48, 128), HBM)],
        [pltpu.VMEM((48, 128), F32), pltpu.SemaphoreType.DMA((GX,))],
        (10**4, 10**6, 0),
    )
    far = lax.all_to_all(chunks, "mx", 0, 0)
    second = [con[n] for n in TREE_CONSTANTS]
    tend, *tables = call(
        flux_xy_kernel,
        "flux_xy",
        fields + [(along_z, HBM)] + halos + [(x, HBM) for x in second],
        [(whole, HBM)] + [(x.shape, VMEM, x.dtype) for x in second],
        [
            pltpu.VMEM((NF, 352, 128), F32),
            pltpu.VMEM((NF, 272, 128), F32),
            pltpu.VMEM((NF, 512, 128), F32),
            pltpu.VMEM((NF, 384, 128), F32),
            halo,
            halo,
            block,
            block,
            pltpu.SemaphoreType.DMA((14 + len(second),)),
        ],
        (4 * 10**7, 6 * 10**6, 6 * 10**5),
    )
    section, accel = call(
        tree_kernel,
        "tree",
        [(far, VMEM)] + fields + [(tend, HBM)] + [(x, VMEM) for x in tables],
        [(whole, HBM), ((3, ROWS, 128), HBM)],
        [
            pltpu.VMEM((NA * WIN, 128), F32),
            pltpu.VMEM((192, 512), F32),
            block,
            pltpu.VMEM((3, ROWS, 128), F32),
            block,
            block,
            pltpu.SemaphoreType.DMA((32,)),
        ],
        (10**8, 8 * 10**6, 0),
    )
    return section.reshape(NF, 16, 16, 128), accel.reshape(3, 16, 16, 128)


def solution(mesh):
    placed = (
        P("mx", "my", None),
        P(None, "mx", "my", None),
        P("mx", "my", None),
        P("mx", "my", None),
        P(None, "mx", "my", None),
        P("mx", "my", None),
    )
    return jax.shard_map(
        shards,
        mesh=mesh,
        in_specs=placed,
        out_specs=(P(None, "mx", "my", None), P(None, "mx", "my", None)),
        check_vma=False,
    )
```

```python
import functools
import math

import jax
import jax.numpy as jnp
import ml_dtypes
import numpy as np
from jax import lax
from jax.experimental import pallas as pl
from jax.experimental.pallas import tpu as pltpu
from jax.sharding import PartitionSpec as P

F32 = jnp.float32
BF16 = jnp.bfloat16
HIGHEST = lax.Precision.HIGHEST
GRAVITY = 0.02
GAMMA = 5.0 / 3.0
COURANT = 0.3
SUB = 8
NF = 15
GX, GY = 16, 8
ROWS = 256

ALPHA = [
    (px, py, d - px - py)
    for d in range(4)
    for px in range(d, -1, -1)
    for py in range(d - px, -1, -1)
]
NA = len(ALPHA)
NG = 24
WIN = 40
PAIRS = [(px, py) for px in range(4) for py in range(4 - px)]


def factorial_of(e):
    return math.factorial(e[0]) * math.factorial(e[1]) * math.factorial(e[2])


def inverse_derivative(exponent, r):
    axes = [0] * exponent[0] + [1] * exponent[1] + [2] * exponent[2]
    norm = math.sqrt(r[0] ** 2 + r[1] ** 2 + r[2] ** 2)
    if norm == 0.0:
        return 0.0
    if not axes:
        return 1.0 / norm
    if len(axes) == 1:
        return -r[axes[0]] / norm**3
    if len(axes) == 2:
        a, b = axes
        return 3.0 * r[a] * r[b] / norm**5 - float(a == b) / norm**3
    a, b, c = axes
    crossed = float(a == b) * r[c] + float(a == c) * r[b] + float(b == c) * r[a]
    return -15.0 * r[a] * r[b] * r[c] / norm**7 + 3.0 * crossed / norm**5


def split_np(x):
    high = x.astype(np.float32).astype(ml_dtypes.bfloat16)
    low = (x - high.astype(np.float64)).astype(ml_dtypes.bfloat16)
    return high, low


def exact_np(x):
    y = x.astype(ml_dtypes.bfloat16)
    assert np.array_equal(x, y.astype(np.float64))
    return y


@functools.cache
def constants():
    out = {}
    w = np.zeros((7, NG, NA, WIN))
    for z in range(7):
        for i in range(6):
            for j in range(6):
                r = (-(i - 2.0), -(j - 2.0), -(z - 3.0))
                for g, eg in enumerate(ALPHA):
                    for a, ea in enumerate(ALPHA):
                        if sum(eg) + sum(ea) <= 3:
                            e = tuple(eg[k] + ea[k] for k in range(3))
                            w[z, g, a, i * 6 + j] = (
                                -GRAVITY
                                * (-1.0) ** sum(ea)
                                / (factorial_of(ea) * factorial_of(eg))
                                * inverse_derivative(e, r)
                            )
    out["w_high"], out["w_low"] = split_np(w.reshape(7 * NG, NA * WIN))
    sel = np.zeros((4, WIN, 40))
    sign = np.zeros((4, 384))
    for c in range(4):
        cx, cy = c >> 1, c & 1
        for i in range(6):
            for j in range(6):
                si, sj = (5 - i if cx else i), (5 - j if cy else j)
                sel[c, i * 6 + j, ((si // 2) * 3 + sj // 2) * 4 + (si % 2) * 2 + sj % 2] = 1.0
        for a, e in enumerate(ALPHA):
            sign[c, a * 16 : a * 16 + 16] = (-1.0) ** (cx * e[0] + cy * e[1])
    out["sel_zero"] = sel.reshape(4 * WIN, 40).astype(ml_dtypes.bfloat16)
    lanes = np.zeros((16, 384), np.float32)
    lanes[0:4] = sign
    for a, e in enumerate(ALPHA):
        for r in range(16):
            lane = a * 16 + r
            level = 1 if r < 8 else 2 if r < 12 else 3
            lanes[4 + level, lane] = e[0] % 2
            lanes[8 + level, lane] = e[1] % 2
    out["lane_odd"] = lanes
    up = np.zeros((384, 384))
    for t, et in enumerate(ALPHA):
        for s, es in enumerate(ALPHA):
            if all(es[k] <= et[k] for k in range(3)):
                for base, to, count in ((0, 8, 8), (8, 12, 4)):
                    for z in range(count):
                        v = 2.0 ** -sum(et)
                        for k in range(3):
                            d = -0.5 if k < 2 or z % 2 == 0 else 0.5
                            v *= math.comb(et[k], es[k]) * d ** (et[k] - es[k])
                        up[s * 16 + base + z, t * 16 + to + z // 2] = v
    out["up"] = exact_np(up)
    odd = np.zeros((16, 384), np.float32)
    for a, e in enumerate(ALPHA):
        odd[0, a * 16 : a * 16 + 16] = e[0] % 2
        odd[1, a * 16 : a * 16 + 16] = e[1] % 2
    out["alpha_odd"] = odd
    agg = np.zeros((32, 128))
    for x in range(GX):
        for y in range(GY):
            agg[(x // 2) * 4 + y // 2, (y % 2) * 64 + x * 4 + y // 2] = 1.0
    out["agg"] = agg.astype(ml_dtypes.bfloat16)
    mask = np.zeros((8, 128), np.float32)
    info = np.zeros((16, 128), np.float32)
    expand = np.zeros((128, 128), np.float32)
    for lane in range(96):
        g, r = lane // 16, lane % 16
        if g < 4:
            n, z, level = 16, r, 0
        elif r < 8:
            n, z, level = 8, r, 1
        elif r < 12:
            n, z, level = 4, r - 8, 2
        elif r < 14:
            n, z, level = 2, r - 12, 3
        else:
            continue
        for k in range(7):
            o = k - 3
            ok = 0 <= z + o < n and abs((z + o) // 2 - z // 2) <= 1
            if g == 4:
                ok = ok and abs(o) > 1
            if g == 5:
                ok = ok and abs(o) <= 1
            mask[k, lane] = float(ok)
        if g < 5:
            info[0, lane] = 2.0**-level
            info[1, lane] = float(g >> 1) if level == 0 else 0.0
            info[2, lane] = float(g & 1) if level == 0 else 0.0
            info[2 + 2 * level, lane] = 1.0 if level else info[2, lane]
            info[9, lane] = float(z % 2)
            if level == 0:
                expand[64 + z // 2, lane] = 1.0
            elif level == 1:
                expand[64 + 8 + z // 2, lane] = 1.0
            elif level == 2:
                expand[64 + 12 + z // 2, lane] = 1.0
    out["mask"] = mask
    out["info"] = info
    out["expand"] = exact_np(expand)
    gamma_odd = np.zeros((3 * NG, 128), np.float32)
    down = np.zeros((NG, NG))
    for g, eg in enumerate(ALPHA):
        for k in range(3):
            gamma_odd[k * NG + g] = eg[k] % 2
        for b, eb in enumerate(ALPHA):
            if all(eb[k] >= eg[k] for k in range(3)):
                v = 2.0 ** -sum(eg)
                for k in range(3):
                    n = eb[k] - eg[k]
                    v *= (-0.25) ** n * math.comb(eb[k], eg[k])
                down[g, b] = v
    out["gamma_odd"] = gamma_odd
    out["down"] = exact_np(down)
    h = (np.arange(SUB) + 0.5) / SUB - 0.5
    spread = np.zeros((16, 384))
    for k in range(3):
        for z in range(128):
            spread[z // 8, k * 128 + z] = h[z % 8] ** k
    out["spread"] = exact_np(spread)
    poly = np.zeros((3, 8, 8, 3, NG))
    for i in range(3):
        for g, e in enumerate(ALPHA):
            if e[i] > 0:
                low = list(e)
                low[i] -= 1
                poly[i, :, :, low[2], g] = (
                    -e[i] * h[:, None] ** low[0] * h[None, :] ** low[1]
                )
    out["poly"] = exact_np(poly.reshape(192, 72))
    cells = np.arange(16)
    near = h[cells % 8]
    far = ((cells + 0.5) / 8 - 1.0) / 2
    left = np.zeros((2, len(PAIRS), 8, 16, 16))
    for q, (px, py) in enumerate(PAIRS):
        for c in range(4):
            block = ((cells // 8 == c >> 1)[:, None] & (cells // 8 == (c & 1))[None, :]).astype(float)
            left[0, q, c] = block * near[:, None] ** px * near[None, :] ** py
            left[1, q, c] = block * far[:, None] ** px * far[None, :] ** py
    out["left"] = left.reshape(160, 256).astype(np.float32)
    right = np.zeros((128, 128))
    flag = np.zeros((128, 128))
    for z in range(128):
        s = z // 8
        f = ((z % 16 + 0.5) / 8 - 1.0) / 2
        for pz in range(4):
            right[z, pz * 16 + s] = h[z % 8] ** pz / SUB**3
            right[z, 64 + (s % 2) * 32 + pz * 8 + s // 2] = f**pz / SUB**3
    for s in range(16):
        for pz in range(4):
            flag[s, pz * 16 + s] = 1.0
            flag[s, 64 + (s % 2) * 32 + pz * 8 + s // 2] = 1.0
    out["right"] = right.astype(np.float32)
    out["flag"] = flag.astype(ml_dtypes.bfloat16)
    return out


def split(x):
    high = x.astype(BF16)
    return high, (x - high.astype(F32)).astype(BF16)


def split_rows(x):
    high = x.astype(BF16).astype(F32)
    return jnp.concatenate([high, x - high], 0).astype(BF16)


def mxu(a, b):
    return jnp.dot(a, b, preferred_element_type=F32)


def exact(a, b):
    return jnp.dot(a, b, precision=HIGHEST, preferred_element_type=F32)


def lane_ids(shape):
    return lax.broadcasted_iota(jnp.int32, shape, len(shape) - 1)


def row_ids(shape):
    return lax.broadcasted_iota(jnp.int32, shape, len(shape) - 2)


def power(s):
    return jnp.exp2(GAMMA * jnp.log2(s))


def root(x):
    return x * lax.rsqrt(x)


PLACES = ((0, 1), (1, 3), (4, 1), (5, 1), (6, 9))


def position():
    return lax.axis_index("mx"), lax.axis_index("my")


def load_all(pairs, sems):
    copies = [pltpu.make_async_copy(source, target, sems.at[k]) for k, (source, target) in enumerate(pairs)]
    for copy in copies:
        copy.start()
    return copies


def fields_into(refs, target, source=slice(0, ROWS), rows=None):
    place = slice(0, source.stop - source.start) if rows is None else rows
    return [
        (ref.at[:, source], target.at[start : start + count, place]) for ref, (start, count) in zip(refs, PLACES)
    ]


def prepare_kernel(den, mom, ene, ent, tra, flags, left, right, flag, pay_h, u, xa, xb, ya, yb, *scratch):
    pos = position()
    pay, sides, fl, flv, leftv, rightv, flagv, sems = scratch
    small = load_all(zip((flags, left, right, flag), (flv, leftv, rightv, flagv)), sems.at[7:11])
    loads = load_all(fields_into((den, mom, ene, ent, tra), u), sems.at[0:5])
    even_x, even_y = pos[0] % 2 == 0, pos[1] % 2 == 0
    for copy in small:
        copy.wait()
    fl[...] = jnp.zeros((8, 128), F32)
    fl[0:2, 0:16] = flv[0].astype(F32)
    fl[2:4, 0:16] = flv[1].astype(F32)
    tile = mxu(fl[...].astype(BF16), flagv[...])
    for k in (0, 1, 3):
        loads[k].wait()
    rho = u[0]
    sums = exact(leftv[...], exact(rho, rightv[...]))
    inverse = 1.0 / rho
    fast = jnp.maximum(jnp.maximum(jnp.abs(u[1]), jnp.abs(u[2])), jnp.abs(u[3]))
    sound = root(GAMMA * (GAMMA - 1.0) * power(u[5]) * inverse)
    fastest = jnp.max(fast * inverse + sound)
    lane = lane_ids((8, 128))
    row = row_ids((8, 128))
    tiles = [jnp.zeros((8, 128), F32) for _ in range(3)]
    zero, one = {}, {}
    for q, pair in enumerate(PAIRS):
        zero[pair] = sums[q * 8 : q * 8 + 8] * tile
        v = jnp.sum(sums[80 + q * 8 : 88 + q * 8] * tile, axis=0, keepdims=True)
        v = jnp.broadcast_to(v, (8, 128))
        one[pair] = v + pltpu.roll(v, 96, 1)
    for a, e in enumerate(ALPHA):
        c, to = a // 8, (a % 8) * 16
        low = pltpu.roll(zero[e[0], e[1]], (to - e[2] * 16) % 128, 1)
        top = pltpu.roll(one[e[0], e[1]], (to - 64 - e[2] * 8) % 128, 1)
        here = (lane >= to) & (lane < to + 16)
        tiles[c] = jnp.where(here & (row < 4), low, tiles[c])
        tiles[c] = jnp.where(here & (row == 4) & (lane < to + 8), top, tiles[c])
    tiles[2] = jnp.where((row == 4) & (lane >= 64) & (lane < 72), fastest, tiles[2])
    pay[8:16] = jnp.zeros((8, 128), F32)
    for c in range(3):
        pay[c * 5 : c * 5 + 5] = tiles[c][0:5]
    slabs = load_all([(pay, pay_h.at[y]) for y in range(GY)], sems.at[13 : 13 + GY])
    for k in (2, 4):
        loads[k].wait()
    row_a, row_b = jnp.where(even_x, 208, 0), jnp.where(even_x, 0, 208)
    slabs += load_all(
        [(u.at[:, pl.ds(pl.multiple_of(r, 8), 48)], slab) for r, slab in ((row_a, xa), (row_b, xb))], sems.at[5:7]
    )
    for f in range(NF):
        for k in range(3):
            for s in range(2):
                at = slice(k * 16 + s * 8, k * 16 + s * 8 + 8)
                sides[0, f, at] = u[f, pl.ds(s * 128 + k, 8, stride=16)]
                sides[1, f, at] = u[f, pl.ds(s * 128 + 13 + k, 8, stride=16)]
    side_a, side_b = jnp.where(even_y, 1, 0), jnp.where(even_y, 0, 1)
    slabs += load_all([(sides.at[side_a], ya), (sides.at[side_b], yb)], sems.at[11:13])
    for copy in slabs:
        copy.wait()


def relay_kernel(column, *rest):
    out_h, out, sems = rest[-3:]
    y = position()[1]
    even = [column[pl.ds(c * 5 + 4, 4, stride=32)] for c in range(3)]
    odd = [column[pl.ds(c * 5 + 20, 4, stride=32)] for c in range(3)]
    near = []
    for dy in range(3):
        here = jnp.clip(y + dy - 1, 0, GY - 1)
        inside = here == y + dy - 1
        for c in range(3):
            tile = column[pl.ds(here * 16 + c * 5, 4)]
            near.append(jnp.where(inside, tile, 0.0))
    for c in range(3):
        out[c * 4 : c * 4 + 4] = even[c] + pltpu.roll(odd[c], 8, 1)
    for n, tile in enumerate(near):
        out[12 + n * 4 : 16 + n * 4] = tile
    for copy in load_all([(out, out_h.at[x]) for x in range(GX)], sems):
        copy.wait()


def states(ol, il, l, r, ir, orr):
    face = (37.0 / 60.0) * (l + r) - (8.0 / 60.0) * (il + ir) + (1.0 / 60.0) * (ol + orr)
    low, high = jnp.minimum(l, r), jnp.maximum(l, r)
    left = jnp.minimum(jnp.maximum(face, jnp.minimum(il, low)), jnp.maximum(il, high))
    right = jnp.minimum(jnp.maximum(face, jnp.minimum(low, ir)), jnp.maximum(high, ir))
    return left, right


def fluxes(load, d, store):
    rl, rr = load(0)
    ml, mr = load(1 + d)
    sl, sr = load(5)
    il, ir = 1.0 / rl, 1.0 / rr
    vl, vr = ml * il, mr * ir
    gl, gr = power(sl), power(sr)
    cl, cr = root(GAMMA * (GAMMA - 1.0) * gl * il), root(GAMMA * (GAMMA - 1.0) * gr * ir)
    a = 4.0 * jnp.maximum(jnp.abs(vl) + cl, jnp.abs(vr) + cr)
    wl, wr = 4.0 * vl, 4.0 * vr
    kl, kr = wl + a, wr - a
    got = {0: (rl, rr), 1 + d: (ml, mr), 5: (sl, sr)}
    for f in range(NF):
        left, right = got[f] if f in got else load(f)
        flux = left * kl + right * kr
        if f == 1 + d:
            flux = flux + (4.0 * (GAMMA - 1.0)) * (gl + gr)
        if f == 4:
            flux = flux + (GAMMA - 1.0) * (gl * wl + gr * wr)
        store(f, flux)


def flux_z_kernel(u, out_h, uz, fz, out, sems):
    for f in range(NF):
        for half in range(2):
            cells = u[f, half * 128 : half * 128 + 128].T
            uz[2 * f + half, 8:136] = cells
            uz[2 * f + half, 0:8] = jnp.broadcast_to(cells[0:1], (8, 128))
            uz[2 * f + half, 136:144] = jnp.broadcast_to(cells[127:128], (8, 128))

    def faces_z(i, carry):
        for half in range(2):

            def load(f):
                return states(*[uz[2 * f + half, pl.ds(i * 8 + 5 + k, 8)] for k in range(6)])

            def store(f, flux):
                fz[2 * f + half, pl.ds(pl.multiple_of(i * 8, 8), 8)] = flux

            fluxes(load, 2, store)
        return carry

    lax.fori_loop(0, 16, faces_z, 0)
    for half in range(2):

        def load_top(f, half=half):
            rows = [uz[2 * f + half, 133 + k : 141 + k] for k in range(4)]
            return states(*rows, rows[3], rows[3])

        def store_top(f, flux, half=half):
            fz[2 * f + half, 128:136] = flux

        fluxes(load_top, 2, store_top)

    stores = []
    for part in range(5):
        for f in range(part * 3, part * 3 + 3):
            for half in range(2):
                out[f, half * 128 : half * 128 + 128] = (fz[2 * f + half, 0:128] - fz[2 * f + half, 1:129]).T
        some = slice(part * 3, part * 3 + 3)
        stores += load_all([(out.at[some], out_h.at[some])], sems.at[part : part + 1])
    for copy in stores:
        copy.wait()


def flux_xy_kernel(den, mom, ene, ent, tra, along_z_h, xa, xb, ya_h, yb_h, *args):
    pos = position()
    count = len(TREE_CONSTANTS)
    out_h = args[count]
    tables = args[count + 1 : 2 * count + 1]
    ux, fx, uy, fy, ya, yb, along_z, out, sems = args[2 * count + 1 :]
    even_x, even_y = pos[0] % 2 == 0, pos[1] % 2 == 0
    row_a, row_b = [pl.ds(pl.multiple_of(jnp.where(even_x, p, q), 8), 48) for p, q in ((304, 0), (0, 304))]
    loads = load_all(
        fields_into((den, mom, ene, ent, tra), ux, rows=slice(48, 304))
        + [(xa, ux.at[:, row_a]), (xb, ux.at[:, row_b]), (ya_h, ya), (yb_h, yb), (along_z_h, along_z)],
        sems.at[0:10],
    )
    late = load_all(list(zip(args[:count], tables)), sems.at[10 : 10 + count])
    for copy in loads[:7]:
        copy.wait()

    def repeat(source, target):
        for f in range(NF):
            cells = ux[f, source : source + 16]
            for k in range(3):
                ux[f, target + k * 16 : target + k * 16 + 16] = cells

    pl.when(pos[0] == 0)(lambda: repeat(48, 0))
    pl.when(pos[0] == GX - 1)(lambda: repeat(288, 304))

    def faces_x(i, carry):
        for s in range(2):

            def load(f):
                return states(*[ux[f, pl.ds(pl.multiple_of((i + k) * 16 + s * 8, 8), 8)] for k in range(6)])

            def store(f, flux):
                fx[f, pl.ds(pl.multiple_of(i * 16 + s * 8, 8), 8)] = flux

            fluxes(load, 0, store)
        return carry

    lax.fori_loop(0, 17, faces_x, 0)

    def spread(x, carry):
        for f in range(NF):
            uy[f, pl.ds(pl.multiple_of(x * 32 + 8, 8), 16)] = ux[f, pl.ds(pl.multiple_of(48 + x * 16, 8), 16)]
        return carry

    lax.fori_loop(0, 16, spread, 0)
    for copy in loads[7:9]:
        copy.wait()
    first, last = pos[1] == 0, pos[1] == GY - 1
    for f in range(NF):
        for s in range(2):
            low, high = ux[f, pl.ds(48 + s * 128, 8, stride=16)], ux[f, pl.ds(63 + s * 128, 8, stride=16)]
            for k in range(3):
                at = slice(k * 16 + s * 8, k * 16 + s * 8 + 8)
                uy[f, pl.ds(s * 256 + 5 + k, 8, stride=32)] = jnp.where(first, low, jnp.where(even_y, yb[f, at], ya[f, at]))
                uy[f, pl.ds(s * 256 + 24 + k, 8, stride=32)] = jnp.where(last, high, jnp.where(even_y, ya[f, at], yb[f, at]))

    for s in range(2):

        def load_end(f, s=s):
            return states(*[uy[f, pl.ds(s * 256 + 21 + k, 8, stride=32)] for k in range(6)])

        def store_end(f, flux, s=s):
            fy[f, pl.ds(s * 192 + 16, 8, stride=24)] = flux

        fluxes(load_end, 1, store_end)
    def faces_y(x):
        for s in range(2):

            def load(f):
                return states(*[uy[f, pl.ds(x * 32 + s * 8 + 5 + k, 8)] for k in range(6)])

            def store(f, flux):
                fy[f, pl.ds(pl.multiple_of(x * 24 + s * 8, 8), 8)] = flux

            fluxes(load, 1, store)

    loads[9].wait()

    def gather(x):
        for f in range(NF):
            for s in range(2):
                at = pl.multiple_of(x * 16 + s * 8, 8)
                rows = pl.ds(at, 8)
                change = along_z[f, rows] + (fx[f, rows] - fx[f, pl.ds(pl.multiple_of(at + 16, 8), 8)])
                y = pl.multiple_of(x * 24 + s * 8, 8)
                out[f, rows] = change + (fy[f, pl.ds(y, 8)] - fy[f, pl.ds(y + 1, 8)])

    def both(x, carry):
        gather(x - 1)
        faces_y(x)
        return carry

    faces_y(0)
    for part in range(4):
        lax.fori_loop(part * 4 + 1, min(part * 4 + 5, 16), both, 0)
        if part == 3:
            gather(15)
        rows = slice(part * 64, part * 64 + 64)
        late += load_all([(out.at[:, rows], out_h.at[:, rows])], sems.at[10 + count + part : 11 + count + part])
    for copy in late:
        copy.wait()


TREE_CONSTANTS = (
    "w_high", "w_low", "sel_zero", "lane_odd", "up", "alpha_odd", "agg", "mask", "info", "expand", "gamma_odd", "down",
    "spread", "poly",
)


def tree_kernel(far, den, mom, ene, ent, tra, change_h, *args):
    count = len(TREE_CONSTANTS)
    w_high, w_low, sel_zero, lane_odd, up, alpha_odd, agg, mask, info, expand, gamma_odd, down, spread, poly = args[:count]
    section, accel, rhs, field, result, force, u, change, sems = args[count:]
    late = []
    for q in range(4):
        rows = slice(q * 64, q * 64 + 64)
        pairs = fields_into((den, mom, ene, ent, tra), u, rows, rows) + [(change_h.at[:, rows], change.at[:, rows])]
        late.append(load_all(pairs, sems.at[8 + 6 * q : 14 + 6 * q]))
    px, py = position()
    blocks = []
    for dx in range(3):
        here = jnp.clip(px + dx - 1, 0, GX - 1)
        inside = here == px + dx - 1
        blocks.append([jnp.where(inside, far[here, 12 + n * 4 : 16 + n * 4], 0.0) for n in range(9)])
    gap = jnp.zeros((4, 128), F32)
    around = jnp.concatenate(
        [jnp.concatenate([blocks[dx][dy * 3 + c] for dx in range(3) for dy in range(3)] + [gap], 0) for c in range(3)], 1
    )
    zero = mxu(sel_zero[...], jnp.concatenate(split(around), 1))
    zero = zero[:, :384] + zero[:, 384:]
    arrays = [zero[c * WIN : c * WIN + WIN] * lane_odd[c : c + 1] for c in range(4)]
    packed = [jnp.concatenate([far[x, c * 4 : c * 4 + 4] for x in range(GX)], 0) for c in range(3)]
    lower = lane_ids((128, 128)) % 16 < 8
    gathered = jnp.concatenate(
        [jnp.where(lower, jnp.concatenate([rows, pltpu.roll(rows, 120, 1)], 0), 0.0) for rows in packed], 1
    )
    speeds = gathered[:, 256:]
    fastest = jnp.max(jnp.where(lane_ids((128, 128)) >= 64, speeds, 0.0))

    def lifted(x, x_odd, y_odd):
        sign = (1.0 - 2.0 * x_odd * alpha_odd[0:1]) * (1.0 - 2.0 * y_odd * alpha_odd[1:2])
        n = x.shape[0]
        z = mxu(jnp.concatenate(split(x * sign), 0), up[...])
        return (z[:n] + z[n:]) * sign

    def picked(matrix, x):
        y = mxu(matrix, jnp.concatenate(split(x), 1))
        return y[:, :384] + y[:, 384:]

    dev = lax.broadcasted_iota(jnp.int32, (128, 1), 0)
    raised = lifted(gathered, ((dev // 4) % 2).astype(F32), (dev // 64).astype(F32))
    two = picked(agg[...], raised)
    cell = lax.broadcasted_iota(jnp.int32, (32, 1), 0)
    raised_two = lifted(two, ((cell // 4) % 2).astype(F32), (cell % 2).astype(F32))

    def window(level, columns, shift):
        tx, ty = px >> (level - 1), py >> (level - 1)
        row = lax.broadcasted_iota(jnp.int32, (WIN, columns), 0)
        col = lax.broadcasted_iota(jnp.int32, (WIN, columns), 1)
        i, j = row // 6, row % 6
        i = jnp.where((tx & 1) == 1, 5 - i, i) + 2 * ((tx >> 1) - 1)
        j = jnp.where((ty & 1) == 1, 5 - j, j) + 2 * ((ty >> 1) - 1)
        if columns == 128:
            sx, sy = (col % 64) // 4, 2 * (col % 4) + col // 64
        else:
            sx, sy = col // 4, col % 4
        sx, sy = sx >> shift, sy >> shift
        return ((row < 36) & (sx == i) & (sy == j)).astype(F32).astype(BF16)

    levels = (
        picked(window(1, 128, 0), gathered)
        + picked(window(2, 128, 1), raised)
        + picked(window(3, 32, 1), raised_two)
    )
    sign = jnp.ones((1, 384), F32)
    for level in (1, 2, 3):
        bx = ((px >> (level - 1)) & 1).astype(F32)
        by = ((py >> (level - 1)) & 1).astype(F32)
        sign = sign * (1.0 - 2.0 * bx * lane_odd[4 + level : 5 + level])
        sign = sign * (1.0 - 2.0 * by * lane_odd[8 + level : 9 + level])
    levels = levels * sign
    wrow = lax.broadcasted_iota(jnp.int32, (WIN, 384), 0)
    wi, wj = wrow // 6, wrow % 6
    touching = (wi >= 1) & (wi <= 3) & (wj >= 1) & (wj <= 3)
    arrays += [levels, jnp.where(touching, 0.0, levels)]
    lane = lane_ids((WIN, 128)) // 16
    for a in range(NA):
        c, off = a // 8, (a % 8) * 16
        block = jnp.zeros((WIN, 128), F32)
        for g, array in enumerate(arrays):
            block = jnp.where(lane == g, pltpu.roll(array[:, c * 128 : c * 128 + 128], (16 * g - off) % 128, 1), block)
        rhs[a * WIN : a * WIN + WIN] = block
    high, low = split(rhs[...])
    y = mxu(w_high[...], jnp.concatenate([high, low], 1))
    y = y[:, :128] + y[:, 128:] + mxu(w_low[...], high)
    base = jnp.zeros((NG, 128), F32)
    for k in range(7):
        base = base + mask[k : k + 1] * pltpu.roll(y[k * NG : k * NG + NG], (3 - k) % 128, 1)
    lanes = lane_ids((NG, 128)) // 16
    base = base + jnp.where(lanes == 4, pltpu.roll(base, 112, 1), 0.0)
    bx, by = info[1:2], info[2:3]
    for level in (1, 2, 3):
        bx = bx + info[2 + 2 * level : 3 + 2 * level] * ((px >> (level - 1)) & 1).astype(F32)
        by = by + info[2 + 2 * level : 3 + 2 * level] * ((py >> (level - 1)) & 1).astype(F32)
    flip = (1.0 - 2.0 * bx * gamma_odd[0:NG]) * (1.0 - 2.0 * by * gamma_odd[NG : 2 * NG])
    base = base * info[0:1] * flip
    flip = flip * (1.0 - 2.0 * info[9:10] * gamma_odd[2 * NG :])
    total = base
    for _ in range(3):
        parents = mxu(split_rows(total), expand[...])
        pieces = jnp.concatenate(split(flip * (parents[:NG] + parents[NG:])), 1)
        carried = mxu(down[...], pieces)
        total = base + flip * (carried[:, :128] + carried[:, 128:])
    rows = jnp.concatenate([pltpu.roll(total, (128 - 16 * c) % 128, 1) for c in range(4)], 0)[:, :16]
    spreads = mxu(split_rows(rows), spread[...])
    spreads = spreads[: 4 * NG] + spreads[4 * NG :]
    terms = jnp.concatenate(
        [
            jnp.concatenate([spreads[c * NG : c * NG + NG, k * 128 : k * 128 + 128] for k in range(3)], 0)
            for c in range(4)
        ],
        1,
    )
    values = mxu(poly[...], jnp.concatenate(split(terms), 1))
    field[...] = values[:, :512] + values[:, 512:]
    step = jnp.full((8, 128), COURANT / SUB, F32) / fastest
    stores = []
    for part in range(4):
        half = part // 2
        for copy in late[part]:
            copy.wait()

        def finish(x, carry, half=half):
            for s in range(2):
                c = half * 2 + s
                at = pl.multiple_of(half * 128 + x * 16 + s * 8, 8)
                rows = pl.ds(at, 8)
                acc = [field[pl.ds(pl.multiple_of(i * 64 + x * 8, 8), 8), c * 128 : c * 128 + 128] for i in range(3)]
                old = [u[f, rows] for f in range(NF)]
                for i in range(3):
                    force[i, rows] = acc[i]
                for f in range(NF):
                    slope = change[f, rows]
                    if 1 <= f <= 3:
                        slope = slope + old[0] * acc[f - 1]
                    if f == 4:
                        slope = slope + (old[1] * acc[0] + old[2] * acc[1] + old[3] * acc[2])
                    result[f, rows] = old[f] + step * slope
            return carry

        lax.fori_loop((part % 2) * 4, (part % 2) * 4 + 4, finish, 0)
        rows = slice(part * 64, part * 64 + 64)
        stores += load_all(
            [(result.at[:, rows], section.at[:, rows]), (force.at[:, rows], accel.at[:, rows])],
            sems.at[2 * part : 2 * part + 2],
        )
    for copy in stores:
        copy.wait()


ANY = pl.BlockSpec(memory_space=pl.ANY)
HBM = pl.BlockSpec(memory_space=pltpu.HBM)
VMEM = pl.BlockSpec(memory_space=pltpu.VMEM)


def call(kernel, name, ins, outs, scratch, cost, aliases=None):
    outs = [(o[0], o[1], o[2] if len(o) > 2 else F32) for o in outs]
    return pl.pallas_call(
        kernel,
        out_shape=[pltpu.HBM(s, t) if spec is HBM else jax.ShapeDtypeStruct(s, t) for s, spec, t in outs],
        in_specs=[spec for _, spec in ins],
        out_specs=[spec for _, spec, _ in outs],
        scratch_shapes=scratch,
        input_output_aliases=aliases or {},
        cost_estimate=pl.CostEstimate(flops=cost[0], bytes_accessed=cost[1], transcendentals=cost[2]),
        name=name,
        compiler_params=pltpu.CompilerParams(vmem_limit_bytes=32 << 20),
    )(*[in_hbm(x) if spec is HBM else x for x, spec in ins])


def in_hbm(x):
    return pltpu.with_memory_space_constraint(x, pltpu.HBM)


def scratch_like(x):
    return pltpu.VMEM(x.shape, x.dtype)


def shards(density, momentum, energy, entropy, tracers, leaf_flags):
    con = {k: jnp.asarray(v) for k, v in constants().items()}
    fields = [(x.reshape(-1, ROWS, 128), HBM) for x in (density, momentum, energy, entropy, tracers)]
    first = [con[n] for n in ("left", "right", "flag")]
    whole, slab = (NF, ROWS, 128), (NF, 48, 128)
    block, halo = pltpu.VMEM(whole, F32), pltpu.VMEM(slab, F32)
    pay, u, xa, xb, ya, yb = call(
        prepare_kernel,
        "prepare",
        fields + [(leaf_flags, HBM)] + [(x, HBM) for x in first],
        [((GY, 16, 128), HBM), (whole, VMEM)] + [(slab, HBM)] * 4,
        [pltpu.VMEM((16, 128), F32), pltpu.VMEM((2, *slab), F32), pltpu.VMEM((8, 128), F32), scratch_like(leaf_flags)]
        + [scratch_like(x) for x in first]
        + [pltpu.SemaphoreType.DMA((13 + GY,))],
        (10**7, 4 * 10**6, 10**5),
    )

    def pairs(count, start):
        lows = range(start, count, 2)
        return [(i, (i + 1) % count) for i in lows] + [((i + 1) % count, i) for i in lows]

    column = lax.all_to_all(pay, "my", 0, 0)
    swaps = [
        (lax.ppermute(slab, axis, pairs(count, start)), ANY)
        for slab, axis, count, start in ((xb, "mx", GX, 1), (yb, "my", GY, 1), (xa, "mx", GX, 0), (ya, "my", GY, 0))
    ]
    halos = [swaps[i] for i in (2, 0, 3, 1)]
    (along_z,) = call(
        flux_z_kernel,
        "flux_z",
        [(u, VMEM)],
        [(whole, HBM)],
        [pltpu.VMEM((2 * NF, 144, 128), F32), pltpu.VMEM((2 * NF, 136, 128), F32), block, pltpu.SemaphoreType.DMA((5,))],
        (2 * 10**7, 4 * 10**6, 3 * 10**5),
    )
    (chunks,) = call(
        relay_kernel,
        "relay",
        [(column.reshape(GY * 16, 128), VMEM), (along_z, HBM)] + swaps,
        [((GX, 48, 128), HBM)],
        [pltpu.VMEM((48, 128), F32), pltpu.SemaphoreType.DMA((GX,))],
        (10**4, 10**6, 0),
    )
    far = lax.all_to_all(chunks, "mx", 0, 0)
    second = [con[n] for n in TREE_CONSTANTS]
    tend, *tables = call(
        flux_xy_kernel,
        "flux_xy",
        fields + [(along_z, HBM)] + halos + [(x, HBM) for x in second],
        [(whole, HBM)] + [(x.shape, VMEM, x.dtype) for x in second],
        [
            pltpu.VMEM((NF, 352, 128), F32),
            pltpu.VMEM((NF, 272, 128), F32),
            pltpu.VMEM((NF, 512, 128), F32),
            pltpu.VMEM((NF, 384, 128), F32),
            halo,
            halo,
            block,
            block,
            pltpu.SemaphoreType.DMA((14 + len(second),)),
        ],
        (4 * 10**7, 6 * 10**6, 6 * 10**5),
    )
    section, accel = call(
        tree_kernel,
        "tree",
        [(far, VMEM)] + fields + [(tend, HBM)] + [(x, VMEM) for x in tables],
        [(whole, HBM), ((3, ROWS, 128), HBM)],
        [
            pltpu.VMEM((NA * WIN, 128), F32),
            pltpu.VMEM((192, 512), F32),
            block,
            pltpu.VMEM((3, ROWS, 128), F32),
            block,
            block,
            pltpu.SemaphoreType.DMA((32,)),
        ],
        (10**8, 8 * 10**6, 0),
    )
    return section.reshape(NF, 16, 16, 128), accel.reshape(3, 16, 16, 128)


def solution(mesh):
    placed = (
        P("mx", "my", None),
        P(None, "mx", "my", None),
        P("mx", "my", None),
        P("mx", "my", None),
        P(None, "mx", "my", None),
        P("mx", "my", None),
    )
    return jax.shard_map(
        shards,
        mesh=mesh,
        in_specs=placed,
        out_specs=(P(None, "mx", "my", None), P(None, "mx", "my", None)),
        check_vma=False,
    )
```
